32 devices in a mesh: grp: 2 (over y), tile: 8 (over z, x), gene: 2 (over core).
Axes of the slice: x: 2, y: 2, z: 4, core: 2. Of those that a mesh axis runs over, the one named last changes fastest.
Arguments:
- counts: int32 [4096, 8192], P(('grp', 'tile'), 'gene'), parts along dimension 0, may hold values from 0 to 86, as said below
- cell_factor: float32 [32, 4096], P(None, ('grp', 'tile')), parts along dimension 1, may hold values from 0.05 to 1
- gene_factor: bfloat16 [32, 16384], P(None, ('grp', 'gene')), parts along dimension 1, may hold values from 0.049804688 to 1
- tissue: int32 [4096], P(('grp', 'tile')), parts along dimension 0, may hold values from 0 to 1, as said below
- neighbours: int32 [8, 4096], P(None, ('grp', 'tile')), parts along dimension 1, may hold values from 0 to 2047, as said below
Outputs:
- new_cells: float32 [32, 4096], P(None, ('grp', 'tile')), parts along dimension 1
- new_genes: bfloat16 [32, 16384], P(None, ('grp', 'gene')), parts along dimension 1
The draws below stay inside these ranges and needn't reach their ends.
There are 2 independent parts, one for each index of `grp`. The reference program is written for one: setup_inputs(seed, part) draws one part's arguments, and reference() takes and returns one part's arrays. A program takes and returns all parts, laid end to end along the dimension named above; each array names one. Nothing has to cross between parts.
Inputs may be any that keep to these rules, and one draw needn't show every extreme that they name: `counts`: counts of each cell and gene. Share of tissue differs among tiles. `neighbours`: every neighbour index lies within 32 positions of its cell in cell order, and that distance is reached.
All inputs are finite; a program needn't handle non-finite values.
Results may differ from the reference program's by a relative error of at most 0.00165.
Values may be sent and summed in bfloat16 or wider, within the bound.
A program may use at most 64 MiB of HBM per device.

```python
import math
import jax
import jax.numpy as jnp
from jax import lax

RANK = 32
GENES = 8192
C_DEV = 256
BORDER = 32
NEIGH = 8
PASSES = 2
CELLS = 2048
N_TILE = 8


def draw_counts(key, part):
    pair_key = jax.random.fold_in(key, 31)
    base_key = jax.random.fold_in(key, 32)
    extra_key = jax.random.fold_in(key, 33)
    tiles = CELLS // C_DEV
    block = GENES // tiles
    paired = jax.random.permutation(pair_key, tiles)
    target = paired[jnp.arange(CELLS, dtype=jnp.int32) // C_DEV]
    gene_block = jnp.arange(GENES, dtype=jnp.int32) // block
    hit = target[:, None] == gene_block[None, :]
    base = jax.random.randint(base_key, (CELLS, GENES), 0, 8)
    extra = jax.random.randint(extra_key, (CELLS, GENES), 48, 80)
    return (base + jnp.where(hit, extra, 0)).astype(jnp.int32)


def draw_tissue(key, part):
    level_key = jax.random.fold_in(key, 11)
    cell_key = jax.random.fold_in(key, 12)
    tiles = CELLS // C_DEV
    levels = jax.random.randint(level_key, (tiles,), 20, 96)
    per_cell = jnp.repeat(levels, C_DEV, total_repeat_length=CELLS)
    rolls = jax.random.randint(cell_key, (CELLS,), 0, 100)
    return (rolls < per_cell).astype(jnp.int32)


def draw_neighbours(key, part):
    step_key = jax.random.fold_in(key, 21)
    sign_key = jax.random.fold_in(key, 22)
    offsets = jax.random.randint(step_key, (NEIGH, CELLS), -BORDER, BORDER + 1)
    signs = 2 * jax.random.randint(sign_key, (1, CELLS), 0, 2) - 1
    first = signs * BORDER
    offsets = jnp.concatenate([first, offsets[1:]], axis=0)
    position = jnp.arange(CELLS, dtype=jnp.int32)[None, :]
    return jnp.clip(position + offsets, 0, CELLS - 1).astype(jnp.int32)


def block_levels(stream_key, dims, cuts, smallest, top_value):
    gain = 1.0
    for axis_at, parts in cuts:
        steps = jax.random.uniform(jax.random.fold_in(jax.random.fold_in(stream_key, 6), axis_at), (parts,), jnp.float32, smallest / len(cuts), top_value / len(cuts))
        gain = gain * jnp.repeat(jnp.exp(steps), dims[axis_at] // parts).reshape((-1,) + (1,) * (len(dims) - 1 - axis_at))
    return gain


def setup_inputs(seed: int = 0, part: int = 0) -> dict:
    key_list = jax.random.split(jax.random.key(seed), 6)
    part_keys = jax.random.split(jax.random.fold_in(key_list[5], part), 6)
    counts = draw_counts(jax.random.fold_in(jax.random.fold_in(key_list[5], part), 71), part)
    cell_factor = jnp.clip(jnp.exp(math.log(1.0) - 2.9957323 * jax.random.uniform(part_keys[1], (RANK, CELLS), jnp.float32) ** block_levels(part_keys[1], (RANK, CELLS), ((1, 8),), -0.2, 0.2)), 0.05, 1.0)
    gene_factor = jnp.clip(jnp.exp(math.log(1.0) - 2.9996462 * jax.random.uniform(part_keys[2], (RANK, GENES), jnp.float32) ** block_levels(part_keys[2], (RANK, GENES), ((1, 2),), -0.2, 0.2)), 0.049804688, 1.0).astype(jnp.bfloat16)
    tissue = draw_tissue(jax.random.fold_in(jax.random.fold_in(key_list[5], part), 71), part)
    neighbours = draw_neighbours(jax.random.fold_in(jax.random.fold_in(key_list[5], part), 71), part)
    return {"counts": counts, "cell_factor": cell_factor, "gene_factor": gene_factor, "tissue": tissue, "neighbours": neighbours}


smooth_weight = 0.5


def smooth(updated, tissue, neighbours):
    maskf = tissue.astype(jnp.float32)
    flat = neighbours.reshape(-1)
    count = neighbours.shape[0]
    near_mask = maskf[flat].reshape(count, CELLS)
    gathered = jnp.take(updated, flat, axis=1).reshape(RANK, count, CELLS)
    near = jnp.sum(gathered * near_mask[None], axis=1) / jnp.maximum(jnp.sum(near_mask, axis=0), 1.0)
    return jnp.where(tissue[None] > 0, (1.0 - smooth_weight) * updated + smooth_weight * near, updated)


def reference(counts, cell_factor, gene_factor, tissue, neighbours):
    hfull = gene_factor.astype(jnp.float32)
    maskf = tissue.astype(jnp.float32)
    gsum = jnp.sum(hfull, axis=1)
    blocks = jnp.arange(N_TILE, dtype=jnp.int32)

    def cell_numer(cells):
        def single(index):
            start = (index * C_DEV).astype(jnp.int32)
            wblock = lax.dynamic_slice_in_dim(cells, start, C_DEV, 1)
            xblock = lax.dynamic_slice_in_dim(counts, start, C_DEV, 0).astype(jnp.float32)
            product = lax.dot_general(wblock, hfull, (((0,), (0,)), ((), ())), precision=lax.Precision.HIGHEST)
            ratio = xblock / product
            return lax.dot_general(hfull, ratio, (((1,), (1,)), ((), ())), precision=lax.Precision.HIGHEST)
        pieces = lax.map(single, blocks)
        return jnp.transpose(pieces, (1, 0, 2)).reshape(RANK, CELLS)

    cells = cell_factor
    for step in range(PASSES):
        numer = cell_numer(cells)
        updated = jnp.where(tissue[None] > 0, cells * numer / gsum[:, None], cells)
        cells = smooth(updated, tissue, neighbours)

    def accumulate(total, index):
        start = (index * C_DEV).astype(jnp.int32)
        wblock = lax.dynamic_slice_in_dim(cells, start, C_DEV, 1)
        xblock = lax.dynamic_slice_in_dim(counts, start, C_DEV, 0).astype(jnp.float32)
        mblock = lax.dynamic_slice_in_dim(maskf, start, C_DEV, 0)
        product = lax.dot_general(wblock, hfull, (((0,), (0,)), ((), ())), precision=lax.Precision.HIGHEST)
        ratio = mblock[:, None] * xblock / product
        return total + jnp.dot(wblock, ratio, precision=lax.Precision.HIGHEST), None

    hnum, unused = lax.scan(accumulate, jnp.zeros((RANK, GENES), jnp.float32), blocks)
    hden = jnp.sum(cells * maskf[None], axis=1)
    new_genes = (hfull * hnum / hden[:, None]).astype(jnp.bfloat16)
    return cells, new_genes
```

```python
import functools

import jax
import jax.numpy as jnp
from jax import lax
from jax.experimental import pallas as pl
from jax.experimental.pallas import tpu as pltpu
from jax.sharding import PartitionSpec as P

BORDER = 32
RIM = 2 * BORDER
PASSES = 2
LANES = 128
SUB = 8
MESH = pl.DeviceIdType.MESH
WIRE = jnp.int16
TOP = 32000.0

smooth_weight = 0.5

f32 = jnp.float32
bf16 = jnp.bfloat16


def split(value):
    high = value.astype(bf16)
    low = (value - high.astype(f32)).astype(bf16)
    return high, low


def quotient(top, bottom):
    r = pl.reciprocal(bottom, approx=True)
    return top * (r * (2.0 - bottom * r))


def lane_of(shape):
    return lax.broadcasted_iota(jnp.int32, shape, 1)


def tile_of(columns):
    lane = lane_of((SUB, LANES))
    tile = jnp.zeros((SUB, LANES), f32)
    g = 0
    for column in columns:
        for at in range(0, column.shape[0], SUB):
            tile = jnp.where(lane == g, column[at : at + SUB], tile)
            g += 1
    return tile


def column_of(tile, which, rank):
    groups = rank // SUB
    return jnp.concatenate(
        [tile[:, g : g + 1] for g in range(which * groups, (which + 1) * groups)], axis=0
    )


def kernel(
    n, owners, step, loads,
    x_hbm, w_hbm, h_hbm, t_hbm, nb_hbm,
    cells_ref, genes_ref,
    x_ref, w_ref, h_ref, t_ref, nb_ref, near_ref, acc_ref, own_ref,
    nsend, nrecv, hsend, hrecv, psend, precv, usend, urecv,
    in_sem, e_sem, x_sem, pair_s, pair_r, halo_s, halo_r,
    p_s, p_r, u_s, u_r, g_s, g_r,
):
    rank, width = w_ref.shape
    genes = h_ref.shape[1]
    cols = genes // owners
    me = lax.axis_index("tile")
    core = lax.axis_index("gene")
    other = 1 - core
    barrier = pltpu.get_barrier_semaphore()

    small = [
        pltpu.make_async_copy(src, dst, in_sem.at[i])
        for i, (src, dst) in enumerate(
            ((w_hbm, w_ref), (t_hbm, t_ref), (h_hbm, h_ref), (nb_hbm, nb_ref))
        )
    ]

    def rim_load(side):
        source = pl.ds((width - BORDER, 0)[side], BORDER)
        return pltpu.make_async_copy(
            x_hbm.at[source], x_ref.at[pl.ds(side * BORDER, BORDER)], e_sem.at[side]
        )

    def inner_load(c):
        size = genes // loads
        part = pl.ds(c * size, size)
        return pltpu.make_async_copy(
            x_hbm.at[pl.ds(BORDER, width - RIM), part],
            x_ref.at[pl.ds(RIM, width - RIM), part],
            x_sem.at[c],
        )

    for copy in small[:3]:
        copy.start()
    for side in range(2):
        rim_load(side).start()
    for c in range(loads):
        inner_load(c).start()
    small[3].start()

    def has(side):
        return me > 0 if side == 0 else me < n - 1

    def greet(i, carry):
        pl.semaphore_signal(
            barrier, inc=1, device_id={"tile": lax.rem(me + i, n)}, device_id_type=MESH
        )
        return carry

    few = n <= 16
    lax.fori_loop(1, n, greet, 0, unroll=few)
    pl.semaphore_signal(barrier, inc=1, device_id={"gene": other}, device_id_type=MESH)
    for side in range(2):
        @pl.when(has(side))
        def _():
            pl.semaphore_signal(
                barrier, inc=1, device_id={"tile": me - 1 + 2 * side, "gene": other},
                device_id_type=MESH,
            )

    for side in range(2):
        @pl.when(jnp.logical_not(has(side)))
        def _():
            hrecv[:, side] = jnp.zeros(hrecv.shape[:1] + hrecv.shape[2:], f32)
    hsend[...] = jnp.zeros_like(hsend)

    def halo_rows(p):
        return pl.ds(0, rank + SUB if p == 0 else rank)

    def halo_copy(p, side, k):
        return pltpu.make_async_remote_copy(
            src_ref=hsend.at[p, halo_rows(p)], dst_ref=hrecv.at[p, 1 - side, core, halo_rows(p)],
            send_sem=halo_s.at[p, side, k], recv_sem=halo_r.at[p, 1 - side, core],
            device_id={"tile": me - 1 + 2 * side, "gene": core if k == 0 else other},
            device_id_type=MESH,
        )

    def halo_wait(p, side, k):
        return pltpu.make_async_remote_copy(
            src_ref=hsend.at[p, halo_rows(p)], dst_ref=hrecv.at[p, side, k, halo_rows(p)],
            send_sem=halo_s.at[p, side, k], recv_sem=halo_r.at[p, side, k],
            device_id={"tile": lax.rem(me + 1, n)}, device_id_type=MESH,
        )

    def pair_copy(p):
        part = pl.ds(0, width + LANES if p == 0 else width)
        return pltpu.make_async_remote_copy(
            src_ref=nsend.at[p, :, part], dst_ref=nrecv.at[p, :, part],
            send_sem=pair_s.at[p], recv_sem=pair_r.at[p],
            device_id={"gene": other}, device_id_type=MESH,
        )

    rims, inner = slice(0, RIM), slice(RIM, width)

    def ratio_of(lhs, rows, at, size):
        product = jnp.dot(lhs, h_ref[:, pl.ds(at, size)], preferred_element_type=f32)
        return quotient(x_ref[rows, pl.ds(at, size)].astype(f32), product).astype(bf16)

    def numer_of(lhs, rows, begin):
        acc = None
        for c in range(genes // step):
            if begin is not None:
                begin(c)
            part = lax.dot_general(
                h_ref[:, pl.ds(c * step, step)], ratio_of(lhs, rows, c * step, step),
                (((1,), (1,)), ((), ())), preferred_element_type=f32,
            )
            acc = part if acc is None else acc + part
        return acc

    def put_halo(p, numer):
        hsend[p, 0:rank, rims] = (cells * mask)[:, rims] * numer

    small[0].wait()
    small[1].wait()
    cells = pltpu.roll(w_ref[...], BORDER, 1)
    mrow = pltpu.roll(jnp.broadcast_to(t_ref[...].astype(f32), (2 * SUB, width)), BORDER, 1)
    mask = jnp.broadcast_to(mrow[0:1], (rank, width))
    inside = mask > 0.0
    lane = lane_of((1, LANES))
    hsend[0, rank : rank + SUB, :] = jnp.where(lane_of((SUB, LANES)) < RIM, mrow[0:SUB, 0:LANES], 0.0)
    lhs = jnp.transpose(cells).astype(bf16)
    small[2].wait()
    gsum_part = jnp.sum(h_ref[...].astype(f32), axis=1, keepdims=True)
    nsend[0, :, width : width + LANES] = jnp.broadcast_to(gsum_part, (rank, LANES))

    for side in range(2):
        rim_load(side).wait()
    numer_rim = numer_of(lhs[rims], rims, None)
    put_halo(0, numer_rim)
    pl.semaphore_wait(
        barrier, n + has(0).astype(jnp.int32) + has(1).astype(jnp.int32)
    )

    def halo_start(p):
        for side in range(2):
            @pl.when(has(side))
            def _():
                halo_copy(p, side, 0).start()
                halo_copy(p, side, 1).start()

    halo_start(0)
    every = max(genes // loads // step, 1)

    def arrive(c):
        if c % every == 0:
            inner_load(c // every).wait()

    numer_inner = numer_of(lhs[inner], inner, arrive)
    blend = None
    for p in range(PASSES):
        nsend[p, :, rims] = numer_rim
        nsend[p, :, inner] = numer_inner
        pair_copy(p).start()
        if p == 0:
            small[3].wait()
            a = pltpu.roll(nb_ref[...], BORDER, 1) - (me * width - BORDER)
            spot = jnp.where(a < BORDER, a + width, a)
            spot = jnp.where(jnp.logical_and(a >= width, a < width + BORDER), a - width, spot)
            size = BORDER
            for at in range(0, width + LANES, size):
                index = lax.broadcasted_iota(jnp.int32, (size, width), 0) + at
                total = jnp.zeros((size, width), f32)
                for j in range(nb_ref.shape[0]):
                    total = total + jnp.where(spot[j : j + 1] == index, 1.0, 0.0)
                near_ref[at : at + size, :] = total.astype(bf16)
        pair_copy(p).wait_recv()
        if p == 0:
            inverse = 1.0 / (
                nsend[0, :, width : width + LANES] + nrecv[0, :, width : width + LANES]
            )
            inverse_wide = jnp.concatenate([inverse] * (width // LANES), axis=1)
        numer = nsend[p, :, 0:width] + nrecv[p, :, 0:width]
        updated = jnp.where(inside, cells * numer * inverse_wide, cells)
        stacked = jnp.concatenate(split(updated * mask) + (mrow.astype(bf16),), axis=0)
        mixed = jnp.dot(stacked, near_ref[0:width, :], preferred_element_type=f32)
        near = mixed[0:rank] + mixed[rank : 2 * rank]
        if p == 0:
            count = mixed[2 * rank : 2 * rank + 1]
        cells = jnp.where(
            inside,
            (1.0 - smooth_weight) * updated + smooth_weight * near / jnp.maximum(count, 1.0),
            updated,
        )
        lhs = jnp.transpose(cells).astype(bf16)
        if p + 1 < PASSES:
            numer_inner = numer_of(lhs[inner], inner, None)
        else:
            lift = jnp.concatenate(split(cells * mask), axis=0)[:, inner]
            for c in range(genes // step):
                both = jnp.dot(
                    lift, ratio_of(lhs[inner], inner, c * step, step), preferred_element_type=f32
                )
                acc_ref[:, pl.ds(c * step, step)] = both[0:rank] + both[rank : 2 * rank]
        for side in range(2):
            @pl.when(has(side))
            def _():
                for k in range(2):
                    halo_wait(p, side, k).wait_recv()
        before = hrecv[p, 0, 0, 0:rank] + hrecv[p, 0, 1, 0:rank]
        after = hrecv[p, 1, 0, 0:rank] + hrecv[p, 1, 1, 0:rank]
        halo = jnp.where(lane < BORDER, before, after) * inverse
        if p == 0:
            flags = jnp.where(
                lane_of((SUB, LANES)) < BORDER,
                hrecv[0, 0, 0, rank : rank + SUB], hrecv[0, 1, 0, rank : rank + SUB],
            )
            flags = jnp.concatenate([flags, flags], axis=0).astype(bf16)
        stacked = jnp.concatenate(split(halo) + (flags,), axis=0)
        mixed = jnp.dot(
            stacked, near_ref[width : width + LANES, 0:LANES], preferred_element_type=f32
        )
        near_rim = near[:, 0:LANES] + (mixed[0:rank] + mixed[rank : 2 * rank])
        if p == 0:
            count_rim = jnp.maximum(count[:, 0:LANES] + mixed[2 * rank : 2 * rank + 1], 1.0)
        rim = updated[:, 0:LANES]
        rim = jnp.where(
            inside[:, 0:LANES],
            (1.0 - smooth_weight) * rim + smooth_weight * near_rim / count_rim,
            rim,
        )
        cells = jnp.concatenate([rim, cells[:, LANES:]], axis=1)
        lhs = jnp.transpose(rim).astype(bf16)[rims]
        if p + 1 < PASSES:
            numer_rim = numer_of(lhs, rims, None)
            put_halo(p + 1, numer_rim)
            halo_start(p + 1)

    weighted = cells * mask
    den_part = jnp.sum(weighted, axis=1, keepdims=True)
    lift = jnp.concatenate(split(weighted[:, 0:LANES]), axis=0)[:, rims]

    def is_owner(index):
        return index < owners

    def when_owner(index, call):
        if owners == n:
            call()
        else:
            pl.when(is_owner(index))(call)

    def offset(i):
        return lax.rem(i + n // 2 - 1, n - 1) + 1

    def piece(o):
        return pl.ds(pl.multiple_of(o * cols, LANES), cols)

    def total_of(o):
        at = pl.multiple_of(o * cols, LANES)
        both = jnp.dot(lift, ratio_of(lhs, rims, at, cols), preferred_element_type=f32)
        return acc_ref[:, pl.ds(at, cols)] + (both[0:rank] + both[rank : 2 * rank])

    def part_copies(o, off):
        slot = n - 1 - off
        return tuple(
            pltpu.make_async_remote_copy(
                src_ref=src.at[o], dst_ref=dst.at[slot], send_sem=ssem.at[off - 1],
                recv_sem=rsem.at[slot], device_id={"tile": o}, device_id_type=MESH,
            )
            for src, dst, ssem, rsem in ((usend, urecv, u_s, u_r), (psend, precv, p_s, p_r))
        )

    def send_part(i, carry):
        off = offset(i)
        o = lax.rem(me + off, n)

        def call():
            part = total_of(o)
            top = jnp.maximum(jnp.max(part, axis=1, keepdims=True), 1e-30)
            psend[o] = (part * (TOP / top) + 0.5).astype(jnp.int32).astype(WIRE)
            usend[o] = tile_of((top * (1.0 / TOP), den_part))
            for copy in part_copies(o, off):
                copy.start()

        when_owner(o, call)
        return carry

    lax.fori_loop(0, n - 1, send_part, 0, unroll=few)

    def gene_copy(o, off):
        ref = genes_ref.at[:, piece(o)]
        return pltpu.make_async_remote_copy(
            src_ref=ref, dst_ref=ref, send_sem=g_s.at[off - 1], recv_sem=g_r,
            device_id={"tile": lax.rem(me + off, n)}, device_id_type=MESH,
        )

    def finish_part():
        own_ref[...] = total_of(me)
        lead = h_ref[:, piece(me)].astype(f32)
        cells_ref[...] = pltpu.roll(cells, width - BORDER, 1)

        def add(i, carry):
            total, units = carry
            off = offset(i)
            for copy in part_copies(0, off):
                copy.wait_recv()
            unit = urecv[n - 1 - off]
            value = precv[n - 1 - off].astype(jnp.int32).astype(f32)
            return total + value * column_of(unit, 0, rank), units + unit

        start = tile_of((jnp.zeros_like(den_part), den_part))
        total, units = lax.fori_loop(0, n - 1, add, (own_ref[...], start), unroll=few)
        lead = lead * (1.0 / column_of(units, 1, rank))
        genes_ref[:, piece(me)] = (lead * total).astype(genes_ref.dtype)

        def spread(i, carry):
            gene_copy(me, offset(i)).start()
            return carry

        lax.fori_loop(0, n - 1, spread, 0, unroll=few)

    def arrived(pieces):
        ref = genes_ref.at[:, pl.ds(0, pieces * cols)]
        pltpu.make_async_remote_copy(
            src_ref=ref, dst_ref=ref, send_sem=g_s.at[0], recv_sem=g_r,
            device_id={"tile": lax.rem(me + 1, n)}, device_id_type=MESH,
        ).wait_recv()

    if owners == n:
        finish_part()
        arrived(owners - 1)
    else:
        pl.when(is_owner(me))(finish_part)

        @pl.when(is_owner(me))
        def _():
            arrived(owners - 1)

        @pl.when(jnp.logical_not(is_owner(me)))
        def _():
            cells_ref[...] = pltpu.roll(cells, width - BORDER, 1)
            arrived(owners)

    def ended(i, carry):
        off = offset(i)
        o = lax.rem(me + off, n)

        def parts_sent():
            for copy in part_copies(o, off):
                copy.wait_send()

        when_owner(o, parts_sent)
        when_owner(me, lambda: gene_copy(me, off).wait_send())
        return carry

    lax.fori_loop(0, n - 1, ended, 0, unroll=few)
    for p in range(PASSES):
        pair_copy(p).wait_send()
        for side in range(2):
            @pl.when(has(side))
            def _():
                halo_copy(p, side, 0).wait_send()
                halo_copy(p, side, 1).wait_send()


def settle(cells_in, genes_in, cells_ref, genes_ref):
    cells_ref[...] = cells_in[...]
    genes_ref[...] = genes_in[...]


def on_device(n, counts, cell_factor, gene_factor, tissue, neighbours):
    width, genes = counts.shape
    rank = cell_factor.shape[0]
    near = neighbours.shape[0]
    owners = min(n, genes // LANES)
    step = min(512, genes)
    loads = min(4, genes // step)
    cols = genes // owners
    dma = pltpu.SemaphoreType.DMA
    vmem = pl.BlockSpec(memory_space=pltpu.VMEM)
    shapes = (
        jax.ShapeDtypeStruct((rank, width), f32),
        jax.ShapeDtypeStruct((rank, genes), bf16),
    )
    results = pl.pallas_call(
        functools.partial(kernel, n, owners, step, loads),
        out_shape=tuple(pltpu.VMEM(s.shape, s.dtype) for s in shapes),
        in_specs=[pl.BlockSpec(memory_space=pl.ANY)] * 5,
        out_specs=(vmem, vmem),
        scratch_shapes=[
            pltpu.VMEM((width, genes), jnp.int32),
            pltpu.VMEM((rank, width), f32),
            pltpu.VMEM((rank, genes), bf16),
            pltpu.VMEM((1, width), jnp.int32),
            pltpu.VMEM((near, width), jnp.int32),
            pltpu.VMEM((width + LANES, width), bf16),
            pltpu.VMEM((rank, genes), f32),
            pltpu.VMEM((rank, cols), f32),
            pltpu.VMEM((PASSES, rank, width + LANES), f32),
            pltpu.VMEM((PASSES, rank, width + LANES), f32),
            pltpu.VMEM((PASSES, rank + SUB, LANES), f32),
            pltpu.VMEM((PASSES, 2, 2, rank + SUB, LANES), f32),
            pltpu.VMEM((owners, rank, cols), WIRE),
            pltpu.VMEM((n - 1, rank, cols), WIRE),
            pltpu.VMEM((owners, SUB, LANES), f32),
            pltpu.VMEM((n - 1, SUB, LANES), f32),
            dma((4,)),
            dma((2,)),
            dma((loads,)),
            dma((PASSES,)),
            dma((PASSES,)),
            dma((PASSES, 2, 2)),
            dma((PASSES, 2, 2)),
            dma((n - 1,)),
            dma((n - 1,)),
            dma((n - 1,)),
            dma((n - 1,)),
            dma((n - 1,)),
            dma,
        ],
        compiler_params=pltpu.CompilerParams(
            collective_id=0, has_side_effects=True, vmem_limit_bytes=63_160_000
        ),
    )(counts, cell_factor, gene_factor, tissue.reshape(1, width), neighbours)
    return pl.pallas_call(
        settle, out_shape=shapes, in_specs=[vmem] * 2, out_specs=(vmem, vmem),
        compiler_params=pltpu.CompilerParams(vmem_limit_bytes=16 * 1024 * 1024),
    )(*results)


def solution(mesh):
    return jax.shard_map(
        functools.partial(on_device, mesh.shape["tile"]),
        mesh=mesh,
        in_specs=(
            P(("grp", "tile"), "gene"),
            P(None, ("grp", "tile")),
            P(None, ("grp", "gene")),
            P(("grp", "tile")),
            P(None, ("grp", "tile")),
        ),
        out_specs=(P(None, ("grp", "tile")), P(None, ("grp", "gene"))),
        check_vma=False,
    )
```

```python
import functools

import jax
import jax.numpy as jnp
from jax import lax
from jax.experimental import pallas as pl
from jax.experimental.pallas import tpu as pltpu
from jax.sharding import PartitionSpec as P

BORDER = 32
RIM = 2 * BORDER
PASSES = 2
LANES = 128
SUB = 8
MESH = pl.DeviceIdType.MESH
WIRE = jnp.int16
TOP = 32000.0

smooth_weight = 0.5

f32 = jnp.float32
bf16 = jnp.bfloat16


def split(value):
    high = value.astype(bf16)
    low = (value - high.astype(f32)).astype(bf16)
    return high, low


def quotient(top, bottom):
    r = pl.reciprocal(bottom, approx=True)
    return top * (r * (2.0 - bottom * r))


def lane_of(shape):
    return lax.broadcasted_iota(jnp.int32, shape, 1)


def tile_of(columns):
    pieces = [
        column[at : at + SUB] for column in columns for at in range(0, column.shape[0], SUB)
    ]
    lane = lane_of((SUB, len(pieces)))
    tile = jnp.zeros((SUB, len(pieces)), f32)
    for g, piece in enumerate(pieces):
        tile = jnp.where(lane == g, piece, tile)
    return tile


def column_of(tile, which, rank):
    groups = rank // SUB
    return jnp.concatenate(
        [tile[:, g : g + 1] for g in range(which * groups, (which + 1) * groups)], axis=0
    )


def kernel(
    n, owners, quarters, step, loads,
    x_hbm, w_hbm, h_hbm, t_hbm, nb_hbm,
    cells_ref, genes_ref,
    x_ref, w_ref, h_ref, t_ref, nb_ref, near_ref, acc_ref,
    nsend, nrecv, hsend, hrecv, psend, precv, usend, urecv,
    in_sem, e_sem, x_sem, pair_s, pair_r, halo_s, halo_r,
    p_s, p_r, u_s, u_r, g_s, g_r,
):
    rank, width = w_ref.shape
    genes = h_ref.shape[1]
    cols = genes // owners
    me = lax.axis_index("tile")
    core = lax.axis_index("gene")
    other = 1 - core
    barrier = pltpu.get_barrier_semaphore()

    small = [
        pltpu.make_async_copy(src, dst, in_sem.at[i])
        for i, (src, dst) in enumerate(
            ((w_hbm, w_ref), (t_hbm, t_ref), (h_hbm, h_ref), (nb_hbm, nb_ref))
        )
    ]

    def rim_load(side):
        source = pl.ds((width - BORDER, 0)[side], BORDER)
        return pltpu.make_async_copy(
            x_hbm.at[source], x_ref.at[pl.ds(side * BORDER, BORDER)], e_sem.at[side]
        )

    def inner_load(c):
        size = genes // loads
        part = pl.ds(c * size, size)
        return pltpu.make_async_copy(
            x_hbm.at[pl.ds(BORDER, width - RIM), part],
            x_ref.at[pl.ds(RIM, width - RIM), part],
            x_sem.at[c],
        )

    for copy in small[:3]:
        copy.start()
    for side in range(2):
        rim_load(side).start()
    small[3].start()

    def has(side):
        return me > 0 if side == 0 else me < n - 1

    def greet(i, carry):
        pl.semaphore_signal(
            barrier, inc=1, device_id={"tile": lax.rem(me + i, n)}, device_id_type=MESH
        )
        return carry

    few = n <= 16
    lax.fori_loop(1, n, greet, 0, unroll=few)
    pl.semaphore_signal(barrier, inc=1, device_id={"gene": other}, device_id_type=MESH)
    for side in range(2):
        @pl.when(has(side))
        def _():
            pl.semaphore_signal(
                barrier, inc=1, device_id={"tile": me - 1 + 2 * side, "gene": other},
                device_id_type=MESH,
            )

    for side in range(2):
        @pl.when(jnp.logical_not(has(side)))
        def _():
            hrecv[:, side] = jnp.zeros(hrecv.shape[:1] + hrecv.shape[2:], f32)
    hsend[...] = jnp.zeros_like(hsend)

    def halo_rows(p):
        return pl.ds(0, rank + SUB if p == 0 else rank)

    def halo_copy(p, side, k):
        return pltpu.make_async_remote_copy(
            src_ref=hsend.at[p, halo_rows(p)], dst_ref=hrecv.at[p, 1 - side, core, halo_rows(p)],
            send_sem=halo_s.at[p, side], recv_sem=halo_r.at[p, 1 - side],
            device_id={"tile": me - 1 + 2 * side, "gene": core if k == 0 else other},
            device_id_type=MESH,
        )

    def halo_both(p, side):
        ref = hrecv.at[p, side, :, halo_rows(p)]
        return pltpu.make_async_remote_copy(
            src_ref=ref, dst_ref=ref, send_sem=halo_s.at[p, side], recv_sem=halo_r.at[p, side],
            device_id={"tile": lax.rem(me + 1, n)}, device_id_type=MESH,
        )

    def pair_copy(p):
        part = pl.ds(0, width + LANES if p == 0 else width)
        return pltpu.make_async_remote_copy(
            src_ref=nsend.at[p, :, part], dst_ref=nrecv.at[p, :, part],
            send_sem=pair_s.at[p], recv_sem=pair_r.at[p],
            device_id={"gene": other}, device_id_type=MESH,
        )

    rims, inner = slice(0, RIM), slice(RIM, width)

    def ratio_of(lhs, rows, at, size):
        product = jnp.dot(lhs, h_ref[:, pl.ds(at, size)], preferred_element_type=f32)
        return quotient(x_ref[rows, pl.ds(at, size)].astype(f32), product).astype(bf16)

    def numer_of(lhs, rows, begin):
        acc = None
        for c in range(genes // step):
            if begin is not None:
                begin(c)
            part = lax.dot_general(
                h_ref[:, pl.ds(c * step, step)], ratio_of(lhs, rows, c * step, step),
                (((1,), (1,)), ((), ())), preferred_element_type=f32,
            )
            acc = part if acc is None else acc + part
        return acc

    def put_halo(p, numer):
        hsend[p, 0:rank, rims] = (cells * mask)[:, rims] * numer

    small[0].wait()
    small[1].wait()
    for c in range(loads):
        inner_load(c).start()
    cells = pltpu.roll(w_ref[...], BORDER, 1)
    mrow = pltpu.roll(jnp.broadcast_to(t_ref[...].astype(f32), (2 * SUB, width)), BORDER, 1)
    mask = jnp.broadcast_to(mrow[0:1], (rank, width))
    inside = mask > 0.0
    lane = lane_of((1, LANES))
    hsend[0, rank : rank + SUB, :] = jnp.where(lane_of((SUB, LANES)) < RIM, mrow[0:SUB, 0:LANES], 0.0)
    lhs = jnp.transpose(cells).astype(bf16)
    small[2].wait()
    for side in range(2):
        rim_load(side).wait()
    numer_rim = numer_of(lhs[rims], rims, None)
    put_halo(0, numer_rim)
    pl.semaphore_wait(
        barrier, n + has(0).astype(jnp.int32) + has(1).astype(jnp.int32)
    )

    def halo_start(p):
        for side in range(2):
            @pl.when(has(side))
            def _():
                halo_copy(p, side, 0).start()
                halo_copy(p, side, 1).start()

    halo_start(0)
    gsum_part = jnp.sum(h_ref[...].astype(f32), axis=1, keepdims=True)
    nsend[0, :, width : width + LANES] = jnp.broadcast_to(gsum_part, (rank, LANES))
    every = max(genes // loads // step, 1)

    def arrive(c):
        if c % every == 0:
            inner_load(c // every).wait()

    numer_inner = numer_of(lhs[inner], inner, arrive)
    blend = None
    for p in range(PASSES):
        nsend[p, :, rims] = numer_rim
        nsend[p, :, inner] = numer_inner
        pair_copy(p).start()
        if p == 0:
            small[3].wait()
            a = pltpu.roll(nb_ref[...], BORDER, 1) - (me * width - BORDER)
            spot = jnp.where(a < BORDER, a + width, a)
            spot = jnp.where(jnp.logical_and(a >= width, a < width + BORDER), a - width, spot)
            size = BORDER
            for at in range(0, width + LANES, size):
                index = lax.broadcasted_iota(jnp.int32, (size, width), 0) + at
                total = jnp.zeros((size, width), f32)
                for j in range(nb_ref.shape[0]):
                    total = total + jnp.where(spot[j : j + 1] == index, 1.0, 0.0)
                near_ref[at : at + size, :] = total.astype(bf16)
        pair_copy(p).wait_recv()
        if p == 0:
            inverse = 1.0 / (
                nsend[0, :, width : width + LANES] + nrecv[0, :, width : width + LANES]
            )
            inverse_wide = jnp.concatenate([inverse] * (width // LANES), axis=1)
        numer = nsend[p, :, 0:width] + nrecv[p, :, 0:width]
        updated = jnp.where(inside, cells * numer * inverse_wide, cells)
        stacked = jnp.concatenate(split(updated * mask) + (mrow.astype(bf16),), axis=0)
        mixed = jnp.dot(stacked, near_ref[0:width, :], preferred_element_type=f32)
        near = mixed[0:rank] + mixed[rank : 2 * rank]
        if p == 0:
            count = mixed[2 * rank : 2 * rank + 1]
        cells = jnp.where(
            inside,
            (1.0 - smooth_weight) * updated + smooth_weight * near / jnp.maximum(count, 1.0),
            updated,
        )
        lhs = jnp.transpose(cells).astype(bf16)
        if p + 1 < PASSES:
            numer_inner = numer_of(lhs[inner], inner, None)
        else:
            lift = jnp.concatenate(split(cells * mask), axis=0)[:, inner]
            wide = min(4 * step, genes)
            for at in range(0, genes, wide):
                both = jnp.dot(
                    lift, ratio_of(lhs[inner], inner, at, wide), preferred_element_type=f32
                )
                acc_ref[:, pl.ds(at, wide)] = both[0:rank] + both[rank : 2 * rank]
        for side in range(2):
            @pl.when(has(side))
            def _():
                halo_both(p, side).wait_recv()
        before = hrecv[p, 0, 0, 0:rank] + hrecv[p, 0, 1, 0:rank]
        after = hrecv[p, 1, 0, 0:rank] + hrecv[p, 1, 1, 0:rank]
        halo = jnp.where(lane < BORDER, before, after) * inverse
        if p == 0:
            flags = jnp.where(
                lane_of((SUB, LANES)) < BORDER,
                hrecv[0, 0, 0, rank : rank + SUB], hrecv[0, 1, 0, rank : rank + SUB],
            )
            flags = jnp.concatenate([flags, flags], axis=0).astype(bf16)
        stacked = jnp.concatenate(split(halo) + (flags,), axis=0)
        mixed = jnp.dot(
            stacked, near_ref[width : width + LANES, 0:LANES], preferred_element_type=f32
        )
        near_rim = near[:, 0:LANES] + (mixed[0:rank] + mixed[rank : 2 * rank])
        if p == 0:
            count_rim = jnp.maximum(count[:, 0:LANES] + mixed[2 * rank : 2 * rank + 1], 1.0)
        rim = updated[:, 0:LANES]
        rim = jnp.where(
            inside[:, 0:LANES],
            (1.0 - smooth_weight) * rim + smooth_weight * near_rim / count_rim,
            rim,
        )
        cells = jnp.concatenate([rim, cells[:, LANES:]], axis=1)
        lhs = jnp.transpose(rim).astype(bf16)[rims]
        if p + 1 < PASSES:
            numer_rim = numer_of(lhs, rims, None)
            put_halo(p + 1, numer_rim)
            halo_start(p + 1)

    weighted = cells * mask
    den_part = jnp.sum(weighted, axis=1, keepdims=True)
    lift = jnp.concatenate(split(weighted[:, 0:LANES]), axis=0)[:, rims]

    blk = cols // quarters

    def when_owner(index, call):
        if owners == n:
            call()
        else:
            pl.when(index < owners)(call)

    def move(src, dst, ssem, rsem, tile):
        return pltpu.make_async_remote_copy(
            src_ref=src, dst_ref=dst, send_sem=ssem, recv_sem=rsem,
            device_id={"tile": tile}, device_id_type=MESH,
        )

    def part_start(q, j):
        o = lax.rem(me + j, n)

        def call():
            slot = n - 1 - j
            move(usend.at[q * owners + o], urecv.at[q, slot], u_s, u_r.at[q], o).start()
            move(psend.at[q * owners + o], precv.at[q, slot], p_s, p_r.at[q], o).start()

        when_owner(o, call)

    def all_peers(call):
        if few:
            for j in range(1, n):
                call(j)
        else:
            def body(j, carry):
                call(j)
                return carry

            lax.fori_loop(1, n, body, 0)

    for q in range(quarters):
        places = [slice(o * cols + q * blk, o * cols + (q + 1) * blk) for o in range(owners)]
        product = jnp.dot(
            lhs, jnp.concatenate([h_ref[:, at] for at in places], axis=1),
            preferred_element_type=f32,
        )
        seen = jnp.concatenate([x_ref[rims, at] for at in places], axis=1).astype(f32)
        both = jnp.dot(lift, quotient(seen, product).astype(bf16), preferred_element_type=f32)
        part = both[0:rank] + both[rank : 2 * rank]
        for o, at in enumerate(places):
            total = acc_ref[:, at] + part[:, o * blk : (o + 1) * blk]
            acc_ref[:, at] = total
            top = jnp.maximum(jnp.max(total, axis=1, keepdims=True), 1e-30)
            psend[q * owners + o] = (total * (TOP / top) + 0.5).astype(jnp.int32).astype(WIRE)
            usend[q * owners + o] = tile_of((top * (1.0 / TOP), den_part))
        all_peers(lambda j: part_start(q, j))
    cells_ref[...] = pltpu.roll(cells, width - BORDER, 1)

    def gene_piece(q):
        return genes_ref.at[:, pl.ds(pl.multiple_of(me * cols + q * blk, LANES), blk)]

    def finish_part():
        ahead = lax.rem(me + 1, n)
        for q in range(quarters):
            here = pl.ds(pl.multiple_of(me * cols + q * blk, LANES), blk)
            total = acc_ref[:, here]
            units = tile_of((jnp.zeros_like(den_part), den_part))
            move(urecv.at[q], urecv.at[q], u_s, u_r.at[q], ahead).wait_recv()
            move(precv.at[q], precv.at[q], p_s, p_r.at[q], ahead).wait_recv()

            def add(slot, carry):
                total, units = carry
                unit = urecv[q, slot]
                value = precv[q, slot].astype(jnp.int32).astype(f32)
                return total + value * column_of(unit, 0, rank), units + unit

            total, units = lax.fori_loop(0, n - 1, add, (total, units), unroll=few)
            if q == 0:
                inverse_den = 1.0 / column_of(units, 1, rank)
            lead = h_ref[:, here].astype(f32) * inverse_den
            genes_ref[:, here] = (lead * total).astype(genes_ref.dtype)
            all_peers(
                lambda j: move(
                    gene_piece(q), gene_piece(q), g_s, g_r, lax.rem(me + j, n)
                ).start()
            )

    def wait_all(owned):
        others = owners - 1 if owned else owners
        ahead = lax.rem(me + 1, n)
        ref = genes_ref.at[:, pl.ds(0, others * cols)]
        move(ref, ref, g_s, g_r, ahead).wait_recv()
        sent = pl.ds(0, quarters * others)
        for ref, sem in ((usend, u_s), (psend, p_s)):
            move(ref.at[sent], ref.at[sent], sem, g_r, ahead).wait_send()
        if owned:
            move(precv, precv, g_s, g_r, ahead).wait_send()

    when_owner(me, finish_part)
    when_owner(me, lambda: wait_all(True))
    if owners < n:
        pl.when(me >= owners)(lambda: wait_all(False))
    for p in range(PASSES):
        pair_copy(p).wait_send()
        for side in range(2):
            @pl.when(has(side))
            def _():
                halo_both(p, side).wait_send()


def settle(cells_in, genes_in, cells_ref, genes_ref):
    cells_ref[...] = cells_in[...]
    genes_ref[...] = genes_in[...]


def on_device(n, counts, cell_factor, gene_factor, tissue, neighbours):
    width, genes = counts.shape
    rank = cell_factor.shape[0]
    near = neighbours.shape[0]
    owners = min(n, genes // LANES)
    step = min(512, genes)
    loads = min(4, genes // step)
    cols = genes // owners
    quarters = max(1, min(4, cols // LANES))
    dma = pltpu.SemaphoreType.DMA
    vmem = pl.BlockSpec(memory_space=pltpu.VMEM)
    shapes = (
        jax.ShapeDtypeStruct((rank, width), f32),
        jax.ShapeDtypeStruct((rank, genes), bf16),
    )
    results = pl.pallas_call(
        functools.partial(kernel, n, owners, quarters, step, loads),
        out_shape=tuple(pltpu.VMEM(s.shape, s.dtype) for s in shapes),
        in_specs=[pl.BlockSpec(memory_space=pl.ANY)] * 5,
        out_specs=(vmem, vmem),
        scratch_shapes=[
            pltpu.VMEM((width, genes), jnp.int32),
            pltpu.VMEM((rank, width), f32),
            pltpu.VMEM((rank, genes), bf16),
            pltpu.VMEM((1, width), jnp.int32),
            pltpu.VMEM((near, width), jnp.int32),
            pltpu.VMEM((width + LANES, width), bf16),
            pltpu.VMEM((rank, genes), f32),
            pltpu.VMEM((PASSES, rank, width + LANES), f32),
            pltpu.VMEM((PASSES, rank, width + LANES), f32),
            pltpu.VMEM((PASSES, rank + SUB, LANES), f32),
            pltpu.VMEM((PASSES, 2, 2, rank + SUB, LANES), f32),
            pltpu.VMEM((quarters * owners, rank, cols // quarters), WIRE),
            pltpu.VMEM((quarters, n - 1, rank, cols // quarters), WIRE),
            pltpu.VMEM((quarters * owners, SUB, 2 * rank // SUB), f32),
            pltpu.VMEM((quarters, n - 1, SUB, 2 * rank // SUB), f32),
            dma((4,)),
            dma((2,)),
            dma((loads,)),
            dma((PASSES,)),
            dma((PASSES,)),
            dma((PASSES, 2)),
            dma((PASSES, 2)),
            dma,
            dma((quarters,)),
            dma,
            dma((quarters,)),
            dma,
            dma,
        ],
        compiler_params=pltpu.CompilerParams(
            collective_id=0, has_side_effects=True, vmem_limit_bytes=63_160_000
        ),
    )(counts, cell_factor, gene_factor, tissue.reshape(1, width), neighbours)
    return pl.pallas_call(
        settle, out_shape=shapes, in_specs=[vmem] * 2, out_specs=(vmem, vmem),
        compiler_params=pltpu.CompilerParams(vmem_limit_bytes=16 * 1024 * 1024),
    )(*results)


def solution(mesh):
    return jax.shard_map(
        functools.partial(on_device, mesh.shape["tile"]),
        mesh=mesh,
        in_specs=(
            P(("grp", "tile"), "gene"),
            P(None, ("grp", "tile")),
            P(None, ("grp", "gene")),
            P(("grp", "tile")),
            P(None, ("grp", "tile")),
        ),
        out_specs=(P(None, ("grp", "tile")), P(None, ("grp", "gene"))),
        check_vma=False,
    )
```

```python
import functools

import jax
import jax.numpy as jnp
from jax import lax
from jax.experimental import pallas as pl
from jax.experimental.pallas import tpu as pltpu
from jax.sharding import PartitionSpec as P

BORDER = 32
RIM = 2 * BORDER
PASSES = 2
LANES = 128
SUB = 8
MESH = pl.DeviceIdType.MESH
WIRE = jnp.int16
TOP = 65000.0
HALF = 32768.0

smooth_weight = 0.5

f32 = jnp.float32
bf16 = jnp.bfloat16


def split(value):
    high = value.astype(bf16)
    low = (value - high.astype(f32)).astype(bf16)
    return high, low


def quotient(top, bottom):
    r = pl.reciprocal(bottom, approx=True)
    return top * (r * (2.0 - bottom * r))


def lane_of(shape):
    return lax.broadcasted_iota(jnp.int32, shape, 1)


def row_of(columns):
    rank = columns[0].shape[0]
    index = lax.broadcasted_iota(jnp.int32, (rank, LANES), 0)
    lane = lane_of((rank, LANES))
    spread = jnp.zeros((rank, LANES), f32)
    for g, column in enumerate(columns):
        spread = jnp.where(lane == index + g * rank, column, spread)
    return jnp.sum(spread, axis=0, keepdims=True)


def kernel(
    n, owners, quarters, step, loads,
    x_hbm, w_hbm, h_hbm, t_hbm, nb_hbm,
    cells_ref, genes_ref,
    x_ref, w_ref, h_ref, t_ref, nb_ref, near_ref, acc_ref,
    nsend, nrecv, hsend, hrecv, psend, precv, usend, urecv,
    in_sem, e_sem, x_sem, pair_s, pair_r, halo_s, halo_r,
    p_s, p_r, u_s, u_r, g_s, g_r,
):
    rank, width = w_ref.shape
    genes = h_ref.shape[1]
    cols = genes // owners
    me = lax.axis_index("tile")
    core = lax.axis_index("gene")
    other = 1 - core
    barrier = pltpu.get_barrier_semaphore()

    small = [
        pltpu.make_async_copy(src, dst, in_sem.at[i])
        for i, (src, dst) in enumerate(
            ((w_hbm, w_ref), (t_hbm, t_ref), (h_hbm, h_ref), (nb_hbm, nb_ref))
        )
    ]

    def rim_load(side):
        source = pl.ds((width - BORDER, 0)[side], BORDER)
        return pltpu.make_async_copy(
            x_hbm.at[source], x_ref.at[pl.ds(side * BORDER, BORDER)], e_sem.at[side]
        )

    def inner_load(c):
        size = genes // loads
        part = pl.ds(c * size, size)
        return pltpu.make_async_copy(
            x_hbm.at[pl.ds(BORDER, width - RIM), part],
            x_ref.at[pl.ds(RIM, width - RIM), part],
            x_sem.at[c],
        )

    for copy in small[:3]:
        copy.start()
    for side in range(2):
        rim_load(side).start()
    small[3].start()

    def has(side):
        return me > 0 if side == 0 else me < n - 1

    def greet(i, carry):
        pl.semaphore_signal(
            barrier, inc=1, device_id={"tile": lax.rem(me + i, n)}, device_id_type=MESH
        )
        return carry

    few = n <= 16
    lax.fori_loop(1, n, greet, 0, unroll=few)
    pl.semaphore_signal(barrier, inc=1, device_id={"gene": other}, device_id_type=MESH)
    for side in range(2):
        @pl.when(has(side))
        def _():
            pl.semaphore_signal(
                barrier, inc=1, device_id={"tile": me - 1 + 2 * side, "gene": other},
                device_id_type=MESH,
            )

    for side in range(2):
        @pl.when(jnp.logical_not(has(side)))
        def _():
            hrecv[:, side] = jnp.zeros(hrecv.shape[:1] + hrecv.shape[2:], f32)
    hsend[...] = jnp.zeros_like(hsend)

    def halo_rows(p):
        return pl.ds(0, rank + SUB if p == 0 else rank)

    def halo_copy(p, side, k):
        return pltpu.make_async_remote_copy(
            src_ref=hsend.at[p, halo_rows(p)], dst_ref=hrecv.at[p, 1 - side, core, halo_rows(p)],
            send_sem=halo_s.at[p, side], recv_sem=halo_r.at[p, 1 - side],
            device_id={"tile": me - 1 + 2 * side, "gene": core if k == 0 else other},
            device_id_type=MESH,
        )

    def halo_both(p, side):
        ref = hrecv.at[p, side, :, halo_rows(p)]
        return pltpu.make_async_remote_copy(
            src_ref=ref, dst_ref=ref, send_sem=halo_s.at[p, side], recv_sem=halo_r.at[p, side],
            device_id={"tile": lax.rem(me + 1, n)}, device_id_type=MESH,
        )

    def pair_copy(p):
        part = pl.ds(0, width + LANES if p == 0 else width)
        return pltpu.make_async_remote_copy(
            src_ref=nsend.at[p, :, part], dst_ref=nrecv.at[p, :, part],
            send_sem=pair_s.at[p], recv_sem=pair_r.at[p],
            device_id={"gene": other}, device_id_type=MESH,
        )

    rims, inner = slice(0, RIM), slice(RIM, width)

    def ratio_of(lhs, rows, at, size):
        product = jnp.dot(lhs, h_ref[:, pl.ds(at, size)], preferred_element_type=f32)
        return quotient(x_ref[rows, pl.ds(at, size)].astype(f32), product).astype(bf16)

    def numer_of(lhs, rows, begin):
        acc = None
        for c in range(genes // step):
            if begin is not None:
                begin(c)
            part = lax.dot_general(
                h_ref[:, pl.ds(c * step, step)], ratio_of(lhs, rows, c * step, step),
                (((1,), (1,)), ((), ())), preferred_element_type=f32,
            )
            acc = part if acc is None else acc + part
        return acc

    def put_halo(p, numer):
        hsend[p, 0:rank, rims] = (cells * mask)[:, rims] * numer

    wide = min(4 * step, genes)
    small[0].wait()
    small[1].wait()
    for c in range(loads):
        inner_load(c).start()
    cells = pltpu.roll(w_ref[...], BORDER, 1)
    mrow = pltpu.roll(jnp.broadcast_to(t_ref[...].astype(f32), (2 * SUB, width)), BORDER, 1)
    mask = jnp.broadcast_to(mrow[0:1], (rank, width))
    inside = mask > 0.0
    lane = lane_of((1, LANES))
    hsend[0, rank : rank + SUB, :] = jnp.where(lane_of((SUB, LANES)) < RIM, mrow[0:SUB, 0:LANES], 0.0)
    lhs = jnp.transpose(cells).astype(bf16)
    small[2].wait()
    for side in range(2):
        rim_load(side).wait()
    numer_rim = numer_of(lhs[rims], rims, None)
    put_halo(0, numer_rim)
    pl.semaphore_wait(
        barrier, n + has(0).astype(jnp.int32) + has(1).astype(jnp.int32)
    )

    def halo_start(p):
        for side in range(2):
            @pl.when(has(side))
            def _():
                halo_copy(p, side, 0).start()
                halo_copy(p, side, 1).start()

    halo_start(0)
    gsum_part = jnp.sum(h_ref[...].astype(f32), axis=1, keepdims=True)
    nsend[0, :, width : width + LANES] = jnp.broadcast_to(gsum_part, (rank, LANES))
    every = max(genes // loads // step, 1)

    def arrive(c):
        if c % every == 0:
            inner_load(c // every).wait()

    numer_inner = numer_of(lhs[inner], inner, arrive)
    blend = None
    for p in range(PASSES):
        nsend[p, :, rims] = numer_rim
        nsend[p, :, inner] = numer_inner
        pair_copy(p).start()
        if p == 0:
            small[3].wait()
            a = pltpu.roll(nb_ref[...], BORDER, 1) - (me * width - BORDER)
            spot = jnp.where(a < BORDER, a + width, a)
            spot = jnp.where(jnp.logical_and(a >= width, a < width + BORDER), a - width, spot)
            size = BORDER
            for at in range(0, width + LANES, size):
                index = lax.broadcasted_iota(jnp.int32, (size, width), 0) + at
                total = jnp.zeros((size, width), f32)
                for j in range(nb_ref.shape[0]):
                    total = total + jnp.where(spot[j : j + 1] == index, 1.0, 0.0)
                near_ref[at : at + size, :] = total.astype(bf16)
        pair_copy(p).wait_recv()
        if p == 0:
            inverse = 1.0 / (
                nsend[0, :, width : width + LANES] + nrecv[0, :, width : width + LANES]
            )
            inverse_wide = jnp.concatenate([inverse] * (width // LANES), axis=1)
        numer = nsend[p, :, 0:width] + nrecv[p, :, 0:width]
        updated = jnp.where(inside, cells * numer * inverse_wide, cells)
        stacked = jnp.concatenate(split(updated * mask) + (mrow.astype(bf16),), axis=0)
        mixed = jnp.dot(stacked, near_ref[0:width, :], preferred_element_type=f32)
        near = mixed[0:rank] + mixed[rank : 2 * rank]
        if p == 0:
            count = mixed[2 * rank : 2 * rank + 1]
        cells = jnp.where(
            inside,
            (1.0 - smooth_weight) * updated + smooth_weight * near / jnp.maximum(count, 1.0),
            updated,
        )
        lhs = jnp.transpose(cells).astype(bf16)
        if p + 1 < PASSES:
            numer_inner = numer_of(lhs[inner], inner, None)
        else:
            lift = jnp.concatenate(split(cells * mask), axis=0)[:, inner]
            for at in range(0, genes, wide):
                both = jnp.dot(
                    lift, ratio_of(lhs[inner], inner, at, wide), preferred_element_type=f32
                )
                acc_ref[:, pl.ds(at, wide)] = both[0:rank] + both[rank : 2 * rank]
        for side in range(2):
            @pl.when(has(side))
            def _():
                halo_both(p, side).wait_recv()
        before = hrecv[p, 0, 0, 0:rank] + hrecv[p, 0, 1, 0:rank]
        after = hrecv[p, 1, 0, 0:rank] + hrecv[p, 1, 1, 0:rank]
        halo = jnp.where(lane < BORDER, before, after) * inverse
        if p == 0:
            flags = jnp.where(
                lane_of((SUB, LANES)) < BORDER,
                hrecv[0, 0, 0, rank : rank + SUB], hrecv[0, 1, 0, rank : rank + SUB],
            )
            flags = jnp.concatenate([flags, flags], axis=0).astype(bf16)
        stacked = jnp.concatenate(split(halo) + (flags,), axis=0)
        mixed = jnp.dot(
            stacked, near_ref[width : width + LANES, 0:LANES], preferred_element_type=f32
        )
        near_rim = near[:, 0:LANES] + (mixed[0:rank] + mixed[rank : 2 * rank])
        if p == 0:
            count_rim = jnp.maximum(count[:, 0:LANES] + mixed[2 * rank : 2 * rank + 1], 1.0)
        rim = updated[:, 0:LANES]
        rim = jnp.where(
            inside[:, 0:LANES],
            (1.0 - smooth_weight) * rim + smooth_weight * near_rim / count_rim,
            rim,
        )
        cells = jnp.concatenate([rim, cells[:, LANES:]], axis=1)
        lhs = jnp.transpose(rim).astype(bf16)[rims]
        if p + 1 < PASSES:
            numer_rim = numer_of(lhs, rims, None)
            put_halo(p + 1, numer_rim)
            halo_start(p + 1)

    weighted = cells * mask
    den_part = jnp.sum(weighted, axis=1, keepdims=True)
    lift = jnp.concatenate(split(weighted[:, 0:LANES]), axis=0)[:, rims]

    blk = cols // quarters

    def when_owner(index, call):
        if owners == n:
            call()
        else:
            pl.when(index < owners)(call)

    def move(src, dst, ssem, rsem, tile):
        return pltpu.make_async_remote_copy(
            src_ref=src, dst_ref=dst, send_sem=ssem, recv_sem=rsem,
            device_id={"tile": tile}, device_id_type=MESH,
        )

    def part_start(q, j):
        o = lax.rem(me + j, n)

        def call():
            slot = n - 1 - j
            move(psend.at[q * owners + o], precv.at[q, slot], p_s, p_r.at[q], o).start()

        when_owner(o, call)

    def unit_start(j):
        o = lax.rem(me + j, n)
        when_owner(
            o,
            lambda: move(
                usend.at[pl.ds(0, 1)], urecv.at[pl.ds(n - 1 - j, 1)], u_s, u_r, o
            ).start(),
        )

    def all_peers(call):
        if few:
            for j in range(1, n):
                call(j)
        else:
            def body(j, carry):
                call(j)
                return carry

            lax.fori_loop(1, n, body, 0)

    top = jnp.full((rank, 1), 1e-30, f32)
    for at in range(0, genes, wide):
        both = jnp.dot(lift, ratio_of(lhs, rims, at, wide), preferred_element_type=f32)
        total = acc_ref[:, pl.ds(at, wide)] + (both[0:rank] + both[rank : 2 * rank])
        acc_ref[:, pl.ds(at, wide)] = total
        top = jnp.maximum(top, jnp.max(total, axis=1, keepdims=True))
    usend[...] = jnp.broadcast_to(row_of((top * (1.0 / TOP), den_part)), usend.shape)
    all_peers(unit_start)
    scale = TOP / top
    for q in range(quarters):
        for o in range(owners):
            value = acc_ref[:, pl.ds(o * cols + q * blk, blk)] * scale + (0.5 - HALF)
            psend[q * owners + o] = jnp.floor(value).astype(jnp.int32).astype(WIRE)
        all_peers(lambda j: part_start(q, j))
    cells_ref[...] = pltpu.roll(cells, width - BORDER, 1)

    def gene_piece(q):
        return genes_ref.at[:, pl.ds(pl.multiple_of(me * cols + q * blk, LANES), blk)]

    def finish_part():
        ahead = lax.rem(me + 1, n)
        rows = urecv.at[pl.ds(0, n - 1)]
        move(rows, rows, u_s, u_r, ahead).wait_recv()
        units = jnp.transpose(urecv[...])
        den = den_part + jnp.sum(units[rank : 2 * rank, 0 : n - 1], axis=1, keepdims=True)
        inverse_den = 1.0 / den
        for q in range(quarters):
            here = pl.ds(pl.multiple_of(me * cols + q * blk, LANES), blk)
            total = acc_ref[:, here]
            move(precv.at[q], precv.at[q], p_s, p_r.at[q], ahead).wait_recv()
            for slot in range(n - 1):
                value = precv[q, slot].astype(jnp.int32).astype(f32) + HALF
                total = total + value * units[0:rank, slot : slot + 1]
            lead = h_ref[:, here].astype(f32) * inverse_den
            genes_ref[:, here] = (lead * total).astype(genes_ref.dtype)
            all_peers(
                lambda j: move(
                    gene_piece(q), gene_piece(q), g_s, g_r, lax.rem(me + j, n)
                ).start()
            )

    def wait_all(owned):
        others = owners - 1 if owned else owners
        ahead = lax.rem(me + 1, n)
        ref = genes_ref.at[:, pl.ds(0, others * cols)]
        move(ref, ref, g_s, g_r, ahead).wait_recv()
        sent = pl.ds(0, quarters * others)
        move(psend.at[sent], psend.at[sent], p_s, g_r, ahead).wait_send()
        rows = urecv.at[pl.ds(0, others)]
        move(rows, rows, u_s, g_r, ahead).wait_send()
        if owned:
            move(precv, precv, g_s, g_r, ahead).wait_send()

    when_owner(me, finish_part)
    when_owner(me, lambda: wait_all(True))
    if owners < n:
        pl.when(me >= owners)(lambda: wait_all(False))
    for p in range(PASSES):
        pair_copy(p).wait_send()
        for side in range(2):
            @pl.when(has(side))
            def _():
                halo_both(p, side).wait_send()


def settle(cells_in, genes_in, cells_ref, genes_ref):
    cells_ref[...] = cells_in[...]
    genes_ref[...] = genes_in[...]


def on_device(n, counts, cell_factor, gene_factor, tissue, neighbours):
    width, genes = counts.shape
    rank = cell_factor.shape[0]
    near = neighbours.shape[0]
    owners = min(n, genes // LANES)
    step = min(512, genes)
    loads = min(2, genes // step)
    cols = genes // owners
    quarters = max(1, min(4, cols // LANES))
    dma = pltpu.SemaphoreType.DMA
    vmem = pl.BlockSpec(memory_space=pltpu.VMEM)
    shapes = (
        jax.ShapeDtypeStruct((rank, width), f32),
        jax.ShapeDtypeStruct((rank, genes), bf16),
    )
    results = pl.pallas_call(
        functools.partial(kernel, n, owners, quarters, step, loads),
        out_shape=tuple(pltpu.VMEM(s.shape, s.dtype) for s in shapes),
        in_specs=[pl.BlockSpec(memory_space=pl.ANY)] * 5,
        out_specs=(vmem, vmem),
        scratch_shapes=[
            pltpu.VMEM((width, genes), jnp.int32),
            pltpu.VMEM((rank, width), f32),
            pltpu.VMEM((rank, genes), bf16),
            pltpu.VMEM((1, width), jnp.int32),
            pltpu.VMEM((near, width), jnp.int32),
            pltpu.VMEM((width + LANES, width), bf16),
            pltpu.VMEM((rank, genes), f32),
            pltpu.VMEM((PASSES, rank, width + LANES), f32),
            pltpu.VMEM((PASSES, rank, width + LANES), f32),
            pltpu.VMEM((PASSES, rank + SUB, LANES), f32),
            pltpu.VMEM((PASSES, 2, 2, rank + SUB, LANES), f32),
            pltpu.VMEM((quarters * owners, rank, cols // quarters), WIRE),
            pltpu.VMEM((quarters, n - 1, rank, cols // quarters), WIRE),
            pltpu.VMEM((SUB, LANES), f32),
            pltpu.VMEM((pl.cdiv(n, LANES) * LANES, LANES), f32),
            dma((4,)),
            dma((2,)),
            dma((loads,)),
            dma((PASSES,)),
            dma((PASSES,)),
            dma((PASSES, 2)),
            dma((PASSES, 2)),
            dma,
            dma((quarters,)),
            dma,
            dma,
            dma,
            dma,
        ],
        compiler_params=pltpu.CompilerParams(
            collective_id=0, has_side_effects=True, vmem_limit_bytes=63_160_000
        ),
    )(counts, cell_factor, gene_factor, tissue.reshape(1, width), neighbours)
    return pl.pallas_call(
        settle, out_shape=shapes, in_specs=[vmem] * 2, out_specs=(vmem, vmem),
        compiler_params=pltpu.CompilerParams(vmem_limit_bytes=16 * 1024 * 1024),
    )(*results)


def solution(mesh):
    return jax.shard_map(
        functools.partial(on_device, mesh.shape["tile"]),
        mesh=mesh,
        in_specs=(
            P(("grp", "tile"), "gene"),
            P(None, ("grp", "tile")),
            P(None, ("grp", "gene")),
            P(("grp", "tile")),
            P(None, ("grp", "tile")),
        ),
        out_specs=(P(None, ("grp", "tile")), P(None, ("grp", "gene"))),
        check_vma=False,
    )
```

```python
import functools

import jax
import jax.numpy as jnp
from jax import lax
from jax.experimental import pallas as pl
from jax.experimental.pallas import tpu as pltpu
from jax.sharding import PartitionSpec as P

BORDER = 32
RIM = 2 * BORDER
PASSES = 2
LANES = 128
SUB = 8
MESH = pl.DeviceIdType.MESH
WIRE = jnp.int16
TOP = 65000.0
HALF = 32768.0

smooth_weight = 0.5

f32 = jnp.float32
bf16 = jnp.bfloat16


def split(value):
    high = value.astype(bf16)
    low = (value - high.astype(f32)).astype(bf16)
    return high, low


def quotient(top, bottom):
    r = pl.reciprocal(bottom, approx=True)
    return top * (r * (2.0 - bottom * r))


def lane_of(shape):
    return lax.broadcasted_iota(jnp.int32, shape, 1)


def row_of(columns):
    rank = columns[0].shape[0]
    index = lax.broadcasted_iota(jnp.int32, (rank, LANES), 0)
    lane = lane_of((rank, LANES))
    spread = jnp.zeros((rank, LANES), f32)
    for g, column in enumerate(columns):
        spread = jnp.where(lane == index + g * rank, column, spread)
    return jnp.sum(spread, axis=0, keepdims=True)


def kernel(
    n, owners, quarters, relays, step, loads,
    x_hbm, w_hbm, h_hbm, t_hbm, nb_hbm,
    cells_ref, genes_ref,
    x_ref, w_ref, h_ref, t_ref, nb_ref, near_ref, acc_ref, halo_ref,
    nsend, nrecv, hsend, hrecv, psend, precv, stage, usend, urecv,
    in_sem, e_sem, x_sem, pair_s, pair_r, halo_s, halo_r,
    p_s, p_r, stage_r, u_s, u_r, g_s, g_r,
):
    rank, width = w_ref.shape
    genes = h_ref.shape[1]
    cols = genes // owners
    me = lax.axis_index("tile")
    core = lax.axis_index("gene")
    other = 1 - core
    barrier = pltpu.get_barrier_semaphore()

    small = [
        pltpu.make_async_copy(src, dst, in_sem.at[i])
        for i, (src, dst) in enumerate(
            ((w_hbm, w_ref), (t_hbm, t_ref), (h_hbm, h_ref), (nb_hbm, nb_ref))
        )
    ]

    def rim_load(side):
        source = pl.ds((width - BORDER, 0)[side], BORDER)
        return pltpu.make_async_copy(
            x_hbm.at[source], x_ref.at[pl.ds(side * BORDER, BORDER)], e_sem.at[side]
        )

    def inner_load(c):
        size = genes // loads
        part = pl.ds(c * size, size)
        return pltpu.make_async_copy(
            x_hbm.at[pl.ds(BORDER, width - RIM), part],
            x_ref.at[pl.ds(RIM, width - RIM), part],
            x_sem.at[c],
        )

    for copy in small[:3]:
        copy.start()
    for side in range(2):
        rim_load(side).start()
    small[3].start()

    def has(side):
        return me > 0 if side == 0 else me < n - 1

    def greet(i, carry):
        pl.semaphore_signal(
            barrier, inc=1, device_id={"tile": lax.rem(me + i, n)}, device_id_type=MESH
        )
        return carry

    few = n <= 16
    lax.fori_loop(1, n, greet, 0, unroll=few)
    pl.semaphore_signal(barrier, inc=1, device_id={"gene": other}, device_id_type=MESH)
    for side in range(2):
        @pl.when(has(side))
        def _():
            pl.semaphore_signal(
                barrier, inc=1, device_id={"tile": me - 1 + 2 * side, "gene": other},
                device_id_type=MESH,
            )

    for side in range(2):
        @pl.when(jnp.logical_not(has(side)))
        def _():
            hrecv[:, side] = jnp.zeros(hrecv.shape[:1] + hrecv.shape[2:], f32)
    halo_ref[...] = jnp.zeros_like(halo_ref)

    def halo_rows(p):
        return pl.ds(0, 2 * SUB if p == 0 else SUB)

    def halo_copy(p, side, k):
        return pltpu.make_async_remote_copy(
            src_ref=hsend.at[p, side, halo_rows(p)], dst_ref=hrecv.at[p, 1 - side, core, halo_rows(p)],
            send_sem=halo_s.at[p, side], recv_sem=halo_r.at[p, 1 - side],
            device_id={"tile": me - 1 + 2 * side, "gene": core if k == 0 else other},
            device_id_type=MESH,
        )

    def halo_both(p, side):
        ref = hrecv.at[p, side, :, halo_rows(p)]
        return pltpu.make_async_remote_copy(
            src_ref=ref, dst_ref=ref, send_sem=halo_s.at[p, side], recv_sem=halo_r.at[p, side],
            device_id={"tile": lax.rem(me + 1, n)}, device_id_type=MESH,
        )

    def pair_copy(p):
        part = pl.ds(0, width + LANES if p == 0 else width)
        return pltpu.make_async_remote_copy(
            src_ref=nsend.at[p, :, part], dst_ref=nrecv.at[p, :, part],
            send_sem=pair_s.at[p], recv_sem=pair_r.at[p],
            device_id={"gene": other}, device_id_type=MESH,
        )

    rims, inner = slice(0, RIM), slice(RIM, width)

    def ratio_of(lhs, rows, at, size):
        product = jnp.dot(lhs, h_ref[:, pl.ds(at, size)], preferred_element_type=f32)
        return quotient(x_ref[rows, pl.ds(at, size)].astype(f32), product).astype(bf16)

    def numer_of(lhs, rows, begin):
        acc = None
        for c in range(genes // step):
            if begin is not None:
                begin(c)
            part = lax.dot_general(
                h_ref[:, pl.ds(c * step, step)], ratio_of(lhs, rows, c * step, step),
                (((1,), (1,)), ((), ())), preferred_element_type=f32,
            )
            acc = part if acc is None else acc + part
        return acc

    def put_halo(p, numer):
        value = (cells * mask)[:, rims] * numer
        for side, first in enumerate((BORDER, 0)):
            for g in range(rank // SUB):
                hsend[p, side, 0:SUB, g * BORDER : (g + 1) * BORDER] = value[
                    g * SUB : (g + 1) * SUB, first : first + BORDER
                ]

    wide = min(4 * step, genes)
    small[0].wait()
    small[1].wait()
    for c in range(loads):
        inner_load(c).start()
    cells = pltpu.roll(w_ref[...], BORDER, 1)
    mrow = pltpu.roll(jnp.broadcast_to(t_ref[...].astype(f32), (2 * SUB, width)), BORDER, 1)
    mask = jnp.broadcast_to(mrow[0:1], (rank, width))
    inside = mask > 0.0
    for side in range(2):
        hsend[0, side, SUB : 2 * SUB, 0:LANES] = jnp.where(
            lane_of((SUB, LANES)) < RIM, mrow[0:SUB, 0:LANES], 0.0
        )
    lhs = jnp.transpose(cells).astype(bf16)
    small[2].wait()
    for side in range(2):
        rim_load(side).wait()
    numer_rim = numer_of(lhs[rims], rims, None)
    put_halo(0, numer_rim)
    pl.semaphore_wait(
        barrier, n + has(0).astype(jnp.int32) + has(1).astype(jnp.int32)
    )

    def halo_start(p):
        for side in range(2):
            @pl.when(has(side))
            def _():
                halo_copy(p, side, 0).start()
                halo_copy(p, side, 1).start()

    halo_start(0)
    gsum_part = jnp.sum(h_ref[...].astype(f32), axis=1, keepdims=True)
    nsend[0, :, width : width + LANES] = jnp.broadcast_to(gsum_part, (rank, LANES))
    every = max(genes // loads // step, 1)

    def arrive(c):
        if c % every == 0:
            inner_load(c // every).wait()

    numer_inner = numer_of(lhs[inner], inner, arrive)
    blend = None
    for p in range(PASSES):
        nsend[p, :, rims] = numer_rim
        nsend[p, :, inner] = numer_inner
        pair_copy(p).start()
        if p == 0:
            small[3].wait()
            a = pltpu.roll(nb_ref[...], BORDER, 1) - (me * width - BORDER)
            spot = jnp.where(a < BORDER, a + width, a)
            spot = jnp.where(jnp.logical_and(a >= width, a < width + BORDER), a - width, spot)
            size = BORDER
            for at in range(0, width + LANES, size):
                index = lax.broadcasted_iota(jnp.int32, (size, width), 0) + at
                total = jnp.zeros((size, width), f32)
                for j in range(nb_ref.shape[0]):
                    total = total + jnp.where(spot[j : j + 1] == index, 1.0, 0.0)
                near_ref[at : at + size, :] = total.astype(bf16)
        pair_copy(p).wait_recv()
        if p == 0:
            inverse = 1.0 / (
                nsend[0, :, width : width + LANES] + nrecv[0, :, width : width + LANES]
            )
            inverse_wide = jnp.concatenate([inverse] * (width // LANES), axis=1)
        numer = nsend[p, :, 0:width] + nrecv[p, :, 0:width]
        updated = jnp.where(inside, cells * numer * inverse_wide, cells)
        stacked = jnp.concatenate(split(updated * mask) + (mrow.astype(bf16),), axis=0)
        mixed = jnp.dot(stacked, near_ref[0:width, :], preferred_element_type=f32)
        near = mixed[0:rank] + mixed[rank : 2 * rank]
        if p == 0:
            count = mixed[2 * rank : 2 * rank + 1]
        cells = jnp.where(
            inside,
            (1.0 - smooth_weight) * updated + smooth_weight * near / jnp.maximum(count, 1.0),
            updated,
        )
        lhs = jnp.transpose(cells).astype(bf16)
        if p + 1 < PASSES:
            numer_inner = numer_of(lhs[inner], inner, None)
        else:
            lift = jnp.concatenate(split(cells * mask), axis=0)[:, inner]
            for at in range(0, genes, wide):
                both = jnp.dot(
                    lift, ratio_of(lhs[inner], inner, at, wide), preferred_element_type=f32
                )
                acc_ref[:, pl.ds(at, wide)] = both[0:rank] + both[rank : 2 * rank]
        for side in range(2):
            @pl.when(has(side))
            def _():
                halo_both(p, side).wait_recv()
        for side in range(2):
            packed = hrecv[p, side, 0, 0:SUB] + hrecv[p, side, 1, 0:SUB]
            for g in range(rank // SUB):
                halo_ref[g * SUB : (g + 1) * SUB, side * BORDER : (side + 1) * BORDER] = packed[
                    :, g * BORDER : (g + 1) * BORDER
                ]
        halo = halo_ref[...] * inverse
        if p == 0:
            flags = jnp.where(
                lane_of((SUB, LANES)) < BORDER,
                hrecv[0, 0, 0, SUB : 2 * SUB, 0:LANES], hrecv[0, 1, 0, SUB : 2 * SUB, 0:LANES],
            )
            flags = jnp.concatenate([flags, flags], axis=0).astype(bf16)
        stacked = jnp.concatenate(split(halo) + (flags,), axis=0)
        mixed = jnp.dot(
            stacked, near_ref[width : width + LANES, 0:LANES], preferred_element_type=f32
        )
        near_rim = near[:, 0:LANES] + (mixed[0:rank] + mixed[rank : 2 * rank])
        if p == 0:
            count_rim = jnp.maximum(count[:, 0:LANES] + mixed[2 * rank : 2 * rank + 1], 1.0)
        rim = updated[:, 0:LANES]
        rim = jnp.where(
            inside[:, 0:LANES],
            (1.0 - smooth_weight) * rim + smooth_weight * near_rim / count_rim,
            rim,
        )
        cells = jnp.concatenate([rim, cells[:, LANES:]], axis=1)
        lhs = jnp.transpose(rim).astype(bf16)[rims]
        if p + 1 < PASSES:
            numer_rim = numer_of(lhs, rims, None)
            put_halo(p + 1, numer_rim)
            halo_start(p + 1)

    weighted = cells * mask
    den_part = jnp.sum(weighted, axis=1, keepdims=True)
    lift = jnp.concatenate(split(weighted[:, 0:LANES]), axis=0)[:, rims]

    blk = cols // quarters

    relayed = range(quarters - relays, quarters)
    even = lax.rem(me, 2) == 0
    mate = me + 1 - 2 * lax.rem(me, 2)
    far = lax.rem(me + n // 2, n)
    far_mate = far + 1 - 2 * lax.rem(far, 2)

    def when_owner(index, call):
        if owners == n:
            call()
        else:
            pl.when(index < owners)(call)

    def move(src, dst, ssem, rsem, tile):
        return pltpu.make_async_remote_copy(
            src_ref=src, dst_ref=dst, send_sem=ssem, recv_sem=rsem,
            device_id={"tile": tile}, device_id_type=MESH,
        )

    def part_start(q, j):
        o = lax.rem(me + j, n)

        def call():
            slot = n - 1 - j
            move(psend.at[q * owners + o], precv.at[q, slot], p_s, p_r.at[q], o).start()

        if q in relayed:
            if j in (n // 2 - 1, n // 2 + 1):
                pl.when(o != far_mate)(call)
            elif j != n // 2:
                call()
        else:
            when_owner(o, call)

    def unit_start(j):
        o = lax.rem(me + j, n)
        when_owner(
            o,
            lambda: move(
                usend.at[pl.ds(0, 1)], urecv.at[pl.ds(n - 1 - j, 1)], u_s, u_r, o
            ).start(),
        )

    def all_peers(call):
        if few:
            for j in range(1, n):
                call(j)
        else:
            def body(j, carry):
                call(j)
                return carry

            lax.fori_loop(1, n, body, 0)

    top = jnp.full((rank, 1), 1e-30, f32)
    for at in range(0, genes, wide):
        both = jnp.dot(lift, ratio_of(lhs, rims, at, wide), preferred_element_type=f32)
        total = acc_ref[:, pl.ds(at, wide)] + (both[0:rank] + both[rank : 2 * rank])
        acc_ref[:, pl.ds(at, wide)] = total
        top = jnp.maximum(top, jnp.max(total, axis=1, keepdims=True))
    usend[...] = jnp.broadcast_to(row_of((top * (1.0 / TOP), den_part)), usend.shape)
    all_peers(unit_start)
    scale = TOP / top
    for q in range(quarters):
        for o in range(owners):
            value = acc_ref[:, pl.ds(o * cols + q * blk, blk)] * scale + (0.5 - HALF)
            psend[q * owners + o] = jnp.floor(value).astype(jnp.int32).astype(WIRE)
    for i, q in enumerate(relayed):
        move(psend.at[q * owners + far_mate], stage.at[i], p_s, stage_r.at[i], mate).start()
    for q in range(quarters):
        all_peers(lambda j: part_start(q, j))
    cells_ref[...] = pltpu.roll(cells, width - BORDER, 1)

    def gene_piece(q):
        return genes_ref.at[:, pl.ds(pl.multiple_of(me * cols + q * blk, LANES), blk)]

    def finish_part():
        ahead = lax.rem(me + 1, n)
        rows = urecv.at[pl.ds(0, n - 1)]
        move(rows, rows, u_s, u_r, ahead).wait_recv()
        units = jnp.transpose(urecv[...])
        den = den_part + jnp.sum(units[rank : 2 * rank, 0 : n - 1], axis=1, keepdims=True)
        inverse_den = 1.0 / den
        unit_of = [units[0:rank, slot : slot + 1] for slot in range(n - 1)]
        if relays:
            unit_mate = jnp.where(even, unit_of[0], unit_of[n - 2])
            joint = 1.0 / (top * (1.0 / TOP) + unit_mate)
            middle = n // 2 - 1
            joint_of = list(unit_of)
            joint_of[middle] += jnp.where(even, unit_of[middle + 1], unit_of[middle - 1])
            joint_of[middle + 1] = jnp.where(even, 0.0, unit_of[middle + 1])
            joint_of[middle - 1] = jnp.where(even, unit_of[middle - 1], 0.0)
        for i, q in enumerate(relayed):
            move(stage.at[i], stage.at[i], p_s, stage_r.at[i], ahead).wait_recv()
            there = pl.ds(pl.multiple_of(far * cols + q * blk, LANES), blk)
            value = (stage[i].astype(jnp.int32).astype(f32) + HALF) * unit_mate
            value = (acc_ref[:, there] + value) * joint + (0.5 - HALF)
            psend[q * owners + far] = jnp.floor(value).astype(jnp.int32).astype(WIRE)
            move(
                psend.at[q * owners + far], precv.at[q, middle], p_s, p_r.at[q], far
            ).start()
        for q in range(quarters):
            here = pl.ds(pl.multiple_of(me * cols + q * blk, LANES), blk)
            total = acc_ref[:, here]
            come = precv.at[q, pl.ds(0, n - 2 if q in relayed else n - 1)]
            move(come, come, p_s, p_r.at[q], ahead).wait_recv()
            for slot in range(n - 1):
                value = precv[q, slot].astype(jnp.int32).astype(f32) + HALF
                total = total + value * (joint_of if q in relayed else unit_of)[slot]
            lead = h_ref[:, here].astype(f32) * inverse_den
            genes_ref[:, here] = (lead * total).astype(genes_ref.dtype)
            all_peers(
                lambda j: move(
                    gene_piece(q), gene_piece(q), g_s, g_r, lax.rem(me + j, n)
                ).start()
            )

    def wait_all(owned):
        others = owners - 1 if owned else owners
        ahead = lax.rem(me + 1, n)
        ref = genes_ref.at[:, pl.ds(0, others * cols)]
        move(ref, ref, g_s, g_r, ahead).wait_recv()
        sent = pl.ds(0, quarters * others)
        move(psend.at[sent], psend.at[sent], p_s, g_r, ahead).wait_send()
        rows = urecv.at[pl.ds(0, others)]
        move(rows, rows, u_s, g_r, ahead).wait_send()
        if owned:
            move(precv, precv, g_s, g_r, ahead).wait_send()

    when_owner(me, finish_part)
    when_owner(me, lambda: wait_all(True))
    if owners < n:
        pl.when(me >= owners)(lambda: wait_all(False))
    for p in range(PASSES):
        pair_copy(p).wait_send()
        for side in range(2):
            @pl.when(has(side))
            def _():
                halo_both(p, side).wait_send()


def settle(cells_in, genes_in, cells_ref, genes_ref):
    cells_ref[...] = cells_in[...]
    genes_ref[...] = genes_in[...]


def on_device(n, counts, cell_factor, gene_factor, tissue, neighbours):
    width, genes = counts.shape
    rank = cell_factor.shape[0]
    near = neighbours.shape[0]
    owners = min(n, genes // LANES)
    step = min(512, genes)
    loads = min(2, genes // step)
    cols = genes // owners
    quarters = max(1, min(4, cols // LANES))
    relays = quarters // 2 if n == owners and n % 4 == 0 and n <= 16 else 0
    dma = pltpu.SemaphoreType.DMA
    vmem = pl.BlockSpec(memory_space=pltpu.VMEM)
    shapes = (
        jax.ShapeDtypeStruct((rank, width), f32),
        jax.ShapeDtypeStruct((rank, genes), bf16),
    )
    results = pl.pallas_call(
        functools.partial(kernel, n, owners, quarters, relays, step, loads),
        out_shape=tuple(pltpu.VMEM(s.shape, s.dtype) for s in shapes),
        in_specs=[pl.BlockSpec(memory_space=pl.ANY)] * 5,
        out_specs=(vmem, vmem),
        scratch_shapes=[
            pltpu.VMEM((width, genes), jnp.int32),
            pltpu.VMEM((rank, width), f32),
            pltpu.VMEM((rank, genes), bf16),
            pltpu.VMEM((1, width), jnp.int32),
            pltpu.VMEM((near, width), jnp.int32),
            pltpu.VMEM((width + LANES, width), bf16),
            pltpu.VMEM((rank, genes), f32),
            pltpu.VMEM((rank, LANES), f32),
            pltpu.VMEM((PASSES, rank, width + LANES), f32),
            pltpu.VMEM((PASSES, rank, width + LANES), f32),
            pltpu.VMEM((PASSES, 2, 2 * SUB, max(rank // SUB * BORDER, LANES)), f32),
            pltpu.VMEM((PASSES, 2, 2, 2 * SUB, max(rank // SUB * BORDER, LANES)), f32),
            pltpu.VMEM((quarters * owners, rank, cols // quarters), WIRE),
            pltpu.VMEM((quarters, n - 1, rank, cols // quarters), WIRE),
            pltpu.VMEM((max(relays, 1), rank, cols // quarters), WIRE),
            pltpu.VMEM((SUB, LANES), f32),
            pltpu.VMEM((pl.cdiv(n, LANES) * LANES, LANES), f32),
            dma((4,)),
            dma((2,)),
            dma((loads,)),
            dma((PASSES,)),
            dma((PASSES,)),
            dma((PASSES, 2)),
            dma((PASSES, 2)),
            dma,
            dma((quarters,)),
            dma((max(relays, 1),)),
            dma,
            dma,
            dma,
            dma,
        ],
        compiler_params=pltpu.CompilerParams(
            collective_id=0, has_side_effects=True, vmem_limit_bytes=63_160_000
        ),
    )(counts, cell_factor, gene_factor, tissue.reshape(1, width), neighbours)
    return pl.pallas_call(
        settle, out_shape=shapes, in_specs=[vmem] * 2, out_specs=(vmem, vmem),
        compiler_params=pltpu.CompilerParams(vmem_limit_bytes=16 * 1024 * 1024),
    )(*results)


def solution(mesh):
    return jax.shard_map(
        functools.partial(on_device, mesh.shape["tile"]),
        mesh=mesh,
        in_specs=(
            P(("grp", "tile"), "gene"),
            P(None, ("grp", "tile")),
            P(None, ("grp", "gene")),
            P(("grp", "tile")),
            P(None, ("grp", "tile")),
        ),
        out_specs=(P(None, ("grp", "tile")), P(None, ("grp", "gene"))),
        check_vma=False,
    )
```

```python
import functools

import jax
import jax.numpy as jnp
from jax import lax
from jax.experimental import pallas as pl
from jax.experimental.pallas import tpu as pltpu
from jax.sharding import PartitionSpec as P

BORDER = 32
RIM = 2 * BORDER
PASSES = 2
LANES = 128
SUB = 8
MESH = pl.DeviceIdType.MESH
WIRE = jnp.int16
TOP = 65000.0
HALF = 32768.0

smooth_weight = 0.5

f32 = jnp.float32
bf16 = jnp.bfloat16


def split(value):
    high = value.astype(bf16)
    low = (value - high.astype(f32)).astype(bf16)
    return high, low


def quotient(top, bottom):
    r = pl.reciprocal(bottom, approx=True)
    return top * (r * (2.0 - bottom * r))


def lane_of(shape):
    return lax.broadcasted_iota(jnp.int32, shape, 1)


def row_of(columns):
    rank = columns[0].shape[0]
    index = lax.broadcasted_iota(jnp.int32, (rank, LANES), 0)
    lane = lane_of((rank, LANES))
    spread = jnp.zeros((rank, LANES), f32)
    for g, column in enumerate(columns):
        spread = jnp.where(lane == index + g * rank, column, spread)
    return jnp.sum(spread, axis=0, keepdims=True)


def kernel(
    n, owners, quarters, relays, step, loads,
    x_hbm, w_hbm, h_hbm, t_hbm, nb_hbm,
    cells_ref, genes_ref,
    x_ref, w_ref, h_ref, t_ref, nb_ref, near_ref, acc_ref, halo_ref,
    nsend, nrecv, hsend, hrecv, psend, precv, stage, usend, urecv,
    in_sem, e_sem, x_sem, pair_s, pair_r, halo_s, halo_r,
    p_s, p_r, stage_r, u_s, u_r, g_s, g_r, f_r,
):
    rank, width = w_ref.shape
    genes = h_ref.shape[1]
    cols = genes // owners
    me = lax.axis_index("tile")
    core = lax.axis_index("gene")
    other = 1 - core
    barrier = pltpu.get_barrier_semaphore()

    small = [
        pltpu.make_async_copy(src, dst, in_sem.at[i])
        for i, (src, dst) in enumerate(
            ((w_hbm, w_ref), (t_hbm, t_ref), (nb_hbm, nb_ref), (h_hbm, h_ref))
        )
    ]

    def rim_load(side):
        source = pl.ds((width - BORDER, 0)[side], BORDER)
        return pltpu.make_async_copy(
            x_hbm.at[source], x_ref.at[pl.ds(side * BORDER, BORDER)], e_sem.at[side]
        )

    def inner_load(c):
        size = genes // loads
        part = pl.ds(c * size, size)
        return pltpu.make_async_copy(
            x_hbm.at[pl.ds(BORDER, width - RIM), part],
            x_ref.at[pl.ds(RIM, width - RIM), part],
            x_sem.at[c],
        )

    for copy in small:
        copy.start()
    for side in range(2):
        rim_load(side).start()

    def has(side):
        return me > 0 if side == 0 else me < n - 1

    def greet(i, carry):
        pl.semaphore_signal(
            barrier, inc=1, device_id={"tile": lax.rem(me + i, n)}, device_id_type=MESH
        )
        return carry

    few = n <= 16
    lax.fori_loop(1, n, greet, 0, unroll=few)
    pl.semaphore_signal(barrier, inc=1, device_id={"gene": other}, device_id_type=MESH)
    for side in range(2):
        @pl.when(has(side))
        def _():
            pl.semaphore_signal(
                barrier, inc=1, device_id={"tile": me - 1 + 2 * side, "gene": other},
                device_id_type=MESH,
            )

    for side in range(2):
        @pl.when(jnp.logical_not(has(side)))
        def _():
            hrecv[:, side] = jnp.zeros(hrecv.shape[:1] + hrecv.shape[2:], f32)
    halo_ref[...] = jnp.zeros_like(halo_ref)

    def halo_rows(p):
        return pl.ds(0, 2 * SUB if p == 0 else SUB)

    def halo_copy(p, side, k):
        return pltpu.make_async_remote_copy(
            src_ref=hsend.at[p, side, halo_rows(p)], dst_ref=hrecv.at[p, 1 - side, core, halo_rows(p)],
            send_sem=halo_s.at[p, side], recv_sem=halo_r.at[p, 1 - side],
            device_id={"tile": me - 1 + 2 * side, "gene": core if k == 0 else other},
            device_id_type=MESH,
        )

    def halo_both(p, side):
        ref = hrecv.at[p, side, :, halo_rows(p)]
        return pltpu.make_async_remote_copy(
            src_ref=ref, dst_ref=ref, send_sem=halo_s.at[p, side], recv_sem=halo_r.at[p, side],
            device_id={"tile": lax.rem(me + 1, n)}, device_id_type=MESH,
        )

    def pair_copy(p):
        part = pl.ds(0, width + LANES if p == 0 else width)
        return pltpu.make_async_remote_copy(
            src_ref=nsend.at[p, :, part], dst_ref=nrecv.at[p, :, part],
            send_sem=pair_s.at[p], recv_sem=pair_r.at[p],
            device_id={"gene": other}, device_id_type=MESH,
        )

    rims, inner = slice(0, RIM), slice(RIM, width)

    def ratio_of(lhs, rows, at, size):
        product = jnp.dot(lhs, h_ref[:, pl.ds(at, size)], preferred_element_type=f32)
        return quotient(x_ref[rows, pl.ds(at, size)].astype(f32), product).astype(bf16)

    def numer_of(lhs, rows, begin):
        acc = None
        for c in range(genes // step):
            if begin is not None:
                begin(c)
            part = lax.dot_general(
                h_ref[:, pl.ds(c * step, step)], ratio_of(lhs, rows, c * step, step),
                (((1,), (1,)), ((), ())), preferred_element_type=f32,
            )
            acc = part if acc is None else acc + part
        return acc

    def put_halo(p, numer):
        value = (cells * mask)[:, rims] * numer
        for side, first in enumerate((BORDER, 0)):
            for g in range(rank // SUB):
                hsend[p, side, 0:SUB, g * BORDER : (g + 1) * BORDER] = value[
                    g * SUB : (g + 1) * SUB, first : first + BORDER
                ]

    wide = min(4 * step, genes)
    small[0].wait()
    small[1].wait()
    for c in range(loads):
        inner_load(c).start()
    cells = pltpu.roll(w_ref[...], BORDER, 1)
    mrow = pltpu.roll(jnp.broadcast_to(t_ref[...].astype(f32), (2 * SUB, width)), BORDER, 1)
    mask = jnp.broadcast_to(mrow[0:1], (rank, width))
    inside = mask > 0.0
    for side in range(2):
        hsend[0, side, SUB : 2 * SUB, 0:LANES] = jnp.where(
            lane_of((SUB, LANES)) < RIM, mrow[0:SUB, 0:LANES], 0.0
        )
    lhs = jnp.transpose(cells).astype(bf16)
    small[2].wait()
    a = pltpu.roll(nb_ref[...], BORDER, 1) - (me * width - BORDER)
    spot = jnp.where(a < BORDER, a + width, a)
    spot = jnp.where(jnp.logical_and(a >= width, a < width + BORDER), a - width, spot)
    for at in range(0, width + LANES, BORDER):
        index = lax.broadcasted_iota(jnp.int32, (BORDER, width), 0) + at
        total = jnp.zeros((BORDER, width), f32)
        for j in range(nb_ref.shape[0]):
            total = total + jnp.where(spot[j : j + 1] == index, 1.0, 0.0)
        near_ref[at : at + BORDER, :] = total.astype(bf16)
    small[3].wait()
    for side in range(2):
        rim_load(side).wait()
    def halo_start(p):
        for side in range(2):
            @pl.when(has(side))
            def _():
                halo_copy(p, side, 0).start()
                halo_copy(p, side, 1).start()

    every = max(genes // loads // step, 1)

    def arrive(c):
        if c % every == 0:
            inner_load(c // every).wait()
        if c // every == loads - 1 and c % every == 0:
            gsum_part = jnp.sum(h_ref[...].astype(f32), axis=1, keepdims=True)
            nsend[0, :, width : width + LANES] = jnp.broadcast_to(gsum_part, (rank, LANES))

    for p in range(PASSES):
        numer_rim = numer_of(lhs[rims], rims, None)
        put_halo(p, numer_rim)
        if p == 0:
            pl.semaphore_wait(
                barrier, n + has(0).astype(jnp.int32) + has(1).astype(jnp.int32)
            )
        halo_start(p)
        numer_inner = numer_of(lhs[inner], inner, arrive if p == 0 else None)
        nsend[p, :, rims] = numer_rim
        nsend[p, :, inner] = numer_inner
        pair_copy(p).start()
        pair_copy(p).wait_recv()
        if p == 0:
            inverse = 1.0 / (
                nsend[0, :, width : width + LANES] + nrecv[0, :, width : width + LANES]
            )
            inverse_wide = jnp.concatenate([inverse] * (width // LANES), axis=1)
        numer = nsend[p, :, 0:width] + nrecv[p, :, 0:width]
        updated = jnp.where(inside, cells * numer * inverse_wide, cells)
        stacked = jnp.concatenate(split(updated * mask) + (mrow.astype(bf16),), axis=0)
        mixed = jnp.dot(stacked, near_ref[0:width, :], preferred_element_type=f32)
        near = mixed[0:rank] + mixed[rank : 2 * rank]
        if p == 0:
            count = mixed[2 * rank : 2 * rank + 1]
        cells = jnp.where(
            inside,
            (1.0 - smooth_weight) * updated + smooth_weight * near / jnp.maximum(count, 1.0),
            updated,
        )
        if p + 1 == PASSES:
            lhs = jnp.transpose(cells).astype(bf16)[inner]
            lift = jnp.concatenate(split(cells * mask), axis=0)[:, inner]
            for at in range(0, genes, wide):
                both = jnp.dot(
                    lift, ratio_of(lhs, inner, at, wide), preferred_element_type=f32
                )
                acc_ref[:, pl.ds(at, wide)] = both[0:rank] + both[rank : 2 * rank]
        for side in range(2):
            @pl.when(has(side))
            def _():
                halo_both(p, side).wait_recv()
        for side in range(2):
            packed = hrecv[p, side, 0, 0:SUB] + hrecv[p, side, 1, 0:SUB]
            for g in range(rank // SUB):
                halo_ref[g * SUB : (g + 1) * SUB, side * BORDER : (side + 1) * BORDER] = packed[
                    :, g * BORDER : (g + 1) * BORDER
                ]
        halo = halo_ref[...] * inverse
        if p == 0:
            flags = jnp.where(
                lane_of((SUB, LANES)) < BORDER,
                hrecv[0, 0, 0, SUB : 2 * SUB, 0:LANES], hrecv[0, 1, 0, SUB : 2 * SUB, 0:LANES],
            )
            flags = jnp.concatenate([flags, flags], axis=0).astype(bf16)
        stacked = jnp.concatenate(split(halo) + (flags,), axis=0)
        mixed = jnp.dot(
            stacked, near_ref[width : width + LANES, 0:LANES], preferred_element_type=f32
        )
        near_rim = near[:, 0:LANES] + (mixed[0:rank] + mixed[rank : 2 * rank])
        if p == 0:
            count_rim = jnp.maximum(count[:, 0:LANES] + mixed[2 * rank : 2 * rank + 1], 1.0)
        rim = updated[:, 0:LANES]
        rim = jnp.where(
            inside[:, 0:LANES],
            (1.0 - smooth_weight) * rim + smooth_weight * near_rim / count_rim,
            rim,
        )
        cells = jnp.concatenate([rim, cells[:, LANES:]], axis=1)
        lhs = jnp.transpose(cells).astype(bf16)

    weighted = cells * mask
    den_part = jnp.sum(weighted, axis=1, keepdims=True)
    lift = jnp.concatenate(split(weighted[:, 0:LANES]), axis=0)[:, rims]

    blk = cols // quarters

    relayed = range(quarters - relays, quarters)
    early = range(relays)
    even = lax.rem(me, 2) == 0
    mate = me + 1 - 2 * lax.rem(me, 2)
    far = lax.rem(me + n // 2, n)
    far_mate = far + 1 - 2 * lax.rem(far, 2)

    def when_owner(index, call):
        if owners == n:
            call()
        else:
            pl.when(index < owners)(call)

    def move(src, dst, ssem, rsem, tile):
        return pltpu.make_async_remote_copy(
            src_ref=src, dst_ref=dst, send_sem=ssem, recv_sem=rsem,
            device_id={"tile": tile}, device_id_type=MESH,
        )

    def part_start(q, j):
        o = lax.rem(me + j, n)

        def call():
            slot = n - 1 - j
            move(psend.at[q * owners + o], precv.at[q, slot], p_s, p_r.at[q], o).start()

        if q in relayed:
            if j in (n // 2 - 1, n // 2 + 1):
                pl.when(o != far_mate)(call)
            elif j != n // 2:
                call()
        else:
            when_owner(o, call)

    def unit_start(j):
        o = lax.rem(me + j, n)
        when_owner(
            o,
            lambda: move(
                usend.at[pl.ds(0, 1)], urecv.at[pl.ds(n - 1 - j, 1)], u_s, u_r, o
            ).start(),
        )

    def all_peers(call):
        if few:
            for j in sorted(range(1, n), key=lambda j: (abs(j - n // 2), j)):
                call(j)
        else:
            def body(j, carry):
                call(j)
                return carry

            lax.fori_loop(1, n, body, 0)

    top = jnp.full((rank, 1), 1e-30, f32)
    for at in range(0, genes, wide):
        both = jnp.dot(lift, ratio_of(lhs[rims], rims, at, wide), preferred_element_type=f32)
        total = acc_ref[:, pl.ds(at, wide)] + (both[0:rank] + both[rank : 2 * rank])
        acc_ref[:, pl.ds(at, wide)] = total
        top = jnp.maximum(top, jnp.max(total, axis=1, keepdims=True))
    usend[...] = jnp.broadcast_to(row_of((top * (1.0 / TOP), den_part)), usend.shape)
    all_peers(unit_start)
    scale = TOP / top
    for q in range(quarters):
        for o in range(owners):
            value = acc_ref[:, pl.ds(o * cols + q * blk, blk)] * scale + (0.5 - HALF)
            psend[q * owners + o] = jnp.floor(value).astype(jnp.int32).astype(WIRE)
    for i, q in enumerate(relayed):
        move(psend.at[q * owners + far_mate], stage.at[i], p_s, stage_r.at[i], mate).start()
    for q in range(quarters):
        all_peers(lambda j: part_start(q, j))
    cells_ref[...] = pltpu.roll(cells, width - BORDER, 1)

    def gene_piece(q):
        return genes_ref.at[:, pl.ds(pl.multiple_of(me * cols + q * blk, LANES), blk)]

    def gene_start(q, j):
        o = lax.rem(me + j, n)
        come = f_r.at[q] if q in early and j == n // 2 else g_r
        call = move(gene_piece(q), gene_piece(q), g_s, come, o).start
        if q in early and j in (n // 2 - 1, n // 2 + 1):
            pl.when(o != far_mate)(call)
        else:
            call()

    def finish_part():
        ahead = lax.rem(me + 1, n)
        rows = urecv.at[pl.ds(0, n - 1)]
        move(rows, rows, u_s, u_r, ahead).wait_recv()
        units = jnp.transpose(urecv[...])
        den = den_part + jnp.sum(units[rank : 2 * rank, 0 : n - 1], axis=1, keepdims=True)
        inverse_den = 1.0 / den
        unit_of = [units[0:rank, slot : slot + 1] for slot in range(n - 1)]
        if relays:
            unit_mate = jnp.where(even, unit_of[0], unit_of[n - 2])
            joint = 1.0 / (top * (1.0 / TOP) + unit_mate)
            middle = n // 2 - 1
            joint_of = list(unit_of)
            joint_of[middle] += jnp.where(even, unit_of[middle + 1], unit_of[middle - 1])
            joint_of[middle + 1] = jnp.where(even, 0.0, unit_of[middle + 1])
            joint_of[middle - 1] = jnp.where(even, unit_of[middle - 1], 0.0)
        for i, q in enumerate(relayed):
            move(stage.at[i], stage.at[i], p_s, stage_r.at[i], ahead).wait_recv()
            there = pl.ds(pl.multiple_of(far * cols + q * blk, LANES), blk)
            value = (stage[i].astype(jnp.int32).astype(f32) + HALF) * unit_mate
            value = (acc_ref[:, there] + value) * joint + (0.5 - HALF)
            psend[q * owners + far] = jnp.floor(value).astype(jnp.int32).astype(WIRE)
            move(
                psend.at[q * owners + far], precv.at[q, middle], p_s, p_r.at[q], far
            ).start()
        for q in range(quarters):
            here = pl.ds(pl.multiple_of(me * cols + q * blk, LANES), blk)
            total = acc_ref[:, here]
            come = precv.at[q, pl.ds(0, n - 2 if q in relayed else n - 1)]
            move(come, come, p_s, p_r.at[q], ahead).wait_recv()
            for slot in range(n - 1):
                value = precv[q, slot].astype(jnp.int32).astype(f32) + HALF
                total = total + value * (joint_of if q in relayed else unit_of)[slot]
            lead = h_ref[:, here].astype(f32) * inverse_den
            genes_ref[:, here] = (lead * total).astype(genes_ref.dtype)
            all_peers(lambda j: gene_start(q, j))
        for q in early:
            there = genes_ref.at[:, pl.ds(pl.multiple_of(far * cols + q * blk, LANES), blk)]
            move(there, there, g_s, f_r.at[q], ahead).wait_recv()
            move(there, there, g_s, g_r, mate).start()

    def wait_all(owned):
        others = owners - 1 if owned else owners
        ahead = lax.rem(me + 1, n)
        ref = genes_ref.at[:, pl.ds(0, others * cols - len(early) * blk)]
        move(ref, ref, g_s, g_r, ahead).wait_recv()
        sent = pl.ds(0, quarters * others)
        move(psend.at[sent], psend.at[sent], p_s, g_r, ahead).wait_send()
        rows = urecv.at[pl.ds(0, others)]
        move(rows, rows, u_s, g_r, ahead).wait_send()
        if owned:
            move(precv, precv, g_s, g_r, ahead).wait_send()

    when_owner(me, finish_part)
    when_owner(me, lambda: wait_all(True))
    if owners < n:
        pl.when(me >= owners)(lambda: wait_all(False))
    for p in range(PASSES):
        pair_copy(p).wait_send()
        for side in range(2):
            @pl.when(has(side))
            def _():
                halo_both(p, side).wait_send()


def settle(cells_in, genes_in, cells_ref, genes_ref):
    cells_ref[...] = cells_in[...]
    genes_ref[...] = genes_in[...]


def on_device(n, counts, cell_factor, gene_factor, tissue, neighbours):
    width, genes = counts.shape
    rank = cell_factor.shape[0]
    near = neighbours.shape[0]
    owners = min(n, genes // LANES)
    step = min(512, genes)
    loads = min(2, genes // step)
    cols = genes // owners
    quarters = max(1, min(4, cols // LANES))
    relays = quarters // 2 if n == owners and n % 4 == 0 and n <= 16 else 0
    dma = pltpu.SemaphoreType.DMA
    vmem = pl.BlockSpec(memory_space=pltpu.VMEM)
    shapes = (
        jax.ShapeDtypeStruct((rank, width), f32),
        jax.ShapeDtypeStruct((rank, genes), bf16),
    )
    results = pl.pallas_call(
        functools.partial(kernel, n, owners, quarters, relays, step, loads),
        out_shape=tuple(pltpu.VMEM(s.shape, s.dtype) for s in shapes),
        in_specs=[pl.BlockSpec(memory_space=pl.ANY)] * 5,
        out_specs=(vmem, vmem),
        scratch_shapes=[
            pltpu.VMEM((width, genes), jnp.int32),
            pltpu.VMEM((rank, width), f32),
            pltpu.VMEM((rank, genes), bf16),
            pltpu.VMEM((1, width), jnp.int32),
            pltpu.VMEM((near, width), jnp.int32),
            pltpu.VMEM((width + LANES, width), bf16),
            pltpu.VMEM((rank, genes), f32),
            pltpu.VMEM((rank, LANES), f32),
            pltpu.VMEM((PASSES, rank, width + LANES), f32),
            pltpu.VMEM((PASSES, rank, width + LANES), f32),
            pltpu.VMEM((PASSES, 2, 2 * SUB, max(rank // SUB * BORDER, LANES)), f32),
            pltpu.VMEM((PASSES, 2, 2, 2 * SUB, max(rank // SUB * BORDER, LANES)), f32),
            pltpu.VMEM((quarters * owners, rank, cols // quarters), WIRE),
            pltpu.VMEM((quarters, n - 1, rank, cols // quarters), WIRE),
            pltpu.VMEM((max(relays, 1), rank, cols // quarters), WIRE),
            pltpu.VMEM((SUB, LANES), f32),
            pltpu.VMEM((pl.cdiv(n, LANES) * LANES, LANES), f32),
            dma((4,)),
            dma((2,)),
            dma((loads,)),
            dma((PASSES,)),
            dma((PASSES,)),
            dma((PASSES, 2)),
            dma((PASSES, 2)),
            dma,
            dma((quarters,)),
            dma((max(relays, 1),)),
            dma,
            dma,
            dma,
            dma,
            dma((max(relays, 1),)),
        ],
        compiler_params=pltpu.CompilerParams(
            collective_id=0, has_side_effects=True, vmem_limit_bytes=63_160_000
        ),
    )(counts, cell_factor, gene_factor, tissue.reshape(1, width), neighbours)
    return pl.pallas_call(
        settle, out_shape=shapes, in_specs=[vmem] * 2, out_specs=(vmem, vmem),
        compiler_params=pltpu.CompilerParams(vmem_limit_bytes=16 * 1024 * 1024),
    )(*results)


def solution(mesh):
    return jax.shard_map(
        functools.partial(on_device, mesh.shape["tile"]),
        mesh=mesh,
        in_specs=(
            P(("grp", "tile"), "gene"),
            P(None, ("grp", "tile")),
            P(None, ("grp", "gene")),
            P(("grp", "tile")),
            P(None, ("grp", "tile")),
        ),
        out_specs=(P(None, ("grp", "tile")), P(None, ("grp", "gene"))),
        check_vma=False,
    )
```

```python
import functools

import jax
import jax.numpy as jnp
from jax import lax
from jax.experimental import pallas as pl
from jax.experimental.pallas import tpu as pltpu
from jax.sharding import PartitionSpec as P

BORDER = 32
RIM = 2 * BORDER
PASSES = 2
LANES = 128
SUB = 8
MESH = pl.DeviceIdType.MESH
WIRE = jnp.int16
TOP = 65000.0
HALF = 32768.0

smooth_weight = 0.5

f32 = jnp.float32
bf16 = jnp.bfloat16


def split(value):
    high = value.astype(bf16)
    low = (value - high.astype(f32)).astype(bf16)
    return high, low


def quotient(top, bottom):
    r = pl.reciprocal(bottom, approx=True)
    return top * (r * (2.0 - bottom * r))


def lane_of(shape):
    return lax.broadcasted_iota(jnp.int32, shape, 1)


def row_of(columns):
    rank = columns[0].shape[0]
    index = lax.broadcasted_iota(jnp.int32, (rank, LANES), 0)
    lane = lane_of((rank, LANES))
    spread = jnp.zeros((rank, LANES), f32)
    for g, column in enumerate(columns):
        spread = jnp.where(lane == index + g * rank, column, spread)
    return jnp.sum(spread, axis=0, keepdims=True)


def column_of(row, rank):
    index = lax.broadcasted_iota(jnp.int32, (rank, LANES), 0)
    return jnp.sum(jnp.where(lane_of((rank, LANES)) == index, row, 0.0), axis=1, keepdims=True)


def kernel(
    n, owners, quarters, relays, step, loads,
    x_hbm, w_hbm, h_hbm, t_hbm, nb_hbm,
    cells_ref, genes_ref,
    x_ref, w_ref, h_ref, t_ref, nb_ref, near_ref, acc_ref, halo_ref,
    nsend, nrecv, hsend, hrecv, psend, precv, stage, usend, urecv, lead_ref, done_ref,
    in_sem, e_sem, x_sem, pair_s, pair_r, halo_s, halo_r,
    p_s, p_r, stage_r, u_s, u_r, g_s, g_r, f_r, l_s, l_r,
):
    rank, width = w_ref.shape
    genes = h_ref.shape[1]
    cols = genes // owners
    me = lax.axis_index("tile")
    core = lax.axis_index("gene")
    other = 1 - core
    barrier = pltpu.get_barrier_semaphore()

    small = [
        pltpu.make_async_copy(src, dst, in_sem.at[i])
        for i, (src, dst) in enumerate(
            ((w_hbm, w_ref), (t_hbm, t_ref), (nb_hbm, nb_ref), (h_hbm, h_ref))
        )
    ]

    def rim_load(side):
        source = pl.ds((width - BORDER, 0)[side], BORDER)
        return pltpu.make_async_copy(
            x_hbm.at[source], x_ref.at[pl.ds(side * BORDER, BORDER)], e_sem.at[side]
        )

    def inner_load(c):
        size = genes // loads
        part = pl.ds(c * size, size)
        return pltpu.make_async_copy(
            x_hbm.at[pl.ds(BORDER, width - RIM), part],
            x_ref.at[pl.ds(RIM, width - RIM), part],
            x_sem.at[c],
        )

    for copy in small:
        copy.start()
    for side in range(2):
        rim_load(side).start()

    def has(side):
        return me > 0 if side == 0 else me < n - 1

    def greet(i, carry):
        pl.semaphore_signal(
            barrier, inc=1, device_id={"tile": lax.rem(me + i, n), "gene": other},
            device_id_type=MESH,
        )
        return carry

    few = n <= 16
    lax.fori_loop(1, n, greet, 0, unroll=few)
    pl.semaphore_signal(barrier, inc=1, device_id={"gene": other}, device_id_type=MESH)
    for side in range(2):
        @pl.when(has(side))
        def _():
            pl.semaphore_signal(
                barrier, inc=1, device_id={"tile": me - 1 + 2 * side}, device_id_type=MESH
            )

    for side in range(2):
        @pl.when(jnp.logical_not(has(side)))
        def _():
            hrecv[:, side] = jnp.zeros(hrecv.shape[:1] + hrecv.shape[2:], f32)
    halo_ref[...] = jnp.zeros_like(halo_ref)

    def halo_rows(p):
        return pl.ds(0, 2 * SUB if p == 0 else SUB)

    def halo_copy(p, side, k):
        return pltpu.make_async_remote_copy(
            src_ref=hsend.at[p, side, halo_rows(p)], dst_ref=hrecv.at[p, 1 - side, core, halo_rows(p)],
            send_sem=halo_s.at[p, side], recv_sem=halo_r.at[p, 1 - side],
            device_id={"tile": me - 1 + 2 * side, "gene": core if k == 0 else other},
            device_id_type=MESH,
        )

    def halo_both(p, side):
        ref = hrecv.at[p, side, :, halo_rows(p)]
        return pltpu.make_async_remote_copy(
            src_ref=ref, dst_ref=ref, send_sem=halo_s.at[p, side], recv_sem=halo_r.at[p, side],
            device_id={"tile": lax.rem(me + 1, n)}, device_id_type=MESH,
        )

    def pair_copy(p):
        part = pl.ds(0, width + LANES if p == 0 else width)
        return pltpu.make_async_remote_copy(
            src_ref=nsend.at[p, :, part], dst_ref=nrecv.at[p, :, part],
            send_sem=pair_s.at[p], recv_sem=pair_r.at[p],
            device_id={"gene": other}, device_id_type=MESH,
        )

    blk = cols // quarters

    relayed = range(quarters - relays, quarters)
    early = range(relays)
    even = lax.rem(me, 2) == 0
    mate = me + 1 - 2 * lax.rem(me, 2)
    far = lax.rem(me + n // 2, n)
    far_mate = far + 1 - 2 * lax.rem(far, 2)

    def when_owner(index, call):
        if owners == n:
            call()
        else:
            pl.when(index < owners)(call)

    def move(src, dst, ssem, rsem, tile, gene=None):
        return pltpu.make_async_remote_copy(
            src_ref=src, dst_ref=dst, send_sem=ssem, recv_sem=rsem,
            device_id={"tile": tile, "gene": other if gene is None else gene},
            device_id_type=MESH,
        )

    def lead_copy():
        mine = pl.ds(pl.multiple_of(me * cols, LANES), cols)
        return move(h_ref.at[:, mine], lead_ref, l_s, l_r, me)

    rims, inner = slice(0, RIM), slice(RIM, width)

    def ratio_of(lhs, rows, at, size):
        product = jnp.dot(lhs, h_ref[:, pl.ds(at, size)], preferred_element_type=f32)
        return quotient(x_ref[rows, pl.ds(at, size)].astype(f32), product).astype(bf16)

    def numer_of(lhs, rows, begin):
        acc = None
        for c in range(genes // step):
            if begin is not None:
                begin(c)
            part = lax.dot_general(
                h_ref[:, pl.ds(c * step, step)], ratio_of(lhs, rows, c * step, step),
                (((1,), (1,)), ((), ())), preferred_element_type=f32,
            )
            acc = part if acc is None else acc + part
        return acc

    def put_halo(p, numer):
        value = (cells * mask)[:, rims] * numer
        for side, first in enumerate((BORDER, 0)):
            for g in range(rank // SUB):
                hsend[p, side, 0:SUB, g * BORDER : (g + 1) * BORDER] = value[
                    g * SUB : (g + 1) * SUB, first : first + BORDER
                ]

    wide = min(4 * step, genes)
    small[0].wait()
    small[1].wait()
    for c in range(loads):
        inner_load(c).start()
    cells = pltpu.roll(w_ref[...], BORDER, 1)
    mrow = pltpu.roll(jnp.broadcast_to(t_ref[...].astype(f32), (2 * SUB, width)), BORDER, 1)
    mask = jnp.broadcast_to(mrow[0:1], (rank, width))
    inside = mask > 0.0
    for side in range(2):
        hsend[0, side, SUB : 2 * SUB, 0:LANES] = jnp.where(
            lane_of((SUB, LANES)) < RIM, mrow[0:SUB, 0:LANES], 0.0
        )
    lhs = jnp.transpose(cells).astype(bf16)
    small[2].wait()
    a = pltpu.roll(nb_ref[...], BORDER, 1) - (me * width - BORDER)
    spot = jnp.where(a < BORDER, a + width, a)
    spot = jnp.where(jnp.logical_and(a >= width, a < width + BORDER), a - width, spot)
    for at in range(0, width + LANES, BORDER):
        index = lax.broadcasted_iota(jnp.int32, (BORDER, width), 0) + at
        total = jnp.zeros((BORDER, width), f32)
        for j in range(nb_ref.shape[0]):
            total = total + jnp.where(spot[j : j + 1] == index, 1.0, 0.0)
        near_ref[at : at + BORDER, :] = total.astype(bf16)
    small[3].wait()
    for side in range(2):
        rim_load(side).wait()
    def halo_start(p):
        for side in range(2):
            @pl.when(has(side))
            def _():
                halo_copy(p, side, 0).start()
                halo_copy(p, side, 1).start()

    every = max(genes // loads // step, 1)

    def arrive(c):
        if c % every == 0:
            inner_load(c // every).wait()
        if c // every == loads - 1 and c % every == 0:
            gsum_part = jnp.sum(h_ref[...].astype(f32), axis=1, keepdims=True)
            nsend[0, :, width : width + LANES] = jnp.broadcast_to(gsum_part, (rank, LANES))

    for p in range(PASSES):
        numer_rim = numer_of(lhs[rims], rims, None)
        put_halo(p, numer_rim)
        if p == 0:
            pl.semaphore_wait(
                barrier, n + has(0).astype(jnp.int32) + has(1).astype(jnp.int32)
            )
        halo_start(p)
        if p == 0:
            when_owner(me, lambda: lead_copy().start())
        numer_inner = numer_of(lhs[inner], inner, arrive if p == 0 else None)
        nsend[p, :, rims] = numer_rim
        nsend[p, :, inner] = numer_inner
        pair_copy(p).start()
        pair_copy(p).wait_recv()
        if p == 0:
            inverse = 1.0 / (
                nsend[0, :, width : width + LANES] + nrecv[0, :, width : width + LANES]
            )
            inverse_wide = jnp.concatenate([inverse] * (width // LANES), axis=1)
        numer = nsend[p, :, 0:width] + nrecv[p, :, 0:width]
        updated = jnp.where(inside, cells * numer * inverse_wide, cells)
        stacked = jnp.concatenate(split(updated * mask) + (mrow.astype(bf16),), axis=0)
        mixed = jnp.dot(stacked, near_ref[0:width, :], preferred_element_type=f32)
        near = mixed[0:rank] + mixed[rank : 2 * rank]
        if p == 0:
            count = mixed[2 * rank : 2 * rank + 1]
        cells = jnp.where(
            inside,
            (1.0 - smooth_weight) * updated + smooth_weight * near / jnp.maximum(count, 1.0),
            updated,
        )
        if p + 1 == PASSES:
            lhs = jnp.transpose(cells).astype(bf16)[inner]
            lift = jnp.concatenate(split(cells * mask), axis=0)[:, inner]
            for at in range(0, genes, wide):
                both = jnp.dot(
                    lift, ratio_of(lhs, inner, at, wide), preferred_element_type=f32
                )
                acc_ref[:, pl.ds(at, wide)] = both[0:rank] + both[rank : 2 * rank]
        for side in range(2):
            @pl.when(has(side))
            def _():
                halo_both(p, side).wait_recv()
        for side in range(2):
            packed = hrecv[p, side, 0, 0:SUB] + hrecv[p, side, 1, 0:SUB]
            for g in range(rank // SUB):
                halo_ref[g * SUB : (g + 1) * SUB, side * BORDER : (side + 1) * BORDER] = packed[
                    :, g * BORDER : (g + 1) * BORDER
                ]
        halo = halo_ref[...] * inverse
        if p == 0:
            flags = jnp.where(
                lane_of((SUB, LANES)) < BORDER,
                hrecv[0, 0, 0, SUB : 2 * SUB, 0:LANES], hrecv[0, 1, 0, SUB : 2 * SUB, 0:LANES],
            )
            flags = jnp.concatenate([flags, flags], axis=0).astype(bf16)
        stacked = jnp.concatenate(split(halo) + (flags,), axis=0)
        mixed = jnp.dot(
            stacked, near_ref[width : width + LANES, 0:LANES], preferred_element_type=f32
        )
        near_rim = near[:, 0:LANES] + (mixed[0:rank] + mixed[rank : 2 * rank])
        if p == 0:
            count_rim = jnp.maximum(count[:, 0:LANES] + mixed[2 * rank : 2 * rank + 1], 1.0)
        rim = updated[:, 0:LANES]
        rim = jnp.where(
            inside[:, 0:LANES],
            (1.0 - smooth_weight) * rim + smooth_weight * near_rim / count_rim,
            rim,
        )
        cells = jnp.concatenate([rim, cells[:, LANES:]], axis=1)
        lhs = jnp.transpose(cells).astype(bf16)

    weighted = cells * mask
    den_part = jnp.sum(weighted, axis=1, keepdims=True)
    lift = jnp.concatenate(split(weighted[:, 0:LANES]), axis=0)[:, rims]

    def part_start(q, j):
        o = lax.rem(me + j, n)

        def call():
            slot = lax.rem(n - j, n)
            move(psend.at[q * owners + o], precv.at[q, slot], p_s, p_r.at[q], o).start()

        if q in relayed:
            if j in (n // 2 - 1, n // 2 + 1):
                pl.when(o != far_mate)(call)
            elif j != n // 2:
                call()
        else:
            when_owner(o, call)

    def unit_start(j):
        o = lax.rem(me + j, n)
        when_owner(
            o,
            lambda: move(
                usend.at[pl.ds(0, 1)], urecv.at[pl.ds(lax.rem(n - j, n), 1)], u_s, u_r.at[0], o
            ).start(),
        )

    def all_peers(call):
        if few:
            for j in sorted(range(n), key=lambda j: (abs(j - n // 2), j)):
                call(j)
        else:
            def body(j, carry):
                call(j)
                return carry

            lax.fori_loop(0, n, body, 0)

    top = jnp.full((rank, 1), 1e-30, f32)
    for at in range(0, genes, wide):
        both = jnp.dot(lift, ratio_of(lhs[rims], rims, at, wide), preferred_element_type=f32)
        total = acc_ref[:, pl.ds(at, wide)] + (both[0:rank] + both[rank : 2 * rank])
        acc_ref[:, pl.ds(at, wide)] = total
        top = jnp.maximum(top, jnp.max(total, axis=1, keepdims=True))
    usend[...] = jnp.broadcast_to(row_of((top * (1.0 / TOP), den_part)), usend.shape)
    if relays:
        move(
            usend.at[pl.ds(0, 1)], urecv.at[pl.ds(n, 1)], u_s, u_r.at[1], mate, core
        ).start()
    all_peers(unit_start)
    scale = TOP / top
    for q in range(quarters):
        for o in range(owners):
            value = acc_ref[:, pl.ds(o * cols + q * blk, blk)] * scale + (0.5 - HALF)
            psend[q * owners + o] = jnp.floor(value).astype(jnp.int32).astype(WIRE)
    for i, q in enumerate(relayed):
        move(psend.at[q * owners + far_mate], stage.at[i], p_s, stage_r.at[i], mate, core).start()
    for q in range(quarters):
        all_peers(lambda j: part_start(q, j))
    cells_ref[...] = pltpu.roll(cells, width - BORDER, 1)

    def gene_start(q, j):
        o = lax.rem(me + j, n)
        come = f_r.at[q] if q in early and j == n // 2 else g_r
        here = pl.ds(pl.multiple_of(me * cols + q * blk, LANES), blk)
        call = move(done_ref.at[q], genes_ref.at[:, here], g_s, come, o).start
        if q in early and j in (n // 2 - 1, n // 2 + 1):
            pl.when(o != far_mate)(call)
        else:
            call()

    ahead = lax.rem(me + 1, n)
    if relays:
        row = urecv.at[pl.ds(n, 1)]
        move(row, row, u_s, u_r.at[1], ahead).wait_recv()
        unit_mate = column_of(urecv[n : n + 1], rank)
        joint = 1.0 / (top * (1.0 / TOP) + unit_mate)
    for i, q in enumerate(relayed):
        move(stage.at[i], stage.at[i], p_s, stage_r.at[i], ahead).wait_recv()
        there = pl.ds(pl.multiple_of(far * cols + q * blk, LANES), blk)
        value = (stage[i].astype(jnp.int32).astype(f32) + HALF) * unit_mate
        value = (acc_ref[:, there] + value) * joint + (0.5 - HALF)
        psend[q * owners + far] = jnp.floor(value).astype(jnp.int32).astype(WIRE)
        move(psend.at[q * owners + far], precv.at[q, n // 2], p_s, p_r.at[q], far).start()

    def finish_part():
        rows = urecv.at[pl.ds(0, n)]
        move(rows, rows, u_s, u_r.at[0], ahead).wait_recv()
        lead_copy().wait_recv()
        units = jnp.transpose(urecv[...])
        inverse_den = 1.0 / jnp.sum(units[rank : 2 * rank, 0:n], axis=1, keepdims=True)
        unit_of = [units[0:rank, slot : slot + 1] for slot in range(n)]
        if relays:
            middle = n // 2
            joint_of = list(unit_of)
            joint_of[middle] += jnp.where(even, unit_of[middle + 1], unit_of[middle - 1])
            joint_of[middle + 1] = jnp.where(even, 0.0, unit_of[middle + 1])
            joint_of[middle - 1] = jnp.where(even, unit_of[middle - 1], 0.0)
        for q in range(quarters):
            come = precv.at[q, pl.ds(0, n - 1 if q in relayed else n)]
            move(come, come, p_s, p_r.at[q], ahead).wait_recv()
            total = jnp.zeros((rank, blk), f32)
            for slot in range(n):
                value = precv[q, slot].astype(jnp.int32).astype(f32) + HALF
                total = total + value * (joint_of if q in relayed else unit_of)[slot]
            lead = lead_ref[:, q * blk : (q + 1) * blk].astype(f32) * inverse_den
            done_ref[q] = (lead * total).astype(done_ref.dtype)
            all_peers(lambda j: gene_start(q, j))

    when_owner(me, finish_part)
    for q in early:
        there = genes_ref.at[:, pl.ds(pl.multiple_of(far * cols + q * blk, LANES), blk)]
        move(there, there, g_s, f_r.at[q], ahead).wait_recv()
        move(there, there, g_s, g_r, mate, core).start()
    ref = genes_ref.at[:, pl.ds(0, genes - len(early) * blk)]
    move(ref, ref, g_s, g_r, ahead).wait_recv()
    move(psend, psend, p_s, g_r, ahead).wait_send()
    rows = urecv.at[pl.ds(0, owners + 1 if relays else owners)]
    move(rows, rows, u_s, g_r, ahead).wait_send()

    def sent_blocks():
        move(precv, precv, g_s, g_r, ahead).wait_send()
        lead_copy().wait_send()

    when_owner(me, sent_blocks)
    for p in range(PASSES):
        pair_copy(p).wait_send()
        for side in range(2):
            @pl.when(has(side))
            def _():
                halo_both(p, side).wait_send()


def settle(cells_in, genes_in, cells_ref, genes_ref):
    cells_ref[...] = cells_in[...]
    genes_ref[...] = genes_in[...]


def on_device(n, counts, cell_factor, gene_factor, tissue, neighbours):
    width, genes = counts.shape
    rank = cell_factor.shape[0]
    near = neighbours.shape[0]
    owners = min(n, genes // LANES)
    step = min(512, genes)
    loads = min(2, genes // step)
    cols = genes // owners
    quarters = max(1, min(4, cols // LANES))
    relays = quarters // 2 if n == owners and n % 4 == 0 and n <= 16 else 0
    dma = pltpu.SemaphoreType.DMA
    vmem = pl.BlockSpec(memory_space=pltpu.VMEM)
    shapes = (
        jax.ShapeDtypeStruct((rank, width), f32),
        jax.ShapeDtypeStruct((rank, genes), bf16),
    )
    results = pl.pallas_call(
        functools.partial(kernel, n, owners, quarters, relays, step, loads),
        out_shape=tuple(pltpu.VMEM(s.shape, s.dtype) for s in shapes),
        in_specs=[pl.BlockSpec(memory_space=pl.ANY)] * 5,
        out_specs=(vmem, vmem),
        scratch_shapes=[
            pltpu.VMEM((width, genes), jnp.int32),
            pltpu.VMEM((rank, width), f32),
            pltpu.VMEM((rank, genes), bf16),
            pltpu.VMEM((1, width), jnp.int32),
            pltpu.VMEM((near, width), jnp.int32),
            pltpu.VMEM((width + LANES, width), bf16),
            pltpu.VMEM((rank, genes), f32),
            pltpu.VMEM((rank, LANES), f32),
            pltpu.VMEM((PASSES, rank, width + LANES), f32),
            pltpu.VMEM((PASSES, rank, width + LANES), f32),
            pltpu.VMEM((PASSES, 2, 2 * SUB, max(rank // SUB * BORDER, LANES)), f32),
            pltpu.VMEM((PASSES, 2, 2, 2 * SUB, max(rank // SUB * BORDER, LANES)), f32),
            pltpu.VMEM((quarters * owners, rank, cols // quarters), WIRE),
            pltpu.VMEM((quarters, n, rank, cols // quarters), WIRE),
            pltpu.VMEM((max(relays, 1), rank, cols // quarters), WIRE),
            pltpu.VMEM((SUB, LANES), f32),
            pltpu.VMEM((pl.cdiv(n + 1, LANES) * LANES, LANES), f32),
            pltpu.VMEM((rank, cols), bf16),
            pltpu.VMEM((quarters, rank, cols // quarters), bf16),
            dma((4,)),
            dma((2,)),
            dma((loads,)),
            dma((PASSES,)),
            dma((PASSES,)),
            dma((PASSES, 2)),
            dma((PASSES, 2)),
            dma,
            dma((quarters,)),
            dma((max(relays, 1),)),
            dma,
            dma((2,)),
            dma,
            dma,
            dma((max(relays, 1),)),
            dma,
            dma,
        ],
        compiler_params=pltpu.CompilerParams(
            collective_id=0, has_side_effects=True, vmem_limit_bytes=63_160_000
        ),
    )(counts, cell_factor, gene_factor, tissue.reshape(1, width), neighbours)
    return pl.pallas_call(
        settle, out_shape=shapes, in_specs=[vmem] * 2, out_specs=(vmem, vmem),
        compiler_params=pltpu.CompilerParams(vmem_limit_bytes=16 * 1024 * 1024),
    )(*results)


def solution(mesh):
    return jax.shard_map(
        functools.partial(on_device, mesh.shape["tile"]),
        mesh=mesh,
        in_specs=(
            P(("grp", "tile"), "gene"),
            P(None, ("grp", "tile")),
            P(None, ("grp", "gene")),
            P(("grp", "tile")),
            P(None, ("grp", "tile")),
        ),
        out_specs=(P(None, ("grp", "tile")), P(None, ("grp", "gene"))),
        check_vma=False,
    )
```

```python
import functools

import jax
import jax.numpy as jnp
from jax import lax
from jax.experimental import pallas as pl
from jax.experimental.pallas import tpu as pltpu
from jax.sharding import PartitionSpec as P

BORDER = 32
RIM = 2 * BORDER
PASSES = 2
LANES = 128
SUB = 8
MESH = pl.DeviceIdType.MESH
WIRE = jnp.int16
TOP = 65000.0
HALF = 32768.0

smooth_weight = 0.5

f32 = jnp.float32
bf16 = jnp.bfloat16


def split(value):
    high = value.astype(bf16)
    low = (value - high.astype(f32)).astype(bf16)
    return high, low


def quotient(top, bottom):
    r = pl.reciprocal(bottom, approx=True)
    return top * (r * (2.0 - bottom * r))


def lane_of(shape):
    return lax.broadcasted_iota(jnp.int32, shape, 1)


def row_of(columns):
    rank = columns[0].shape[0]
    index = lax.broadcasted_iota(jnp.int32, (rank, LANES), 0)
    lane = lane_of((rank, LANES))
    spread = jnp.zeros((rank, LANES), f32)
    for g, column in enumerate(columns):
        spread = jnp.where(lane == index + g * rank, column, spread)
    return jnp.sum(spread, axis=0, keepdims=True)


def column_of(row, rank):
    index = lax.broadcasted_iota(jnp.int32, (rank, LANES), 0)
    return jnp.sum(jnp.where(lane_of((rank, LANES)) == index, row, 0.0), axis=1, keepdims=True)


def kernel(
    n, owners, quarters, relays, step, loads,
    x_hbm, w_hbm, h_hbm, t_hbm, nb_hbm,
    cells_ref, genes_ref,
    x_ref, w_ref, h_ref, t_ref, nb_ref, near_ref, acc_ref, halo_ref,
    nsend, nrecv, hsend, hrecv, psend, precv, ahead_ref, stage, usend, urecv, lead_ref, done_ref,
    in_sem, e_sem, x_sem, pair_s, pair_r, halo_s, halo_r,
    p_s, p_r, stage_r, u_s, u_r, g_s, g_r, f_r, l_s, l_r,
):
    rank, width = w_ref.shape
    genes = h_ref.shape[1]
    cols = genes // owners
    me = lax.axis_index("tile")
    core = lax.axis_index("gene")
    other = 1 - core
    barrier = pltpu.get_barrier_semaphore()

    small = [
        pltpu.make_async_copy(src, dst, in_sem.at[i])
        for i, (src, dst) in enumerate(
            ((w_hbm, w_ref), (t_hbm, t_ref), (nb_hbm, nb_ref))
        )
    ]

    size = genes // loads

    def first_loads(c):
        part = pl.ds(c * size, size)
        rows = ((width - BORDER, 0), (0, BORDER))
        return [pltpu.make_async_copy(h_hbm.at[:, part], h_ref.at[:, part], e_sem.at[c, 2])] + [
            pltpu.make_async_copy(
                x_hbm.at[pl.ds(source, BORDER), part], x_ref.at[pl.ds(target, BORDER), part],
                e_sem.at[c, side],
            )
            for side, (source, target) in enumerate(rows)
        ]

    def inner_load(c):
        part = pl.ds(c * size, size)
        return pltpu.make_async_copy(
            x_hbm.at[pl.ds(BORDER, width - RIM), part],
            x_ref.at[pl.ds(RIM, width - RIM), part],
            x_sem.at[c],
        )

    for copy in small[:2]:
        copy.start()
    for c in range(loads):
        for copy in first_loads(c):
            copy.start()
    for c in range(loads):
        inner_load(c).start()
    small[2].start()

    def has(side):
        return me > 0 if side == 0 else me < n - 1

    def greet(i, carry):
        pl.semaphore_signal(
            barrier, inc=1, device_id={"tile": lax.rem(me + i, n), "gene": other},
            device_id_type=MESH,
        )
        return carry

    few = n <= 16
    lax.fori_loop(1, n, greet, 0, unroll=few)
    pl.semaphore_signal(barrier, inc=1, device_id={"gene": other}, device_id_type=MESH)
    for side in range(2):
        @pl.when(has(side))
        def _():
            pl.semaphore_signal(
                barrier, inc=1, device_id={"tile": me - 1 + 2 * side}, device_id_type=MESH
            )

    for side in range(2):
        @pl.when(jnp.logical_not(has(side)))
        def _():
            hrecv[:, side] = jnp.zeros(hrecv.shape[:1] + hrecv.shape[2:], f32)
    halo_ref[...] = jnp.zeros_like(halo_ref)

    def halo_rows(p):
        return pl.ds(0, 2 * SUB if p == 0 else SUB)

    def halo_copy(p, side, k):
        return pltpu.make_async_remote_copy(
            src_ref=hsend.at[p, side, halo_rows(p)], dst_ref=hrecv.at[p, 1 - side, core, halo_rows(p)],
            send_sem=halo_s.at[p, side], recv_sem=halo_r.at[p, 1 - side],
            device_id={"tile": me - 1 + 2 * side, "gene": core if k == 0 else other},
            device_id_type=MESH,
        )

    def halo_both(p, side):
        ref = hrecv.at[p, side, :, halo_rows(p)]
        return pltpu.make_async_remote_copy(
            src_ref=ref, dst_ref=ref, send_sem=halo_s.at[p, side], recv_sem=halo_r.at[p, side],
            device_id={"tile": lax.rem(me + 1, n)}, device_id_type=MESH,
        )

    def pair_copy(p):
        part = pl.ds(0, width + LANES if p == 0 else width)
        return pltpu.make_async_remote_copy(
            src_ref=nsend.at[p, :, part], dst_ref=nrecv.at[p, :, part],
            send_sem=pair_s.at[p], recv_sem=pair_r.at[p],
            device_id={"gene": other}, device_id_type=MESH,
        )

    blk = cols // quarters

    relayed = range(quarters - relays, quarters)
    early = range(relays)
    even = lax.rem(me, 2) == 0
    mate = me + 1 - 2 * lax.rem(me, 2)
    far = lax.rem(me + n // 2, n)
    far_mate = far + 1 - 2 * lax.rem(far, 2)

    def when_owner(index, call):
        if owners == n:
            call()
        else:
            pl.when(index < owners)(call)

    def move(src, dst, ssem, rsem, tile, gene=None):
        return pltpu.make_async_remote_copy(
            src_ref=src, dst_ref=dst, send_sem=ssem, recv_sem=rsem,
            device_id={"tile": tile, "gene": other if gene is None else gene},
            device_id_type=MESH,
        )

    def lead_copy():
        mine = pl.ds(pl.multiple_of(me * cols, LANES), cols)
        return move(h_ref.at[:, mine], lead_ref, l_s, l_r, me)

    rims, inner = slice(0, RIM), slice(RIM, width)

    def ratio_of(lhs, rows, at, size):
        product = jnp.dot(lhs, h_ref[:, pl.ds(at, size)], preferred_element_type=f32)
        return quotient(x_ref[rows, pl.ds(at, size)].astype(f32), product).astype(bf16)

    def numer_of(lhs, rows, begin, sums=False):
        acc = None
        for c in range(genes // step):
            if begin is not None:
                begin(c)
            ratio = ratio_of(lhs, rows, c * step, step)
            if sums:
                ratio = jnp.concatenate([ratio, jnp.ones((2 * SUB, step), bf16)], axis=0)
            part = lax.dot_general(
                h_ref[:, pl.ds(c * step, step)], ratio,
                (((1,), (1,)), ((), ())), preferred_element_type=f32,
            )
            acc = part if acc is None else acc + part
        return acc

    def put_halo(p, numer):
        value = (cells * mask)[:, rims] * numer
        for side, first in enumerate((BORDER, 0)):
            for g in range(rank // SUB):
                hsend[p, side, 0:SUB, g * BORDER : (g + 1) * BORDER] = value[
                    g * SUB : (g + 1) * SUB, first : first + BORDER
                ]

    wide = min(4 * step, genes)
    small[0].wait()
    small[1].wait()
    cells = pltpu.roll(w_ref[...], BORDER, 1)
    mrow = pltpu.roll(jnp.broadcast_to(t_ref[...].astype(f32), (2 * SUB, width)), BORDER, 1)
    mask = jnp.broadcast_to(mrow[0:1], (rank, width))
    inside = mask > 0.0
    for side in range(2):
        hsend[0, side, SUB : 2 * SUB, 0:LANES] = jnp.where(
            lane_of((SUB, LANES)) < RIM, mrow[0:SUB, 0:LANES], 0.0
        )
    lhs = jnp.transpose(cells).astype(bf16)
    def halo_start(p):
        for side in range(2):
            @pl.when(has(side))
            def _():
                halo_copy(p, side, 0).start()
                halo_copy(p, side, 1).start()

    every = max(genes // loads // step, 1)

    def arrive(c):
        if c % every == 0:
            inner_load(c // every).wait()

    def first_arrive(c):
        if c % every == 0:
            for copy in first_loads(c // every):
                copy.wait()

    for p in range(PASSES):
        numer_rim = numer_of(lhs[rims], rims, first_arrive if p == 0 else None, p == 0)
        if p == 0:
            nsend[0, :, width : width + LANES] = jnp.broadcast_to(
                numer_rim[:, RIM : RIM + 1], (rank, LANES)
            )
            numer_rim = numer_rim[:, rims]
        put_halo(p, numer_rim)
        if p == 0:
            pl.semaphore_wait(
                barrier, n + has(0).astype(jnp.int32) + has(1).astype(jnp.int32)
            )
        halo_start(p)
        if p == 0:
            when_owner(me, lambda: lead_copy().start())
        numer_inner = numer_of(lhs[inner], inner, arrive if p == 0 else None)
        nsend[p, :, rims] = numer_rim
        nsend[p, :, inner] = numer_inner
        pair_copy(p).start()
        if p == 0:
            small[2].wait()
            a = pltpu.roll(nb_ref[...], BORDER, 1) - (me * width - BORDER)
            spot = jnp.where(a < BORDER, a + width, a)
            spot = jnp.where(jnp.logical_and(a >= width, a < width + BORDER), a - width, spot)
            for at in range(0, width + LANES, BORDER):
                index = lax.broadcasted_iota(jnp.int32, (BORDER, width), 0) + at
                total = jnp.zeros((BORDER, width), f32)
                for j in range(nb_ref.shape[0]):
                    total = total + jnp.where(spot[j : j + 1] == index, 1.0, 0.0)
                near_ref[at : at + BORDER, :] = total.astype(bf16)
        pair_copy(p).wait_recv()
        if p == 0:
            inverse = 1.0 / (
                nsend[0, :, width : width + LANES] + nrecv[0, :, width : width + LANES]
            )
            inverse_wide = jnp.concatenate([inverse] * (width // LANES), axis=1)
        numer = nsend[p, :, 0:width] + nrecv[p, :, 0:width]
        updated = jnp.where(inside, cells * numer * inverse_wide, cells)
        stacked = jnp.concatenate(split(updated * mask) + (mrow.astype(bf16),), axis=0)
        mixed = jnp.dot(stacked, near_ref[0:width, :], preferred_element_type=f32)
        near = mixed[0:rank] + mixed[rank : 2 * rank]
        if p == 0:
            count = mixed[2 * rank : 2 * rank + 1]
        cells = jnp.where(
            inside,
            (1.0 - smooth_weight) * updated + smooth_weight * near / jnp.maximum(count, 1.0),
            updated,
        )
        if p + 1 == PASSES:
            lhs = jnp.transpose(cells).astype(bf16)[inner]
            lift = jnp.concatenate(split(cells * mask), axis=0)[:, inner]
            for at in range(0, genes, wide):
                both = jnp.dot(
                    lift, ratio_of(lhs, inner, at, wide), preferred_element_type=f32
                )
                acc_ref[:, pl.ds(at, wide)] = both[0:rank] + both[rank : 2 * rank]
        for side in range(2):
            @pl.when(has(side))
            def _():
                halo_both(p, side).wait_recv()
        for side in range(2):
            packed = hrecv[p, side, 0, 0:SUB] + hrecv[p, side, 1, 0:SUB]
            for g in range(rank // SUB):
                halo_ref[g * SUB : (g + 1) * SUB, side * BORDER : (side + 1) * BORDER] = packed[
                    :, g * BORDER : (g + 1) * BORDER
                ]
        halo = halo_ref[...] * inverse
        if p == 0:
            flags = jnp.where(
                lane_of((SUB, LANES)) < BORDER,
                hrecv[0, 0, 0, SUB : 2 * SUB, 0:LANES], hrecv[0, 1, 0, SUB : 2 * SUB, 0:LANES],
            )
            flags = jnp.concatenate([flags, flags], axis=0).astype(bf16)
        stacked = jnp.concatenate(split(halo) + (flags,), axis=0)
        mixed = jnp.dot(
            stacked, near_ref[width : width + LANES, 0:LANES], preferred_element_type=f32
        )
        near_rim = near[:, 0:LANES] + (mixed[0:rank] + mixed[rank : 2 * rank])
        if p == 0:
            count_rim = jnp.maximum(count[:, 0:LANES] + mixed[2 * rank : 2 * rank + 1], 1.0)
        rim = updated[:, 0:LANES]
        rim = jnp.where(
            inside[:, 0:LANES],
            (1.0 - smooth_weight) * rim + smooth_weight * near_rim / count_rim,
            rim,
        )
        cells = jnp.concatenate([rim, cells[:, LANES:]], axis=1)
        lhs = jnp.transpose(cells).astype(bf16)

    weighted = cells * mask
    den_part = jnp.sum(weighted, axis=1, keepdims=True)
    lift = jnp.concatenate(split(weighted[:, 0:LANES]), axis=0)[:, rims]

    def part_start(q, j):
        o = lax.rem(me + j, n)

        def call():
            slot = lax.rem(n - j, n)
            move(psend.at[q * owners + o], precv.at[q, slot], p_s, p_r.at[q], o).start()

        if q in relayed:
            if j in (n // 2 - 1, n // 2 + 1):
                pl.when(o != far_mate)(call)
            elif j != n // 2:
                call()
        else:
            when_owner(o, call)

    def unit_start(j):
        o = lax.rem(me + j, n)
        when_owner(
            o,
            lambda: move(
                usend.at[pl.ds(0, 1)], urecv.at[pl.ds(lax.rem(n - j, n), 1)], u_s, u_r.at[0], o
            ).start(),
        )

    def all_peers(call):
        if few:
            for j in sorted(range(n), key=lambda j: (abs(j - n // 2), j)):
                call(j)
        else:
            def body(j, carry):
                call(j)
                return carry

            lax.fori_loop(0, n, body, 0)

    top = jnp.full((rank, 1), 1e-30, f32)
    for at in range(0, genes, wide):
        both = jnp.dot(lift, ratio_of(lhs[rims], rims, at, wide), preferred_element_type=f32)
        total = acc_ref[:, pl.ds(at, wide)] + (both[0:rank] + both[rank : 2 * rank])
        acc_ref[:, pl.ds(at, wide)] = total
        top = jnp.maximum(top, jnp.max(total, axis=1, keepdims=True))
    usend[...] = jnp.broadcast_to(row_of((top * (1.0 / TOP), den_part)), usend.shape)
    if relays:
        move(
            usend.at[pl.ds(0, 1)], urecv.at[pl.ds(n, 1)], u_s, u_r.at[1], mate, core
        ).start()
    all_peers(unit_start)
    scale = TOP / top

    def code(at):
        value = acc_ref[:, pl.ds(at, blk)] * scale + (0.5 - HALF)
        return jnp.floor(value).astype(jnp.int32).astype(WIRE)

    for i, q in enumerate(relayed):
        ahead_ref[i] = code(pl.multiple_of(far_mate * cols + q * blk, LANES))
        move(ahead_ref.at[i], stage.at[i], p_s, stage_r.at[i], mate, core).start()
    for q in range(quarters):
        for o in range(owners):
            psend[q * owners + o] = code(o * cols + q * blk)
        all_peers(lambda j: part_start(q, j))
    cells_ref[...] = pltpu.roll(cells, width - BORDER, 1)

    def gene_start(q, j):
        o = lax.rem(me + j, n)
        come = f_r.at[q] if q in early and j == n // 2 else g_r
        here = pl.ds(pl.multiple_of(me * cols + q * blk, LANES), blk)
        call = move(done_ref.at[q], genes_ref.at[:, here], g_s, come, o).start
        if q in early and j in (n // 2 - 1, n // 2 + 1):
            pl.when(o != far_mate)(call)
        else:
            call()

    ahead = lax.rem(me + 1, n)
    if relays:
        row = urecv.at[pl.ds(n, 1)]
        move(row, row, u_s, u_r.at[1], ahead).wait_recv()
        unit_mate = column_of(urecv[n : n + 1], rank)
        joint = 1.0 / (top * (1.0 / TOP) + unit_mate)
    for i, q in enumerate(relayed):
        move(stage.at[i], stage.at[i], p_s, stage_r.at[i], ahead).wait_recv()
        there = pl.ds(pl.multiple_of(far * cols + q * blk, LANES), blk)
        value = (stage[i].astype(jnp.int32).astype(f32) + HALF) * unit_mate
        value = (acc_ref[:, there] + value) * joint + (0.5 - HALF)
        psend[q * owners + far] = jnp.floor(value).astype(jnp.int32).astype(WIRE)
        move(psend.at[q * owners + far], precv.at[q, n // 2], p_s, p_r.at[q], far).start()

    def finish_part():
        rows = urecv.at[pl.ds(0, n)]
        move(rows, rows, u_s, u_r.at[0], ahead).wait_recv()
        lead_copy().wait_recv()
        units = jnp.transpose(urecv[...])
        inverse_den = 1.0 / jnp.sum(units[rank : 2 * rank, 0:n], axis=1, keepdims=True)
        unit_of = [units[0:rank, slot : slot + 1] for slot in range(n)]
        if relays:
            middle = n // 2
            joint_of = list(unit_of)
            joint_of[middle] += jnp.where(even, unit_of[middle + 1], unit_of[middle - 1])
            joint_of[middle + 1] = jnp.where(even, 0.0, unit_of[middle + 1])
            joint_of[middle - 1] = jnp.where(even, unit_of[middle - 1], 0.0)
        for q in range(quarters):
            come = precv.at[q, pl.ds(0, n - 1 if q in relayed else n)]
            move(come, come, p_s, p_r.at[q], ahead).wait_recv()
            total = jnp.zeros((rank, blk), f32)
            for slot in range(n):
                value = precv[q, slot].astype(jnp.int32).astype(f32) + HALF
                total = total + value * (joint_of if q in relayed else unit_of)[slot]
            lead = lead_ref[:, q * blk : (q + 1) * blk].astype(f32) * inverse_den
            done_ref[q] = (lead * total).astype(done_ref.dtype)
            all_peers(lambda j: gene_start(q, j))

    when_owner(me, finish_part)
    for q in early:
        there = genes_ref.at[:, pl.ds(pl.multiple_of(far * cols + q * blk, LANES), blk)]
        move(there, there, g_s, f_r.at[q], ahead).wait_recv()
        move(there, there, g_s, g_r, mate, core).start()
    ref = genes_ref.at[:, pl.ds(0, genes - len(early) * blk)]
    move(ref, ref, g_s, g_r, ahead).wait_recv()
    move(psend, psend, p_s, g_r, ahead).wait_send()
    rows = urecv.at[pl.ds(0, owners + 1 if relays else owners)]
    move(rows, rows, u_s, g_r, ahead).wait_send()

    def sent_blocks():
        move(precv, precv, g_s, g_r, ahead).wait_send()
        lead_copy().wait_send()

    when_owner(me, sent_blocks)
    for p in range(PASSES):
        pair_copy(p).wait_send()
        for side in range(2):
            @pl.when(has(side))
            def _():
                halo_both(p, side).wait_send()


def settle(cells_in, genes_in, cells_ref, genes_ref):
    cells_ref[...] = cells_in[...]
    genes_ref[...] = genes_in[...]


def on_device(n, counts, cell_factor, gene_factor, tissue, neighbours):
    width, genes = counts.shape
    rank = cell_factor.shape[0]
    near = neighbours.shape[0]
    owners = min(n, genes // LANES)
    step = min(512, genes)
    loads = min(2, genes // step)
    cols = genes // owners
    quarters = max(1, min(4, cols // LANES))
    relays = quarters // 2 if n == owners and n % 4 == 0 and n <= 16 else 0
    dma = pltpu.SemaphoreType.DMA
    vmem = pl.BlockSpec(memory_space=pltpu.VMEM)
    shapes = (
        jax.ShapeDtypeStruct((rank, width), f32),
        jax.ShapeDtypeStruct((rank, genes), bf16),
    )
    results = pl.pallas_call(
        functools.partial(kernel, n, owners, quarters, relays, step, loads),
        out_shape=tuple(pltpu.VMEM(s.shape, s.dtype) for s in shapes),
        in_specs=[pl.BlockSpec(memory_space=pl.ANY)] * 5,
        out_specs=(vmem, vmem),
        scratch_shapes=[
            pltpu.VMEM((width, genes), jnp.int32),
            pltpu.VMEM((rank, width), f32),
            pltpu.VMEM((rank, genes), bf16),
            pltpu.VMEM((1, width), jnp.int32),
            pltpu.VMEM((near, width), jnp.int32),
            pltpu.VMEM((width + LANES, width), bf16),
            pltpu.VMEM((rank, genes), f32),
            pltpu.VMEM((rank, LANES), f32),
            pltpu.VMEM((PASSES, rank, width + LANES), f32),
            pltpu.VMEM((PASSES, rank, width + LANES), f32),
            pltpu.VMEM((PASSES, 2, 2 * SUB, max(rank // SUB * BORDER, LANES)), f32),
            pltpu.VMEM((PASSES, 2, 2, 2 * SUB, max(rank // SUB * BORDER, LANES)), f32),
            pltpu.VMEM((quarters * owners, rank, cols // quarters), WIRE),
            pltpu.VMEM((quarters, n, rank, cols // quarters), WIRE),
            pltpu.VMEM((max(relays, 1), rank, cols // quarters), WIRE),
            pltpu.VMEM((max(relays, 1), rank, cols // quarters), WIRE),
            pltpu.VMEM((SUB, LANES), f32),
            pltpu.VMEM((pl.cdiv(n + 1, LANES) * LANES, LANES), f32),
            pltpu.VMEM((rank, cols), bf16),
            pltpu.VMEM((quarters, rank, cols // quarters), bf16),
            dma((3,)),
            dma((loads, 3)),
            dma((loads,)),
            dma((PASSES,)),
            dma((PASSES,)),
            dma((PASSES, 2)),
            dma((PASSES, 2)),
            dma,
            dma((quarters,)),
            dma((max(relays, 1),)),
            dma,
            dma((2,)),
            dma,
            dma,
            dma((max(relays, 1),)),
            dma,
            dma,
        ],
        compiler_params=pltpu.CompilerParams(
            collective_id=0, has_side_effects=True, vmem_limit_bytes=63_160_000
        ),
    )(counts, cell_factor, gene_factor, tissue.reshape(1, width), neighbours)
    return pl.pallas_call(
        settle, out_shape=shapes, in_specs=[vmem] * 2, out_specs=(vmem, vmem),
        compiler_params=pltpu.CompilerParams(vmem_limit_bytes=16 * 1024 * 1024),
    )(*results)


def solution(mesh):
    return jax.shard_map(
        functools.partial(on_device, mesh.shape["tile"]),
        mesh=mesh,
        in_specs=(
            P(("grp", "tile"), "gene"),
            P(None, ("grp", "tile")),
            P(None, ("grp", "gene")),
            P(("grp", "tile")),
            P(None, ("grp", "tile")),
        ),
        out_specs=(P(None, ("grp", "tile")), P(None, ("grp", "gene"))),
        check_vma=False,
    )
```

```python
import functools

import jax
import jax.numpy as jnp
from jax import lax
from jax.experimental import pallas as pl
from jax.experimental.pallas import tpu as pltpu
from jax.sharding import PartitionSpec as P

BORDER = 32
RIM = 2 * BORDER
PASSES = 2
LANES = 128
SUB = 8
MESH = pl.DeviceIdType.MESH
WIRE = jnp.int16
TOP = 65000.0
HALF = 32768.0

smooth_weight = 0.5

f32 = jnp.float32
bf16 = jnp.bfloat16


def split(value):
    high = value.astype(bf16)
    low = (value - high.astype(f32)).astype(bf16)
    return high, low


def quotient(top, bottom):
    r = pl.reciprocal(bottom, approx=True)
    return top * r


def lane_of(shape):
    return lax.broadcasted_iota(jnp.int32, shape, 1)


def row_of(columns):
    rank = columns[0].shape[0]
    index = lax.broadcasted_iota(jnp.int32, (rank, LANES), 0)
    lane = lane_of((rank, LANES))
    spread = jnp.zeros((rank, LANES), f32)
    for g, column in enumerate(columns):
        spread = jnp.where(lane == index + g * rank, column, spread)
    return jnp.sum(spread, axis=0, keepdims=True)


def column_of(row, rank):
    index = lax.broadcasted_iota(jnp.int32, (rank, LANES), 0)
    return jnp.sum(jnp.where(lane_of((rank, LANES)) == index, row, 0.0), axis=1, keepdims=True)


def kernel(
    n, owners, quarters, relays, step, loads,
    x_hbm, w_hbm, h_hbm, t_hbm, nb_hbm,
    cells_ref, genes_ref,
    x_ref, w_ref, h_ref, t_ref, nb_ref, near_ref, acc_ref, halo_ref,
    nsend, nrecv, hsend, hrecv, psend, precv, ahead_ref, stage, usend, urecv, lead_ref, done_ref,
    in_sem, e_sem, x_sem, pair_s, pair_r, halo_s, halo_r,
    p_s, p_r, stage_r, u_s, u_r, g_s, g_r, f_r, l_s, l_r,
):
    rank, width = w_ref.shape
    genes = h_ref.shape[1]
    cols = genes // owners
    me = lax.axis_index("tile")
    core = lax.axis_index("gene")
    other = 1 - core
    barrier = pltpu.get_barrier_semaphore()

    small = [
        pltpu.make_async_copy(src, dst, in_sem.at[i])
        for i, (src, dst) in enumerate(
            ((w_hbm, w_ref), (t_hbm, t_ref), (nb_hbm, nb_ref))
        )
    ]

    size = genes // loads

    def first_loads(c):
        part = pl.ds(c * size, size)
        rows = ((width - BORDER, 0), (0, BORDER))
        return [pltpu.make_async_copy(h_hbm.at[:, part], h_ref.at[:, part], e_sem.at[c, 2])] + [
            pltpu.make_async_copy(
                x_hbm.at[pl.ds(source, BORDER), part], x_ref.at[pl.ds(target, BORDER), part],
                e_sem.at[c, side],
            )
            for side, (source, target) in enumerate(rows)
        ]

    def inner_load(c):
        part = pl.ds(c * size, size)
        return pltpu.make_async_copy(
            x_hbm.at[pl.ds(BORDER, width - RIM), part],
            x_ref.at[pl.ds(RIM, width - RIM), part],
            x_sem.at[c],
        )

    for copy in small[:2]:
        copy.start()
    for c in range(loads):
        for copy in first_loads(c):
            copy.start()
    for c in range(loads):
        inner_load(c).start()
    small[2].start()

    def has(side):
        return me > 0 if side == 0 else me < n - 1

    def greet(i, carry):
        pl.semaphore_signal(
            barrier, inc=1, device_id={"tile": lax.rem(me + i, n), "gene": other},
            device_id_type=MESH,
        )
        return carry

    few = n <= 16
    lax.fori_loop(1, n, greet, 0, unroll=few)
    pl.semaphore_signal(barrier, inc=1, device_id={"gene": other}, device_id_type=MESH)
    for side in range(2):
        @pl.when(has(side))
        def _():
            pl.semaphore_signal(
                barrier, inc=1, device_id={"tile": me - 1 + 2 * side}, device_id_type=MESH
            )

    for side in range(2):
        @pl.when(jnp.logical_not(has(side)))
        def _():
            hrecv[:, side] = jnp.zeros(hrecv.shape[:1] + hrecv.shape[2:], f32)
    halo_ref[...] = jnp.zeros_like(halo_ref)

    def halo_rows(p):
        return pl.ds(0, 2 * SUB if p == 0 else SUB)

    def halo_copy(p, side, k):
        return pltpu.make_async_remote_copy(
            src_ref=hsend.at[p, side, halo_rows(p)], dst_ref=hrecv.at[p, 1 - side, core, halo_rows(p)],
            send_sem=halo_s.at[p, side], recv_sem=halo_r.at[p, 1 - side],
            device_id={"tile": me - 1 + 2 * side, "gene": core if k == 0 else other},
            device_id_type=MESH,
        )

    def halo_both(p, side):
        ref = hrecv.at[p, side, :, halo_rows(p)]
        return pltpu.make_async_remote_copy(
            src_ref=ref, dst_ref=ref, send_sem=halo_s.at[p, side], recv_sem=halo_r.at[p, side],
            device_id={"tile": lax.rem(me + 1, n)}, device_id_type=MESH,
        )

    def pair_copy(p):
        part = pl.ds(0, width + LANES if p == 0 else width)
        return pltpu.make_async_remote_copy(
            src_ref=nsend.at[p, :, part], dst_ref=nrecv.at[p, :, part],
            send_sem=pair_s.at[p], recv_sem=pair_r.at[p],
            device_id={"gene": other}, device_id_type=MESH,
        )

    blk = cols // quarters

    relayed = range(quarters - relays, quarters)
    early = range(relays)
    even = lax.rem(me, 2) == 0
    mate = me + 1 - 2 * lax.rem(me, 2)
    far = lax.rem(me + n // 2, n)
    far_mate = far + 1 - 2 * lax.rem(far, 2)

    def when_owner(index, call):
        if owners == n:
            call()
        else:
            pl.when(index < owners)(call)

    def move(src, dst, ssem, rsem, tile, gene=None):
        return pltpu.make_async_remote_copy(
            src_ref=src, dst_ref=dst, send_sem=ssem, recv_sem=rsem,
            device_id={"tile": tile, "gene": other if gene is None else gene},
            device_id_type=MESH,
        )

    def lead_copy():
        mine = pl.ds(pl.multiple_of(me * cols, LANES), cols)
        return move(h_ref.at[:, mine], lead_ref, l_s, l_r, me)

    rims, inner = slice(0, RIM), slice(RIM, width)

    def ratio_of(lhs, rows, at, size):
        product = jnp.dot(lhs, h_ref[:, pl.ds(at, size)], preferred_element_type=f32)
        return quotient(x_ref[rows, pl.ds(at, size)].astype(f32), product).astype(bf16)

    def numer_of(lhs, rows, begin, sums=False):
        acc = None
        for c in range(genes // step):
            if begin is not None:
                begin(c)
            ratio = ratio_of(lhs, rows, c * step, step)
            if sums:
                ratio = jnp.concatenate([ratio, jnp.ones((2 * SUB, step), bf16)], axis=0)
            part = lax.dot_general(
                h_ref[:, pl.ds(c * step, step)], ratio,
                (((1,), (1,)), ((), ())), preferred_element_type=f32,
            )
            acc = part if acc is None else acc + part
        return acc

    def put_halo(p, numer):
        value = (cells * mask)[:, rims] * numer
        for side, first in enumerate((BORDER, 0)):
            for g in range(rank // SUB):
                hsend[p, side, 0:SUB, g * BORDER : (g + 1) * BORDER] = value[
                    g * SUB : (g + 1) * SUB, first : first + BORDER
                ]

    wide = min(4 * step, genes)
    small[0].wait()
    small[1].wait()
    cells = pltpu.roll(w_ref[...], BORDER, 1)
    mrow = pltpu.roll(jnp.broadcast_to(t_ref[...].astype(f32), (2 * SUB, width)), BORDER, 1)
    mask = jnp.broadcast_to(mrow[0:1], (rank, width))
    inside = mask > 0.0
    for side in range(2):
        hsend[0, side, SUB : 2 * SUB, 0:LANES] = jnp.where(
            lane_of((SUB, LANES)) < RIM, mrow[0:SUB, 0:LANES], 0.0
        )
    lhs = jnp.transpose(cells).astype(bf16)
    def halo_start(p):
        for side in range(2):
            @pl.when(has(side))
            def _():
                halo_copy(p, side, 0).start()
                halo_copy(p, side, 1).start()

    every = max(genes // loads // step, 1)

    def arrive(c):
        if c % every == 0:
            inner_load(c // every).wait()

    def first_arrive(c):
        if c % every == 0:
            for copy in first_loads(c // every):
                copy.wait()

    for p in range(PASSES):
        numer_rim = numer_of(lhs[rims], rims, first_arrive if p == 0 else None, p == 0)
        if p == 0:
            nsend[0, :, width : width + LANES] = jnp.broadcast_to(
                numer_rim[:, RIM : RIM + 1], (rank, LANES)
            )
            numer_rim = numer_rim[:, rims]
        put_halo(p, numer_rim)
        if p == 0:
            pl.semaphore_wait(
                barrier, n + has(0).astype(jnp.int32) + has(1).astype(jnp.int32)
            )
        halo_start(p)
        if p == 0:
            when_owner(me, lambda: lead_copy().start())
        numer_inner = numer_of(lhs[inner], inner, arrive if p == 0 else None)
        nsend[p, :, rims] = numer_rim
        nsend[p, :, inner] = numer_inner
        pair_copy(p).start()
        if p == 0:
            small[2].wait()
            a = pltpu.roll(nb_ref[...], BORDER, 1) - (me * width - BORDER)
            spot = jnp.where(a < BORDER, a + width, a)
            spot = jnp.where(jnp.logical_and(a >= width, a < width + BORDER), a - width, spot)
            for at in range(0, width + LANES, BORDER):
                index = lax.broadcasted_iota(jnp.int32, (BORDER, width), 0) + at
                total = jnp.zeros((BORDER, width), f32)
                for j in range(nb_ref.shape[0]):
                    total = total + jnp.where(spot[j : j + 1] == index, 1.0, 0.0)
                near_ref[at : at + BORDER, :] = total.astype(bf16)
        pair_copy(p).wait_recv()
        if p == 0:
            inverse = 1.0 / (
                nsend[0, :, width : width + LANES] + nrecv[0, :, width : width + LANES]
            )
            inverse_wide = jnp.concatenate([inverse] * (width // LANES), axis=1)
        numer = nsend[p, :, 0:width] + nrecv[p, :, 0:width]
        updated = jnp.where(inside, cells * numer * inverse_wide, cells)
        stacked = jnp.concatenate(split(updated * mask) + (mrow.astype(bf16),), axis=0)
        mixed = jnp.dot(stacked, near_ref[0:width, :], preferred_element_type=f32)
        near = mixed[0:rank] + mixed[rank : 2 * rank]
        if p == 0:
            count = mixed[2 * rank : 2 * rank + 1]
        cells = jnp.where(
            inside,
            (1.0 - smooth_weight) * updated + smooth_weight * near / jnp.maximum(count, 1.0),
            updated,
        )
        if p + 1 == PASSES:
            lhs = jnp.transpose(cells).astype(bf16)[inner]
            lift = jnp.concatenate(split(cells * mask), axis=0)[:, inner]
            for at in range(0, genes, wide):
                both = jnp.dot(
                    lift, ratio_of(lhs, inner, at, wide), preferred_element_type=f32
                )
                acc_ref[:, pl.ds(at, wide)] = both[0:rank] + both[rank : 2 * rank]
        for side in range(2):
            @pl.when(has(side))
            def _():
                halo_both(p, side).wait_recv()
        for side in range(2):
            packed = hrecv[p, side, 0, 0:SUB] + hrecv[p, side, 1, 0:SUB]
            for g in range(rank // SUB):
                halo_ref[g * SUB : (g + 1) * SUB, side * BORDER : (side + 1) * BORDER] = packed[
                    :, g * BORDER : (g + 1) * BORDER
                ]
        halo = halo_ref[...] * inverse
        if p == 0:
            flags = jnp.where(
                lane_of((SUB, LANES)) < BORDER,
                hrecv[0, 0, 0, SUB : 2 * SUB, 0:LANES], hrecv[0, 1, 0, SUB : 2 * SUB, 0:LANES],
            )
            flags = jnp.concatenate([flags, flags], axis=0).astype(bf16)
        stacked = jnp.concatenate(split(halo) + (flags,), axis=0)
        mixed = jnp.dot(
            stacked, near_ref[width : width + LANES, 0:LANES], preferred_element_type=f32
        )
        near_rim = near[:, 0:LANES] + (mixed[0:rank] + mixed[rank : 2 * rank])
        if p == 0:
            count_rim = jnp.maximum(count[:, 0:LANES] + mixed[2 * rank : 2 * rank + 1], 1.0)
        rim = updated[:, 0:LANES]
        rim = jnp.where(
            inside[:, 0:LANES],
            (1.0 - smooth_weight) * rim + smooth_weight * near_rim / count_rim,
            rim,
        )
        cells = jnp.concatenate([rim, cells[:, LANES:]], axis=1)
        lhs = jnp.transpose(cells).astype(bf16)

    weighted = cells * mask
    den_part = jnp.sum(weighted, axis=1, keepdims=True)
    lift = jnp.concatenate(split(weighted[:, 0:LANES]), axis=0)[:, rims]

    def part_start(q, j):
        o = lax.rem(me + j, n)

        def call():
            slot = lax.rem(n - j, n)
            move(psend.at[q * owners + o], precv.at[q, slot], p_s, p_r.at[q], o).start()

        if q in relayed:
            if j in (n // 2 - 1, n // 2 + 1):
                pl.when(o != far_mate)(call)
            elif j != n // 2:
                call()
        else:
            when_owner(o, call)

    def unit_start(j):
        o = lax.rem(me + j, n)
        when_owner(
            o,
            lambda: move(
                usend.at[pl.ds(0, 1)], urecv.at[pl.ds(lax.rem(n - j, n), 1)], u_s, u_r.at[0], o
            ).start(),
        )

    def all_peers(call):
        if few:
            for j in sorted(range(n), key=lambda j: (abs(j - n // 2), j)):
                call(j)
        else:
            def body(j, carry):
                call(j)
                return carry

            lax.fori_loop(0, n, body, 0)

    top = jnp.full((rank, 1), 1e-30, f32)
    for at in range(0, genes, wide):
        both = jnp.dot(lift, ratio_of(lhs[rims], rims, at, wide), preferred_element_type=f32)
        total = acc_ref[:, pl.ds(at, wide)] + (both[0:rank] + both[rank : 2 * rank])
        acc_ref[:, pl.ds(at, wide)] = total
        top = jnp.maximum(top, jnp.max(total, axis=1, keepdims=True))
    usend[...] = jnp.broadcast_to(row_of((top * (1.0 / TOP), den_part)), usend.shape)
    if relays:
        move(
            usend.at[pl.ds(0, 1)], urecv.at[pl.ds(n, 1)], u_s, u_r.at[1], mate, core
        ).start()
    all_peers(unit_start)
    scale = TOP / top

    def code(at):
        value = acc_ref[:, pl.ds(at, blk)] * scale + (0.5 - HALF)
        return jnp.floor(value).astype(jnp.int32).astype(WIRE)

    for i, q in enumerate(relayed):
        ahead_ref[i] = code(pl.multiple_of(far_mate * cols + q * blk, LANES))
        move(ahead_ref.at[i], stage.at[i], p_s, stage_r.at[i], mate, core).start()
    for q in range(quarters):
        for o in range(owners):
            psend[q * owners + o] = code(o * cols + q * blk)
        all_peers(lambda j: part_start(q, j))
    cells_ref[...] = pltpu.roll(cells, width - BORDER, 1)

    def gene_start(q, j):
        o = lax.rem(me + j, n)
        come = f_r.at[q] if q in early and j == n // 2 else g_r
        here = pl.ds(pl.multiple_of(me * cols + q * blk, LANES), blk)
        call = move(done_ref.at[q], genes_ref.at[:, here], g_s, come, o).start
        if q in early and j in (n // 2 - 1, n // 2 + 1):
            pl.when(o != far_mate)(call)
        else:
            call()

    ahead = lax.rem(me + 1, n)
    if relays:
        row = urecv.at[pl.ds(n, 1)]
        move(row, row, u_s, u_r.at[1], ahead).wait_recv()
        unit_mate = column_of(urecv[n : n + 1], rank)
        joint = 1.0 / (top * (1.0 / TOP) + unit_mate)
    for i, q in enumerate(relayed):
        move(stage.at[i], stage.at[i], p_s, stage_r.at[i], ahead).wait_recv()
        there = pl.ds(pl.multiple_of(far * cols + q * blk, LANES), blk)
        value = (stage[i].astype(jnp.int32).astype(f32) + HALF) * unit_mate
        value = (acc_ref[:, there] + value) * joint + (0.5 - HALF)
        psend[q * owners + far] = jnp.floor(value).astype(jnp.int32).astype(WIRE)
        move(psend.at[q * owners + far], precv.at[q, n // 2], p_s, p_r.at[q], far).start()

    def finish_part():
        rows = urecv.at[pl.ds(0, n)]
        move(rows, rows, u_s, u_r.at[0], ahead).wait_recv()
        lead_copy().wait_recv()
        units = jnp.transpose(urecv[...])
        inverse_den = 1.0 / jnp.sum(units[rank : 2 * rank, 0:n], axis=1, keepdims=True)
        unit_of = [units[0:rank, slot : slot + 1] for slot in range(n)]
        if relays:
            middle = n // 2
            joint_of = list(unit_of)
            joint_of[middle] += jnp.where(even, unit_of[middle + 1], unit_of[middle - 1])
            joint_of[middle + 1] = jnp.where(even, 0.0, unit_of[middle + 1])
            joint_of[middle - 1] = jnp.where(even, unit_of[middle - 1], 0.0)
        for q in range(quarters):
            come = precv.at[q, pl.ds(0, n - 1 if q in relayed else n)]
            move(come, come, p_s, p_r.at[q], ahead).wait_recv()
            total = jnp.zeros((rank, blk), f32)
            for slot in range(n):
                value = precv[q, slot].astype(jnp.int32).astype(f32) + HALF
                total = total + value * (joint_of if q in relayed else unit_of)[slot]
            lead = lead_ref[:, q * blk : (q + 1) * blk].astype(f32) * inverse_den
            done_ref[q] = (lead * total).astype(done_ref.dtype)
            all_peers(lambda j: gene_start(q, j))

    when_owner(me, finish_part)
    for q in early:
        there = genes_ref.at[:, pl.ds(pl.multiple_of(far * cols + q * blk, LANES), blk)]
        move(there, there, g_s, f_r.at[q], ahead).wait_recv()
        move(there, there, g_s, g_r, mate, core).start()
    ref = genes_ref.at[:, pl.ds(0, genes - len(early) * blk)]
    move(ref, ref, g_s, g_r, ahead).wait_recv()
    move(psend, psend, p_s, g_r, ahead).wait_send()
    rows = urecv.at[pl.ds(0, owners + 1 if relays else owners)]
    move(rows, rows, u_s, g_r, ahead).wait_send()

    def sent_blocks():
        move(precv, precv, g_s, g_r, ahead).wait_send()
        lead_copy().wait_send()

    when_owner(me, sent_blocks)
    for p in range(PASSES):
        pair_copy(p).wait_send()
        for side in range(2):
            @pl.when(has(side))
            def _():
                halo_both(p, side).wait_send()


def settle(cells_in, genes_in, cells_ref, genes_ref):
    cells_ref[...] = cells_in[...]
    genes_ref[...] = genes_in[...]


def on_device(n, counts, cell_factor, gene_factor, tissue, neighbours):
    width, genes = counts.shape
    rank = cell_factor.shape[0]
    near = neighbours.shape[0]
    owners = min(n, genes // LANES)
    step = min(512, genes)
    loads = min(2, genes // step)
    cols = genes // owners
    quarters = max(1, min(4, cols // LANES))
    relays = quarters // 2 if n == owners and n % 4 == 0 and n <= 16 else 0
    dma = pltpu.SemaphoreType.DMA
    vmem = pl.BlockSpec(memory_space=pltpu.VMEM)
    shapes = (
        jax.ShapeDtypeStruct((rank, width), f32),
        jax.ShapeDtypeStruct((rank, genes), bf16),
    )
    results = pl.pallas_call(
        functools.partial(kernel, n, owners, quarters, relays, step, loads),
        out_shape=tuple(pltpu.VMEM(s.shape, s.dtype) for s in shapes),
        in_specs=[pl.BlockSpec(memory_space=pl.ANY)] * 5,
        out_specs=(vmem, vmem),
        scratch_shapes=[
            pltpu.VMEM((width, genes), jnp.int32),
            pltpu.VMEM((rank, width), f32),
            pltpu.VMEM((rank, genes), bf16),
            pltpu.VMEM((1, width), jnp.int32),
            pltpu.VMEM((near, width), jnp.int32),
            pltpu.VMEM((width + LANES, width), bf16),
            pltpu.VMEM((rank, genes), f32),
            pltpu.VMEM((rank, LANES), f32),
            pltpu.VMEM((PASSES, rank, width + LANES), f32),
            pltpu.VMEM((PASSES, rank, width + LANES), f32),
            pltpu.VMEM((PASSES, 2, 2 * SUB, max(rank // SUB * BORDER, LANES)), f32),
            pltpu.VMEM((PASSES, 2, 2, 2 * SUB, max(rank // SUB * BORDER, LANES)), f32),
            pltpu.VMEM((quarters * owners, rank, cols // quarters), WIRE),
            pltpu.VMEM((quarters, n, rank, cols // quarters), WIRE),
            pltpu.VMEM((max(relays, 1), rank, cols // quarters), WIRE),
            pltpu.VMEM((max(relays, 1), rank, cols // quarters), WIRE),
            pltpu.VMEM((SUB, LANES), f32),
            pltpu.VMEM((pl.cdiv(n + 1, LANES) * LANES, LANES), f32),
            pltpu.VMEM((rank, cols), bf16),
            pltpu.VMEM((quarters, rank, cols // quarters), bf16),
            dma((3,)),
            dma((loads, 3)),
            dma((loads,)),
            dma((PASSES,)),
            dma((PASSES,)),
            dma((PASSES, 2)),
            dma((PASSES, 2)),
            dma,
            dma((quarters,)),
            dma((max(relays, 1),)),
            dma,
            dma((2,)),
            dma,
            dma,
            dma((max(relays, 1),)),
            dma,
            dma,
        ],
        compiler_params=pltpu.CompilerParams(
            collective_id=0, has_side_effects=True, vmem_limit_bytes=63_160_000
        ),
    )(counts, cell_factor, gene_factor, tissue.reshape(1, width), neighbours)
    return pl.pallas_call(
        settle, out_shape=shapes, in_specs=[vmem] * 2, out_specs=(vmem, vmem),
        compiler_params=pltpu.CompilerParams(vmem_limit_bytes=16 * 1024 * 1024),
    )(*results)


def solution(mesh):
    return jax.shard_map(
        functools.partial(on_device, mesh.shape["tile"]),
        mesh=mesh,
        in_specs=(
            P(("grp", "tile"), "gene"),
            P(None, ("grp", "tile")),
            P(None, ("grp", "gene")),
            P(("grp", "tile")),
            P(None, ("grp", "tile")),
        ),
        out_specs=(P(None, ("grp", "tile")), P(None, ("grp", "gene"))),
        check_vma=False,
    )
```

```python
import functools

import jax
import jax.numpy as jnp
from jax import lax
from jax.experimental import pallas as pl
from jax.experimental.pallas import tpu as pltpu
from jax.sharding import PartitionSpec as P

BORDER = 32
RIM = 2 * BORDER
PASSES = 2
LANES = 128
SUB = 8
MESH = pl.DeviceIdType.MESH
WIRE = jnp.int16
TOP = 65000.0
HALF = 32768.0

smooth_weight = 0.5

f32 = jnp.float32
bf16 = jnp.bfloat16


def split(value):
    high = value.astype(bf16)
    low = (value - high.astype(f32)).astype(bf16)
    return high, low


def quotient(top, bottom):
    r = pl.reciprocal(bottom, approx=True)
    return top * r


def lane_of(shape):
    return lax.broadcasted_iota(jnp.int32, shape, 1)


def row_of(columns):
    rank = columns[0].shape[0]
    index = lax.broadcasted_iota(jnp.int32, (rank, LANES), 0)
    lane = lane_of((rank, LANES))
    spread = jnp.zeros((rank, LANES), f32)
    for g, column in enumerate(columns):
        spread = jnp.where(lane == index + g * rank, column, spread)
    return jnp.sum(spread, axis=0, keepdims=True)


def column_of(row, rank):
    index = lax.broadcasted_iota(jnp.int32, (rank, LANES), 0)
    return jnp.sum(jnp.where(lane_of((rank, LANES)) == index, row, 0.0), axis=1, keepdims=True)


def kernel(
    n, owners, quarters, relays, step, loads,
    x_hbm, w_hbm, h_hbm, t_hbm, nb_hbm,
    cells_ref, genes_ref,
    x_ref, w_ref, h_ref, t_ref, nb_ref, near_ref, acc_ref, halo_ref,
    nsend, nrecv, hsend, hrecv, psend, precv, ahead_ref, stage, usend, urecv, lead_ref, done_ref,
    in_sem, e_sem, x_sem, pair_s, pair_r, halo_s, halo_r,
    p_s, p_r, stage_r, u_s, u_r, g_s, g_r, f_r, l_s, l_r,
):
    rank, width = w_ref.shape
    genes = h_ref.shape[1]
    cols = genes // owners
    me = lax.axis_index("tile")
    core = lax.axis_index("gene")
    other = 1 - core
    barrier = pltpu.get_barrier_semaphore()

    small = [
        pltpu.make_async_copy(src, dst, in_sem.at[i])
        for i, (src, dst) in enumerate(
            ((w_hbm, w_ref), (t_hbm, t_ref), (nb_hbm, nb_ref))
        )
    ]

    size = genes // loads

    def first_loads(c):
        part = pl.ds(c * size, size)
        rows = ((width - BORDER, 0), (0, BORDER))
        return [pltpu.make_async_copy(h_hbm.at[:, part], h_ref.at[:, part], e_sem.at[c, 2])] + [
            pltpu.make_async_copy(
                x_hbm.at[pl.ds(source, BORDER), part], x_ref.at[pl.ds(target, BORDER), part],
                e_sem.at[c, side],
            )
            for side, (source, target) in enumerate(rows)
        ]

    def inner_load(c):
        part = pl.ds(c * size, size)
        return pltpu.make_async_copy(
            x_hbm.at[pl.ds(BORDER, width - RIM), part],
            x_ref.at[pl.ds(RIM, width - RIM), part],
            x_sem.at[c],
        )

    for copy in small[:2]:
        copy.start()
    for c in range(loads):
        for copy in first_loads(c):
            copy.start()
    for c in range(loads):
        inner_load(c).start()
    small[2].start()

    def has(side):
        return me > 0 if side == 0 else me < n - 1

    def greet(i, carry):
        pl.semaphore_signal(
            barrier, inc=1, device_id={"tile": lax.rem(me + i, n), "gene": other},
            device_id_type=MESH,
        )
        return carry

    few = n <= 16
    lax.fori_loop(1, n, greet, 0, unroll=few)
    pl.semaphore_signal(barrier, inc=1, device_id={"gene": other}, device_id_type=MESH)
    for side in range(2):
        @pl.when(has(side))
        def _():
            pl.semaphore_signal(
                barrier, inc=1, device_id={"tile": me - 1 + 2 * side}, device_id_type=MESH
            )

    for side in range(2):
        @pl.when(jnp.logical_not(has(side)))
        def _():
            hrecv[:, side] = jnp.zeros(hrecv.shape[:1] + hrecv.shape[2:], f32)
    halo_ref[...] = jnp.zeros_like(halo_ref)

    def halo_rows(p):
        return pl.ds(0, 2 * SUB if p == 0 else SUB)

    def halo_copy(p, side, k):
        return pltpu.make_async_remote_copy(
            src_ref=hsend.at[p, side, halo_rows(p)], dst_ref=hrecv.at[p, 1 - side, core, halo_rows(p)],
            send_sem=halo_s.at[p, side], recv_sem=halo_r.at[p, 1 - side],
            device_id={"tile": me - 1 + 2 * side, "gene": core if k == 0 else other},
            device_id_type=MESH,
        )

    def halo_both(p, side):
        ref = hrecv.at[p, side, :, halo_rows(p)]
        return pltpu.make_async_remote_copy(
            src_ref=ref, dst_ref=ref, send_sem=halo_s.at[p, side], recv_sem=halo_r.at[p, side],
            device_id={"tile": lax.rem(me + 1, n)}, device_id_type=MESH,
        )

    def pair_copy(p):
        part = pl.ds(0, width + LANES if p == 0 else width)
        return pltpu.make_async_remote_copy(
            src_ref=nsend.at[p, :, part], dst_ref=nrecv.at[p, :, part],
            send_sem=pair_s.at[p], recv_sem=pair_r.at[p],
            device_id={"gene": other}, device_id_type=MESH,
        )

    blk = cols // quarters

    relayed = range(quarters - relays, quarters)
    early = range(relays)
    even = lax.rem(me, 2) == 0
    mate = me + 1 - 2 * lax.rem(me, 2)
    far = lax.rem(me + n // 2, n)
    far_mate = far + 1 - 2 * lax.rem(far, 2)

    def when_owner(index, call):
        if owners == n:
            call()
        else:
            pl.when(index < owners)(call)

    def move(src, dst, ssem, rsem, tile, gene=None):
        return pltpu.make_async_remote_copy(
            src_ref=src, dst_ref=dst, send_sem=ssem, recv_sem=rsem,
            device_id={"tile": tile, "gene": other if gene is None else gene},
            device_id_type=MESH,
        )

    def lead_copy():
        mine = pl.ds(pl.multiple_of(me * cols, LANES), cols)
        return move(h_ref.at[:, mine], lead_ref, l_s, l_r, me)

    rims, inner = slice(0, RIM), slice(RIM, width)

    def ratio_of(lhs, rows, at, size):
        product = jnp.dot(lhs, h_ref[:, pl.ds(at, size)], preferred_element_type=f32)
        return quotient(x_ref[rows, pl.ds(at, size)].astype(f32), product).astype(bf16)

    def numer_of(lhs, rows, begin, sums=False):
        acc = None
        for c in range(genes // step):
            if begin is not None:
                begin(c)
            ratio = ratio_of(lhs, rows, c * step, step)
            if sums:
                ratio = jnp.concatenate([ratio, jnp.ones((2 * SUB, step), bf16)], axis=0)
            part = lax.dot_general(
                h_ref[:, pl.ds(c * step, step)], ratio,
                (((1,), (1,)), ((), ())), preferred_element_type=f32,
            )
            acc = part if acc is None else acc + part
        return acc

    def put_halo(p, numer):
        value = (cells * mask)[:, rims] * numer
        for side, first in enumerate((BORDER, 0)):
            for g in range(rank // SUB):
                hsend[p, side, 0:SUB, g * BORDER : (g + 1) * BORDER] = value[
                    g * SUB : (g + 1) * SUB, first : first + BORDER
                ]

    wide = min(4 * step, genes)
    small[0].wait()
    small[1].wait()
    cells = pltpu.roll(w_ref[...], BORDER, 1)
    mrow = pltpu.roll(jnp.broadcast_to(t_ref[...].astype(f32), (2 * SUB, width)), BORDER, 1)
    mask = jnp.broadcast_to(mrow[0:1], (rank, width))
    inside = mask > 0.0
    for side in range(2):
        hsend[0, side, SUB : 2 * SUB, 0:LANES] = jnp.where(
            lane_of((SUB, LANES)) < RIM, mrow[0:SUB, 0:LANES], 0.0
        )
    lhs = jnp.transpose(cells).astype(bf16)
    def halo_start(p):
        for side in range(2):
            @pl.when(has(side))
            def _():
                halo_copy(p, side, 0).start()
                halo_copy(p, side, 1).start()

    every = max(genes // loads // step, 1)

    def arrive(c):
        if c % every == 0:
            inner_load(c // every).wait()

    def first_arrive(c):
        if c % every == 0:
            for copy in first_loads(c // every):
                copy.wait()

    for p in range(PASSES):
        numer_rim = numer_of(lhs[rims], rims, first_arrive if p == 0 else None, p == 0)
        if p == 0:
            nsend[0, :, width : width + LANES] = jnp.broadcast_to(
                numer_rim[:, RIM : RIM + 1], (rank, LANES)
            )
            numer_rim = numer_rim[:, rims]
        put_halo(p, numer_rim)
        if p == 0:
            pl.semaphore_wait(
                barrier, n + has(0).astype(jnp.int32) + has(1).astype(jnp.int32)
            )
        halo_start(p)
        if p == 0:
            when_owner(me, lambda: lead_copy().start())
        numer_inner = numer_of(lhs[inner], inner, arrive if p == 0 else None)
        nsend[p, :, rims] = numer_rim
        nsend[p, :, inner] = numer_inner
        pair_copy(p).start()
        if p == 0:
            small[2].wait()
            a = pltpu.roll(nb_ref[...], BORDER, 1) - (me * width - BORDER)
            spot = jnp.where(a < BORDER, a + width, a)
            spot = jnp.where(jnp.logical_and(a >= width, a < width + BORDER), a - width, spot)
            for at in range(0, width + LANES, BORDER):
                index = lax.broadcasted_iota(jnp.int32, (BORDER, width), 0) + at
                total = jnp.zeros((BORDER, width), f32)
                for j in range(nb_ref.shape[0]):
                    total = total + jnp.where(spot[j : j + 1] == index, 1.0, 0.0)
                near_ref[at : at + BORDER, :] = total.astype(bf16)
        pair_copy(p).wait_recv()
        if p == 0:
            inverse = 1.0 / (
                nsend[0, :, width : width + LANES] + nrecv[0, :, width : width + LANES]
            )
            inverse_wide = jnp.concatenate([inverse] * (width // LANES), axis=1)
        numer = nsend[p, :, 0:width] + nrecv[p, :, 0:width]
        updated = jnp.where(inside, cells * numer * inverse_wide, cells)
        stacked = jnp.concatenate(split(updated * mask) + (mrow.astype(bf16),), axis=0)
        mixed = jnp.dot(stacked, near_ref[0:width, :], preferred_element_type=f32)
        near = mixed[0:rank] + mixed[rank : 2 * rank]
        if p == 0:
            count = mixed[2 * rank : 2 * rank + 1]
        cells = jnp.where(
            inside,
            (1.0 - smooth_weight) * updated + smooth_weight * near / jnp.maximum(count, 1.0),
            updated,
        )
        if p + 1 == PASSES:
            lhs = jnp.transpose(cells).astype(bf16)[inner]
            lift = jnp.concatenate(split(cells * mask), axis=0)[:, inner]
            for at in range(0, genes, wide):
                both = jnp.dot(
                    lift, ratio_of(lhs, inner, at, wide), preferred_element_type=f32
                )
                acc_ref[:, pl.ds(at, wide)] = both[0:rank] + both[rank : 2 * rank]
        for side in range(2):
            @pl.when(has(side))
            def _():
                halo_both(p, side).wait_recv()
        for side in range(2):
            packed = hrecv[p, side, 0, 0:SUB] + hrecv[p, side, 1, 0:SUB]
            for g in range(rank // SUB):
                halo_ref[g * SUB : (g + 1) * SUB, side * BORDER : (side + 1) * BORDER] = packed[
                    :, g * BORDER : (g + 1) * BORDER
                ]
        halo = halo_ref[...] * inverse
        if p == 0:
            flags = jnp.where(
                lane_of((SUB, LANES)) < BORDER,
                hrecv[0, 0, 0, SUB : 2 * SUB, 0:LANES], hrecv[0, 1, 0, SUB : 2 * SUB, 0:LANES],
            )
            flags = jnp.concatenate([flags, flags], axis=0).astype(bf16)
        stacked = jnp.concatenate(split(halo) + (flags,), axis=0)
        mixed = jnp.dot(
            stacked, near_ref[width : width + LANES, 0:LANES], preferred_element_type=f32
        )
        near_rim = near[:, 0:LANES] + (mixed[0:rank] + mixed[rank : 2 * rank])
        if p == 0:
            count_rim = jnp.maximum(count[:, 0:LANES] + mixed[2 * rank : 2 * rank + 1], 1.0)
        rim = updated[:, 0:LANES]
        rim = jnp.where(
            inside[:, 0:LANES],
            (1.0 - smooth_weight) * rim + smooth_weight * near_rim / count_rim,
            rim,
        )
        cells = jnp.concatenate([rim, cells[:, LANES:]], axis=1)
        lhs = jnp.transpose(cells).astype(bf16)

    weighted = cells * mask
    den_part = jnp.sum(weighted, axis=1, keepdims=True)
    lift = jnp.concatenate(split(weighted[:, 0:LANES]), axis=0)[:, rims]

    def part_start(q, j):
        o = lax.rem(me + j, n)

        def call():
            slot = lax.rem(n - j, n)
            move(psend.at[q * owners + o], precv.at[q, slot], p_s, p_r.at[q], o).start()

        if q in relayed:
            if j in (n // 2 - 1, n // 2 + 1):
                pl.when(o != far_mate)(call)
            elif j != n // 2:
                call()
        else:
            when_owner(o, call)

    def unit_start(j):
        o = lax.rem(me + j, n)
        when_owner(
            o,
            lambda: move(
                usend.at[pl.ds(0, 1)], urecv.at[pl.ds(lax.rem(n - j, n), 1)], u_s, u_r.at[0], o
            ).start(),
        )

    def all_peers(call):
        if few:
            for j in sorted(range(n), key=lambda j: (abs(j - n // 2), j)):
                call(j)
        else:
            def body(j, carry):
                call(j)
                return carry

            lax.fori_loop(0, n, body, 0)

    top = jnp.full((rank, 1), 1e-30, f32)
    for at in range(0, genes, wide):
        both = jnp.dot(lift, ratio_of(lhs[rims], rims, at, wide), preferred_element_type=f32)
        total = acc_ref[:, pl.ds(at, wide)] + (both[0:rank] + both[rank : 2 * rank])
        acc_ref[:, pl.ds(at, wide)] = total
        top = jnp.maximum(top, jnp.max(total, axis=1, keepdims=True))
    usend[...] = jnp.broadcast_to(row_of((top * (1.0 / TOP), den_part)), usend.shape)
    if relays:
        move(
            usend.at[pl.ds(0, 1)], urecv.at[pl.ds(n, 1)], u_s, u_r.at[1], mate, core
        ).start()
    all_peers(unit_start)
    scale = TOP / top

    def code(at):
        value = acc_ref[:, pl.ds(at, blk)] * scale + (0.5 - HALF)
        return jnp.floor(value).astype(jnp.int32).astype(WIRE)

    for i, q in enumerate(relayed):
        ahead_ref[i] = code(pl.multiple_of(far_mate * cols + q * blk, LANES))
        move(ahead_ref.at[i], stage.at[i], p_s, stage_r.at[i], mate, core).start()
    for q in range(quarters):
        for o in range(owners):
            psend[q * owners + o] = code(o * cols + q * blk)
        all_peers(lambda j: part_start(q, j))
    cells_ref[...] = pltpu.roll(cells, width - BORDER, 1)

    def gene_start(q, j):
        o = lax.rem(me + j, n)
        come = f_r.at[q] if q in early and j == n // 2 else g_r
        here = pl.ds(pl.multiple_of(me * cols + q * blk, LANES), blk)
        call = move(done_ref.at[q], genes_ref.at[:, here], g_s, come, o).start
        if q in early and j in (n // 2 - 1, n // 2 + 1):
            pl.when(o != far_mate)(call)
        else:
            call()

    ahead = lax.rem(me + 1, n)
    if relays:
        row = urecv.at[pl.ds(n, 1)]
        move(row, row, u_s, u_r.at[1], ahead).wait_recv()
        unit_mate = column_of(urecv[n : n + 1], rank)
        joint = 1.0 / (top * (1.0 / TOP) + unit_mate)
    for i, q in enumerate(relayed):
        move(stage.at[i], stage.at[i], p_s, stage_r.at[i], ahead).wait_recv()
        there = pl.ds(pl.multiple_of(far * cols + q * blk, LANES), blk)
        value = (stage[i].astype(jnp.int32).astype(f32) + HALF) * unit_mate
        value = (acc_ref[:, there] + value) * joint + (0.5 - HALF)
        psend[q * owners + far] = jnp.floor(value).astype(jnp.int32).astype(WIRE)
        move(psend.at[q * owners + far], precv.at[q, n // 2], p_s, p_r.at[q], far).start()

    def finish_part():
        rows = urecv.at[pl.ds(0, n)]
        move(rows, rows, u_s, u_r.at[0], ahead).wait_recv()
        lead_copy().wait_recv()
        units = jnp.transpose(urecv[...])
        inverse_den = 1.0 / jnp.sum(units[rank : 2 * rank, 0:n], axis=1, keepdims=True)
        unit_of = [units[0:rank, slot : slot + 1] for slot in range(n)]
        if relays:
            middle = n // 2
            joint_of = list(unit_of)
            joint_of[middle] += jnp.where(even, unit_of[middle + 1], unit_of[middle - 1])
            joint_of[middle + 1] = jnp.where(even, 0.0, unit_of[middle + 1])
            joint_of[middle - 1] = jnp.where(even, unit_of[middle - 1], 0.0)
        for q in range(quarters):
            come = precv.at[q, pl.ds(0, n - 1 if q in relayed else n)]
            move(come, come, p_s, p_r.at[q], ahead).wait_recv()
            total = jnp.zeros((rank, blk), f32)
            for slot in range(n):
                value = precv[q, slot].astype(jnp.int32).astype(f32) + HALF
                total = total + value * (joint_of if q in relayed else unit_of)[slot]
            lead = lead_ref[:, q * blk : (q + 1) * blk].astype(f32) * inverse_den
            done_ref[q] = (lead * total).astype(done_ref.dtype)
            all_peers(lambda j: gene_start(q, j))

    when_owner(me, finish_part)
    for q in early:
        there = genes_ref.at[:, pl.ds(pl.multiple_of(far * cols + q * blk, LANES), blk)]
        move(there, there, g_s, f_r.at[q], ahead).wait_recv()
        move(there, there, g_s, g_r, mate, core).start()
    ref = genes_ref.at[:, pl.ds(0, genes - len(early) * blk)]
    move(ref, ref, g_s, g_r, ahead).wait_recv()
    move(psend, psend, p_s, g_r, ahead).wait_send()
    rows = urecv.at[pl.ds(0, owners + 1 if relays else owners)]
    move(rows, rows, u_s, g_r, ahead).wait_send()

    def sent_blocks():
        move(precv, precv, g_s, g_r, ahead).wait_send()
        lead_copy().wait_send()

    when_owner(me, sent_blocks)
    for p in range(PASSES):
        pair_copy(p).wait_send()
        for side in range(2):
            @pl.when(has(side))
            def _():
                halo_both(p, side).wait_send()


def settle(cells_in, genes_in, cells_ref, genes_ref):
    cells_ref[...] = cells_in[...]
    genes_ref[...] = genes_in[...]


def on_device(n, counts, cell_factor, gene_factor, tissue, neighbours):
    width, genes = counts.shape
    rank = cell_factor.shape[0]
    near = neighbours.shape[0]
    owners = min(n, genes // LANES)
    step = min(512, genes)
    loads = 1
    cols = genes // owners
    quarters = max(1, min(4, cols // LANES))
    relays = quarters // 2 if n == owners and n % 4 == 0 and n <= 16 else 0
    dma = pltpu.SemaphoreType.DMA
    vmem = pl.BlockSpec(memory_space=pltpu.VMEM)
    shapes = (
        jax.ShapeDtypeStruct((rank, width), f32),
        jax.ShapeDtypeStruct((rank, genes), bf16),
    )
    results = pl.pallas_call(
        functools.partial(kernel, n, owners, quarters, relays, step, loads),
        out_shape=tuple(pltpu.VMEM(s.shape, s.dtype) for s in shapes),
        in_specs=[pl.BlockSpec(memory_space=pl.ANY)] * 5,
        out_specs=(vmem, vmem),
        scratch_shapes=[
            pltpu.VMEM((width, genes), jnp.int32),
            pltpu.VMEM((rank, width), f32),
            pltpu.VMEM((rank, genes), bf16),
            pltpu.VMEM((1, width), jnp.int32),
            pltpu.VMEM((near, width), jnp.int32),
            pltpu.VMEM((width + LANES, width), bf16),
            pltpu.VMEM((rank, genes), f32),
            pltpu.VMEM((rank, LANES), f32),
            pltpu.VMEM((PASSES, rank, width + LANES), f32),
            pltpu.VMEM((PASSES, rank, width + LANES), f32),
            pltpu.VMEM((PASSES, 2, 2 * SUB, max(rank // SUB * BORDER, LANES)), f32),
            pltpu.VMEM((PASSES, 2, 2, 2 * SUB, max(rank // SUB * BORDER, LANES)), f32),
            pltpu.VMEM((quarters * owners, rank, cols // quarters), WIRE),
            pltpu.VMEM((quarters, n, rank, cols // quarters), WIRE),
            pltpu.VMEM((max(relays, 1), rank, cols // quarters), WIRE),
            pltpu.VMEM((max(relays, 1), rank, cols // quarters), WIRE),
            pltpu.VMEM((SUB, LANES), f32),
            pltpu.VMEM((pl.cdiv(n + 1, LANES) * LANES, LANES), f32),
            pltpu.VMEM((rank, cols), bf16),
            pltpu.VMEM((quarters, rank, cols // quarters), bf16),
            dma((3,)),
            dma((loads, 3)),
            dma((loads,)),
            dma((PASSES,)),
            dma((PASSES,)),
            dma((PASSES, 2)),
            dma((PASSES, 2)),
            dma,
            dma((quarters,)),
            dma((max(relays, 1),)),
            dma,
            dma((2,)),
            dma,
            dma,
            dma((max(relays, 1),)),
            dma,
            dma,
        ],
        compiler_params=pltpu.CompilerParams(
            collective_id=0, has_side_effects=True, vmem_limit_bytes=63_160_000
        ),
    )(counts, cell_factor, gene_factor, tissue.reshape(1, width), neighbours)
    return pl.pallas_call(
        settle, out_shape=shapes, in_specs=[vmem] * 2, out_specs=(vmem, vmem),
        compiler_params=pltpu.CompilerParams(vmem_limit_bytes=16 * 1024 * 1024),
    )(*results)


def solution(mesh):
    return jax.shard_map(
        functools.partial(on_device, mesh.shape["tile"]),
        mesh=mesh,
        in_specs=(
            P(("grp", "tile"), "gene"),
            P(None, ("grp", "tile")),
            P(None, ("grp", "gene")),
            P(("grp", "tile")),
            P(None, ("grp", "tile")),
        ),
        out_specs=(P(None, ("grp", "tile")), P(None, ("grp", "gene"))),
        check_vma=False,
    )
```

```python
import functools

import jax
import jax.numpy as jnp
from jax import lax
from jax.experimental import pallas as pl
from jax.experimental.pallas import tpu as pltpu
from jax.sharding import PartitionSpec as P

BORDER = 32
RIM = 2 * BORDER
PASSES = 2
LANES = 128
SUB = 8
MESH = pl.DeviceIdType.MESH
WIRE = jnp.int16
TOP = 65000.0
HALF = 32768.0

smooth_weight = 0.5

f32 = jnp.float32
bf16 = jnp.bfloat16


def split(value):
    high = value.astype(bf16)
    low = (value - high.astype(f32)).astype(bf16)
    return high, low


def quotient(top, bottom):
    r = pl.reciprocal(bottom, approx=True)
    return top * r


def lane_of(shape):
    return lax.broadcasted_iota(jnp.int32, shape, 1)


def row_of(columns):
    rank = columns[0].shape[0]
    index = lax.broadcasted_iota(jnp.int32, (rank, LANES), 0)
    lane = lane_of((rank, LANES))
    spread = jnp.zeros((rank, LANES), f32)
    for g, column in enumerate(columns):
        spread = jnp.where(lane == index + g * rank, column, spread)
    return jnp.sum(spread, axis=0, keepdims=True)


def column_of(row, rank):
    index = lax.broadcasted_iota(jnp.int32, (rank, LANES), 0)
    return jnp.sum(jnp.where(lane_of((rank, LANES)) == index, row, 0.0), axis=1, keepdims=True)


def kernel(
    n, owners, quarters, relays, step, loads,
    x_hbm, w_hbm, h_hbm, t_hbm, nb_hbm,
    cells_ref, genes_ref,
    x_ref, w_ref, h_ref, t_ref, nb_ref, near_ref, acc_ref, halo_ref,
    nsend, nrecv, hsend, hrecv, psend, precv, ahead_ref, stage, usend, urecv, lead_ref, done_ref,
    in_sem, e_sem, x_sem, pair_s, pair_r, halo_s, halo_r,
    p_s, p_r, stage_r, u_s, u_r, g_s, g_r, f_r, l_s, l_r,
):
    rank, width = w_ref.shape
    genes = h_ref.shape[1]
    cols = genes // owners
    me = lax.axis_index("tile")
    core = lax.axis_index("gene")
    other = 1 - core
    barrier = pltpu.get_barrier_semaphore()

    small = [
        pltpu.make_async_copy(src, dst, in_sem.at[i])
        for i, (src, dst) in enumerate(
            ((w_hbm, w_ref), (t_hbm, t_ref), (nb_hbm, nb_ref))
        )
    ]

    size = genes // loads

    def first_loads(c):
        part = pl.ds(c * size, size)
        rows = ((width - BORDER, 0), (0, BORDER))
        return [pltpu.make_async_copy(h_hbm.at[:, part], h_ref.at[:, part], e_sem.at[c, 2])] + [
            pltpu.make_async_copy(
                x_hbm.at[pl.ds(source, BORDER), part], x_ref.at[pl.ds(target, BORDER), part],
                e_sem.at[c, side],
            )
            for side, (source, target) in enumerate(rows)
        ]

    def inner_load(c):
        part = pl.ds(c * size, size)
        return pltpu.make_async_copy(
            x_hbm.at[pl.ds(BORDER, width - RIM), part],
            x_ref.at[pl.ds(RIM, width - RIM), part],
            x_sem.at[c],
        )

    for copy in small[:2]:
        copy.start()
    for c in range(loads):
        for copy in first_loads(c):
            copy.start()
    for c in range(loads):
        inner_load(c).start()
    small[2].start()

    def has(side):
        return me > 0 if side == 0 else me < n - 1

    def greet(i, carry):
        pl.semaphore_signal(
            barrier, inc=1, device_id={"tile": lax.rem(me + i, n), "gene": other},
            device_id_type=MESH,
        )
        return carry

    few = n <= 16
    lax.fori_loop(1, n, greet, 0, unroll=few)
    pl.semaphore_signal(barrier, inc=1, device_id={"gene": other}, device_id_type=MESH)
    for side in range(2):
        @pl.when(has(side))
        def _():
            pl.semaphore_signal(
                barrier, inc=1, device_id={"tile": me - 1 + 2 * side}, device_id_type=MESH
            )

    for side in range(2):
        @pl.when(jnp.logical_not(has(side)))
        def _():
            hrecv[:, side] = jnp.zeros(hrecv.shape[:1] + hrecv.shape[2:], f32)
    halo_ref[...] = jnp.zeros_like(halo_ref)

    def halo_rows(p):
        return pl.ds(0, 2 * SUB if p == 0 else SUB)

    def halo_copy(p, side, k):
        return pltpu.make_async_remote_copy(
            src_ref=hsend.at[p, side, halo_rows(p)], dst_ref=hrecv.at[p, 1 - side, core, halo_rows(p)],
            send_sem=halo_s.at[p, side], recv_sem=halo_r.at[p, 1 - side],
            device_id={"tile": me - 1 + 2 * side, "gene": core if k == 0 else other},
            device_id_type=MESH,
        )

    def halo_both(p, side):
        ref = hrecv.at[p, side, :, halo_rows(p)]
        return pltpu.make_async_remote_copy(
            src_ref=ref, dst_ref=ref, send_sem=halo_s.at[p, side], recv_sem=halo_r.at[p, side],
            device_id={"tile": lax.rem(me + 1, n)}, device_id_type=MESH,
        )

    def pair_copy(p):
        part = pl.ds(0, width + LANES if p == 0 else width)
        return pltpu.make_async_remote_copy(
            src_ref=nsend.at[p, :, part], dst_ref=nrecv.at[p, :, part],
            send_sem=pair_s.at[p], recv_sem=pair_r.at[p],
            device_id={"gene": other}, device_id_type=MESH,
        )

    blk = cols // quarters

    relayed = range(quarters - relays, quarters)
    early = range(relays + 1 if relays else 0)
    even = lax.rem(me, 2) == 0
    mate = me + 1 - 2 * lax.rem(me, 2)
    far = lax.rem(me + n // 2, n)
    far_mate = far + 1 - 2 * lax.rem(far, 2)

    def when_owner(index, call):
        if owners == n:
            call()
        else:
            pl.when(index < owners)(call)

    def move(src, dst, ssem, rsem, tile, gene=None):
        return pltpu.make_async_remote_copy(
            src_ref=src, dst_ref=dst, send_sem=ssem, recv_sem=rsem,
            device_id={"tile": tile, "gene": other if gene is None else gene},
            device_id_type=MESH,
        )

    def lead_copy():
        mine = pl.ds(pl.multiple_of(me * cols, LANES), cols)
        return move(h_ref.at[:, mine], lead_ref, l_s, l_r, me)

    rims, inner = slice(0, RIM), slice(RIM, width)

    def ratio_of(lhs, rows, at, size):
        product = jnp.dot(lhs, h_ref[:, pl.ds(at, size)], preferred_element_type=f32)
        return quotient(x_ref[rows, pl.ds(at, size)].astype(f32), product).astype(bf16)

    def numer_of(lhs, rows, begin, sums=False):
        acc = None
        for c in range(genes // step):
            if begin is not None:
                begin(c)
            ratio = ratio_of(lhs, rows, c * step, step)
            if sums:
                ratio = jnp.concatenate([ratio, jnp.ones((2 * SUB, step), bf16)], axis=0)
            part = lax.dot_general(
                h_ref[:, pl.ds(c * step, step)], ratio,
                (((1,), (1,)), ((), ())), preferred_element_type=f32,
            )
            acc = part if acc is None else acc + part
        return acc

    def put_halo(p, numer):
        value = (cells * mask)[:, rims] * numer
        for side, first in enumerate((BORDER, 0)):
            for g in range(rank // SUB):
                hsend[p, side, 0:SUB, g * BORDER : (g + 1) * BORDER] = value[
                    g * SUB : (g + 1) * SUB, first : first + BORDER
                ]

    wide = min(4 * step, genes)
    small[0].wait()
    small[1].wait()
    cells = pltpu.roll(w_ref[...], BORDER, 1)
    mrow = pltpu.roll(jnp.broadcast_to(t_ref[...].astype(f32), (2 * SUB, width)), BORDER, 1)
    mask = jnp.broadcast_to(mrow[0:1], (rank, width))
    inside = mask > 0.0
    for side in range(2):
        hsend[0, side, SUB : 2 * SUB, 0:LANES] = jnp.where(
            lane_of((SUB, LANES)) < RIM, mrow[0:SUB, 0:LANES], 0.0
        )
    lhs = jnp.transpose(cells).astype(bf16)
    def halo_start(p):
        for side in range(2):
            @pl.when(has(side))
            def _():
                halo_copy(p, side, 0).start()
                halo_copy(p, side, 1).start()

    every = max(genes // loads // step, 1)

    def arrive(c):
        if c % every == 0:
            inner_load(c // every).wait()

    def first_arrive(c):
        if c % every == 0:
            for copy in first_loads(c // every):
                copy.wait()

    for p in range(PASSES):
        numer_rim = numer_of(lhs[rims], rims, first_arrive if p == 0 else None, p == 0)
        if p == 0:
            nsend[0, :, width : width + LANES] = jnp.broadcast_to(
                numer_rim[:, RIM : RIM + 1], (rank, LANES)
            )
            numer_rim = numer_rim[:, rims]
        put_halo(p, numer_rim)
        if p == 0:
            pl.semaphore_wait(
                barrier, n + has(0).astype(jnp.int32) + has(1).astype(jnp.int32)
            )
        halo_start(p)
        if p == 0:
            when_owner(me, lambda: lead_copy().start())
        numer_inner = numer_of(lhs[inner], inner, arrive if p == 0 else None)
        nsend[p, :, rims] = numer_rim
        nsend[p, :, inner] = numer_inner
        pair_copy(p).start()
        if p == 0:
            small[2].wait()
            a = pltpu.roll(nb_ref[...], BORDER, 1) - (me * width - BORDER)
            spot = jnp.where(a < BORDER, a + width, a)
            spot = jnp.where(jnp.logical_and(a >= width, a < width + BORDER), a - width, spot)
            for at in range(0, width + LANES, BORDER):
                index = lax.broadcasted_iota(jnp.int32, (BORDER, width), 0) + at
                total = jnp.zeros((BORDER, width), f32)
                for j in range(nb_ref.shape[0]):
                    total = total + jnp.where(spot[j : j + 1] == index, 1.0, 0.0)
                near_ref[at : at + BORDER, :] = total.astype(bf16)
        pair_copy(p).wait_recv()
        if p == 0:
            inverse = 1.0 / (
                nsend[0, :, width : width + LANES] + nrecv[0, :, width : width + LANES]
            )
            inverse_wide = jnp.concatenate([inverse] * (width // LANES), axis=1)
        numer = nsend[p, :, 0:width] + nrecv[p, :, 0:width]
        updated = jnp.where(inside, cells * numer * inverse_wide, cells)
        stacked = jnp.concatenate(split(updated * mask) + (mrow.astype(bf16),), axis=0)
        mixed = jnp.dot(stacked, near_ref[0:width, :], preferred_element_type=f32)
        near = mixed[0:rank] + mixed[rank : 2 * rank]
        if p == 0:
            count = mixed[2 * rank : 2 * rank + 1]
        cells = jnp.where(
            inside,
            (1.0 - smooth_weight) * updated + smooth_weight * near / jnp.maximum(count, 1.0),
            updated,
        )
        if p + 1 == PASSES:
            lhs = jnp.transpose(cells).astype(bf16)[inner]
            lift = jnp.concatenate(split(cells * mask), axis=0)[:, inner]
            for at in range(0, genes, wide):
                both = jnp.dot(
                    lift, ratio_of(lhs, inner, at, wide), preferred_element_type=f32
                )
                acc_ref[:, pl.ds(at, wide)] = both[0:rank] + both[rank : 2 * rank]
        for side in range(2):
            @pl.when(has(side))
            def _():
                halo_both(p, side).wait_recv()
        for side in range(2):
            packed = hrecv[p, side, 0, 0:SUB] + hrecv[p, side, 1, 0:SUB]
            for g in range(rank // SUB):
                halo_ref[g * SUB : (g + 1) * SUB, side * BORDER : (side + 1) * BORDER] = packed[
                    :, g * BORDER : (g + 1) * BORDER
                ]
        halo = halo_ref[...] * inverse
        if p == 0:
            flags = jnp.where(
                lane_of((SUB, LANES)) < BORDER,
                hrecv[0, 0, 0, SUB : 2 * SUB, 0:LANES], hrecv[0, 1, 0, SUB : 2 * SUB, 0:LANES],
            )
            flags = jnp.concatenate([flags, flags], axis=0).astype(bf16)
        stacked = jnp.concatenate(split(halo) + (flags,), axis=0)
        mixed = jnp.dot(
            stacked, near_ref[width : width + LANES, 0:LANES], preferred_element_type=f32
        )
        near_rim = near[:, 0:LANES] + (mixed[0:rank] + mixed[rank : 2 * rank])
        if p == 0:
            count_rim = jnp.maximum(count[:, 0:LANES] + mixed[2 * rank : 2 * rank + 1], 1.0)
        rim = updated[:, 0:LANES]
        rim = jnp.where(
            inside[:, 0:LANES],
            (1.0 - smooth_weight) * rim + smooth_weight * near_rim / count_rim,
            rim,
        )
        cells = jnp.concatenate([rim, cells[:, LANES:]], axis=1)
        lhs = jnp.transpose(cells).astype(bf16)

    weighted = cells * mask
    den_part = jnp.sum(weighted, axis=1, keepdims=True)
    lift = jnp.concatenate(split(weighted[:, 0:LANES]), axis=0)[:, rims]

    def part_start(q, j):
        o = lax.rem(me + j, n)

        def call():
            slot = lax.rem(n - j, n)
            move(psend.at[q * owners + o], precv.at[q, slot], p_s, p_r.at[q], o).start()

        if q in relayed:
            if j in (n // 2 - 1, n // 2 + 1):
                pl.when(o != far_mate)(call)
            elif j != n // 2:
                call()
        else:
            when_owner(o, call)

    def unit_start(j):
        o = lax.rem(me + j, n)
        when_owner(
            o,
            lambda: move(
                usend.at[pl.ds(0, 1)], urecv.at[pl.ds(lax.rem(n - j, n), 1)], u_s, u_r.at[0], o
            ).start(),
        )

    def all_peers(call):
        if few:
            for j in sorted(range(n), key=lambda j: (abs(j - n // 2), j)):
                call(j)
        else:
            def body(j, carry):
                call(j)
                return carry

            lax.fori_loop(0, n, body, 0)

    top = jnp.full((rank, 1), 1e-30, f32)
    for at in range(0, genes, wide):
        both = jnp.dot(lift, ratio_of(lhs[rims], rims, at, wide), preferred_element_type=f32)
        total = acc_ref[:, pl.ds(at, wide)] + (both[0:rank] + both[rank : 2 * rank])
        acc_ref[:, pl.ds(at, wide)] = total
        top = jnp.maximum(top, jnp.max(total, axis=1, keepdims=True))
    usend[...] = jnp.broadcast_to(row_of((top * (1.0 / TOP), den_part)), usend.shape)
    if relays:
        move(
            usend.at[pl.ds(0, 1)], urecv.at[pl.ds(n, 1)], u_s, u_r.at[1], mate, core
        ).start()
    all_peers(unit_start)
    scale = TOP / top

    def code(at):
        value = acc_ref[:, pl.ds(at, blk)] * scale + (0.5 - HALF)
        return jnp.floor(value).astype(jnp.int32).astype(WIRE)

    for i, q in enumerate(relayed):
        ahead_ref[i] = code(pl.multiple_of(far_mate * cols + q * blk, LANES))
        move(ahead_ref.at[i], stage.at[i], p_s, stage_r.at[i], mate, core).start()
    for q in range(quarters):
        for o in range(owners):
            psend[q * owners + o] = code(o * cols + q * blk)
        all_peers(lambda j: part_start(q, j))
    cells_ref[...] = pltpu.roll(cells, width - BORDER, 1)

    def gene_start(q, j):
        o = lax.rem(me + j, n)
        come = f_r.at[q] if q in early and j == n // 2 else g_r
        here = pl.ds(pl.multiple_of(me * cols + q * blk, LANES), blk)
        call = move(done_ref.at[q], genes_ref.at[:, here], g_s, come, o).start
        if q in early and j in (n // 2 - 1, n // 2 + 1):
            pl.when(o != far_mate)(call)
        else:
            call()

    ahead = lax.rem(me + 1, n)
    if relays:
        row = urecv.at[pl.ds(n, 1)]
        move(row, row, u_s, u_r.at[1], ahead).wait_recv()
        unit_mate = column_of(urecv[n : n + 1], rank)
        joint = 1.0 / (top * (1.0 / TOP) + unit_mate)
    for i, q in enumerate(relayed):
        move(stage.at[i], stage.at[i], p_s, stage_r.at[i], ahead).wait_recv()
        there = pl.ds(pl.multiple_of(far * cols + q * blk, LANES), blk)
        value = (stage[i].astype(jnp.int32).astype(f32) + HALF) * unit_mate
        value = (acc_ref[:, there] + value) * joint + (0.5 - HALF)
        psend[q * owners + far] = jnp.floor(value).astype(jnp.int32).astype(WIRE)
        move(psend.at[q * owners + far], precv.at[q, n // 2], p_s, p_r.at[q], far).start()

    def finish_part():
        rows = urecv.at[pl.ds(0, n)]
        move(rows, rows, u_s, u_r.at[0], ahead).wait_recv()
        lead_copy().wait_recv()
        units = jnp.transpose(urecv[...])
        inverse_den = 1.0 / jnp.sum(units[rank : 2 * rank, 0:n], axis=1, keepdims=True)
        unit_of = [units[0:rank, slot : slot + 1] for slot in range(n)]
        if relays:
            middle = n // 2
            joint_of = list(unit_of)
            joint_of[middle] += jnp.where(even, unit_of[middle + 1], unit_of[middle - 1])
            joint_of[middle + 1] = jnp.where(even, 0.0, unit_of[middle + 1])
            joint_of[middle - 1] = jnp.where(even, unit_of[middle - 1], 0.0)
        for q in range(quarters):
            come = precv.at[q, pl.ds(0, n - 1 if q in relayed else n)]
            move(come, come, p_s, p_r.at[q], ahead).wait_recv()
            total = jnp.zeros((rank, blk), f32)
            for slot in range(n):
                value = precv[q, slot].astype(jnp.int32).astype(f32) + HALF
                total = total + value * (joint_of if q in relayed else unit_of)[slot]
            lead = lead_ref[:, q * blk : (q + 1) * blk].astype(f32) * inverse_den
            done_ref[q] = (lead * total).astype(done_ref.dtype)
            all_peers(lambda j: gene_start(q, j))

    when_owner(me, finish_part)
    for q in early:
        there = genes_ref.at[:, pl.ds(pl.multiple_of(far * cols + q * blk, LANES), blk)]
        move(there, there, g_s, f_r.at[q], ahead).wait_recv()
        move(there, there, g_s, g_r, mate, core).start()
    ref = genes_ref.at[:, pl.ds(0, genes - len(early) * blk)]
    move(ref, ref, g_s, g_r, ahead).wait_recv()
    move(psend, psend, p_s, g_r, ahead).wait_send()
    rows = urecv.at[pl.ds(0, owners + 1 if relays else owners)]
    move(rows, rows, u_s, g_r, ahead).wait_send()

    def sent_blocks():
        move(precv, precv, g_s, g_r, ahead).wait_send()
        lead_copy().wait_send()

    when_owner(me, sent_blocks)
    for p in range(PASSES):
        pair_copy(p).wait_send()
        for side in range(2):
            @pl.when(has(side))
            def _():
                halo_both(p, side).wait_send()


def settle(cells_in, genes_in, cells_ref, genes_ref):
    cells_ref[...] = cells_in[...]
    genes_ref[...] = genes_in[...]


def on_device(n, counts, cell_factor, gene_factor, tissue, neighbours):
    width, genes = counts.shape
    rank = cell_factor.shape[0]
    near = neighbours.shape[0]
    owners = min(n, genes // LANES)
    step = min(512, genes)
    loads = 1
    cols = genes // owners
    quarters = max(1, min(4, cols // LANES))
    relays = quarters // 2 if n == owners and n % 4 == 0 and n <= 16 else 0
    dma = pltpu.SemaphoreType.DMA
    vmem = pl.BlockSpec(memory_space=pltpu.VMEM)
    shapes = (
        jax.ShapeDtypeStruct((rank, width), f32),
        jax.ShapeDtypeStruct((rank, genes), bf16),
    )
    results = pl.pallas_call(
        functools.partial(kernel, n, owners, quarters, relays, step, loads),
        out_shape=tuple(pltpu.VMEM(s.shape, s.dtype) for s in shapes),
        in_specs=[pl.BlockSpec(memory_space=pl.ANY)] * 5,
        out_specs=(vmem, vmem),
        scratch_shapes=[
            pltpu.VMEM((width, genes), jnp.int32),
            pltpu.VMEM((rank, width), f32),
            pltpu.VMEM((rank, genes), bf16),
            pltpu.VMEM((1, width), jnp.int32),
            pltpu.VMEM((near, width), jnp.int32),
            pltpu.VMEM((width + LANES, width), bf16),
            pltpu.VMEM((rank, genes), f32),
            pltpu.VMEM((rank, LANES), f32),
            pltpu.VMEM((PASSES, rank, width + LANES), f32),
            pltpu.VMEM((PASSES, rank, width + LANES), f32),
            pltpu.VMEM((PASSES, 2, 2 * SUB, max(rank // SUB * BORDER, LANES)), f32),
            pltpu.VMEM((PASSES, 2, 2, 2 * SUB, max(rank // SUB * BORDER, LANES)), f32),
            pltpu.VMEM((quarters * owners, rank, cols // quarters), WIRE),
            pltpu.VMEM((quarters, n, rank, cols // quarters), WIRE),
            pltpu.VMEM((max(relays, 1), rank, cols // quarters), WIRE),
            pltpu.VMEM((max(relays, 1), rank, cols // quarters), WIRE),
            pltpu.VMEM((SUB, LANES), f32),
            pltpu.VMEM((pl.cdiv(n + 1, LANES) * LANES, LANES), f32),
            pltpu.VMEM((rank, cols), bf16),
            pltpu.VMEM((quarters, rank, cols // quarters), bf16),
            dma((3,)),
            dma((loads, 3)),
            dma((loads,)),
            dma((PASSES,)),
            dma((PASSES,)),
            dma((PASSES, 2)),
            dma((PASSES, 2)),
            dma,
            dma((quarters,)),
            dma((relays + 1,)),
            dma,
            dma((2,)),
            dma,
            dma,
            dma((relays + 1,)),
            dma,
            dma,
        ],
        compiler_params=pltpu.CompilerParams(
            collective_id=0, has_side_effects=True, vmem_limit_bytes=63_160_000
        ),
    )(counts, cell_factor, gene_factor, tissue.reshape(1, width), neighbours)
    return pl.pallas_call(
        settle, out_shape=shapes, in_specs=[vmem] * 2, out_specs=(vmem, vmem),
        compiler_params=pltpu.CompilerParams(vmem_limit_bytes=16 * 1024 * 1024),
    )(*results)


def solution(mesh):
    return jax.shard_map(
        functools.partial(on_device, mesh.shape["tile"]),
        mesh=mesh,
        in_specs=(
            P(("grp", "tile"), "gene"),
            P(None, ("grp", "tile")),
            P(None, ("grp", "gene")),
            P(("grp", "tile")),
            P(None, ("grp", "tile")),
        ),
        out_specs=(P(None, ("grp", "tile")), P(None, ("grp", "gene"))),
        check_vma=False,
    )
```
